32 devices in a mesh: gx: 4 (over y, core), gy: 2 (over x), gz: 4 (over z).
Axes of the slice: x: 2, y: 2, z: 4, core: 2. Of those that a mesh axis runs over, the one named last changes fastest.
Arguments:
- charges: float32 [16, 8, 32, 128], P('gx', 'gy', 'gz'), may hold values from -6 to 6
- offset_x: float32 [16, 8, 32, 128], P('gx', 'gy', 'gz'), may hold values from 0 to 4
- offset_y: float32 [16, 8, 32, 128], P('gx', 'gy', 'gz'), may hold values from 0 to 4
- offset_z: float32 [16, 8, 32, 128], P('gx', 'gy', 'gz'), may hold values from 0 to 2
- counts: int32 [16, 8, 32], P('gx', 'gy', 'gz'), may hold values from 32 to 128
Outputs:
- fine_potential: float32 [64, 32, 64], P('gx', 'gy', 'gz')
- atom_potential: float32 [16, 8, 32, 128], P('gx', 'gy', 'gz')
The draws below stay inside these ranges and needn't reach their ends.
Inputs may be any that keep to these rules, and one draw needn't show every extreme that they name: `counts`: slots at or beyond a bin's count are padding and hold no atom.
All inputs are finite; a program needn't handle non-finite values.
Results may differ from the reference program's by a relative error of at most 0.0003.
Values sent between devices are 32-bit elements; how exact they have to be, the bound alone decides.
No kernel may reach another device: no remote copies, remote signals or barrier semaphores. Data moves between devices by JAX's collectives and lax.ppermute only.
A program may use at most 64 MiB of HBM per device.

```python
import math
import jax
import jax.numpy as jnp
from jax import lax

R = 8
SLOTS = 128
NX = 64
NY = 32
NZ = 64
NBX = 16
NBY = 8
NBZ = 32


def place_ends(entries, rng, smallest, high):
    dims = entries.shape
    spot = [jax.random.randint(jax.random.fold_in(rng, axis), (), 0, dims[axis]) for axis in range(len(dims))]
    entries = entries.at[tuple(spot)].set(smallest)
    longest = dims.index(max(dims))
    spot[longest] = (spot[longest] + 1) % dims[longest]
    return entries.at[tuple(spot)].set(high)


def block_scale(key, dims, pieces, low, top_value):
    factor_of = 1.0
    for dim, parts in pieces:
        draws = jax.random.uniform(jax.random.fold_in(jax.random.fold_in(key, 6), dim), (parts,), jnp.float32, low / len(pieces), top_value / len(pieces))
        factor_of = factor_of * jnp.repeat(jnp.exp(draws), dims[dim] // parts).reshape((-1,) + (1,) * (len(dims) - 1 - dim))
    return factor_of


def gaussian(key, dims, width, most, shards=(), kind=jnp.bfloat16):
    level = block_scale(key, dims, shards, -0.22, 0.18) if shards else 1.0
    values = jax.random.normal(key, dims, jnp.float32) * width * level
    return jnp.minimum(jnp.maximum(values, -most), most).astype(kind)


def setup_inputs(seed: int = 0) -> dict:
    splits = jax.random.split(jax.random.key(seed), 6)
    charges = gaussian(splits[0], (NBX, NBY, NBZ, SLOTS), 1.0, 6.0, ((0, 4), (1, 2), (2, 4)), jnp.float32)
    offset_x = jnp.clip(4.0 * jax.random.uniform(splits[1], (NBX, NBY, NBZ, SLOTS), jnp.float32) ** block_scale(splits[1], (NBX, NBY, NBZ, SLOTS), ((0, 4), (1, 2), (2, 4)), -0.2, 0.2), 0.0, 4.0)
    offset_y = jnp.clip(4.0 * jax.random.uniform(splits[2], (NBX, NBY, NBZ, SLOTS), jnp.float32) ** block_scale(splits[2], (NBX, NBY, NBZ, SLOTS), ((0, 4), (1, 2), (2, 4)), -0.2, 0.2), 0.0, 4.0)
    offset_z = jnp.clip(2.0 * jax.random.uniform(splits[3], (NBX, NBY, NBZ, SLOTS), jnp.float32) ** block_scale(splits[3], (NBX, NBY, NBZ, SLOTS), ((0, 4), (1, 2), (2, 4)), -0.2, 0.2), 0.0, 2.0)
    counts = place_ends(jax.random.randint(splits[4], (NBX, NBY, NBZ), 32, SLOTS + 1), jax.random.fold_in(splits[4], 1), 32, SLOTS).astype(jnp.int32)
    return {"charges": charges, "offset_x": offset_x, "offset_y": offset_y, "offset_z": offset_z, "counts": counts}


highest = lax.Precision.HIGHEST
restrict_taps = (-0.0625, 0.0, 0.5625, 1.0, 0.5625, 0.0, -0.0625)


def profile_value(family, offset, reach):
    if family == 0:
        return math.exp(-(offset / (0.4 * reach)) ** 2)
    if family == 1:
        return math.exp(-(offset / (0.8 * reach)) ** 2)
    return 1.0 / (1.0 + (offset / reach) ** 2)


def profile_array(family, offset, reach):
    if family == 0:
        return jnp.exp(-(offset / (0.4 * reach)) ** 2)
    if family == 1:
        return jnp.exp(-(offset / (0.8 * reach)) ** 2)
    return 1.0 / (1.0 + (offset / reach) ** 2)


def norm_factor(family, reach):
    return sum(profile_value(family, float(offset), reach) ** 2 for offset in range(-reach, reach + 1)) ** 1.5


def bspline(spacing):
    magnitude = jnp.abs(spacing)
    inner = 2.0 / 3.0 - magnitude * magnitude + 0.5 * magnitude * magnitude * magnitude
    outer = (2.0 - magnitude) ** 3 / 6.0
    return jnp.where(magnitude < 1.0, inner, jnp.where(magnitude < 2.0, outer, 0.0))


def spline_weights(along_x, along_y, along_z):
    weight_x = bspline(along_x[..., None] + 2.0 - jnp.arange(8).astype(jnp.float32))
    weight_y = bspline(along_y[..., None] + 2.0 - jnp.arange(8).astype(jnp.float32))
    weight_z = bspline(along_z[..., None] + 2.0 - jnp.arange(6).astype(jnp.float32))
    return weight_x, weight_y, weight_z


def spread_patches(weighted, offset_x, offset_y, offset_z):
    def one_slab(items):
        slab_charge, slab_x, slab_y, slab_z = items
        weight_x, weight_y, weight_z = spline_weights(slab_x, slab_y, slab_z)
        outer = (slab_charge[..., None] * weight_x)[..., :, None] * weight_y[..., None, :]
        return jnp.einsum('bcsxy,bcsz->bcxyz', outer, weight_z, precision=highest)
    return lax.map(one_slab, (weighted, offset_x, offset_y, offset_z))


def place_patches(patches):
    nbins_x, nbins_y, nbins_z = patches.shape[:3]
    summed = jnp.zeros((4 * nbins_x + 4, 4 * nbins_y + 4, 2 * nbins_z + 4), jnp.float32)
    for shift_x in range(2):
        for shift_y in range(2):
            for shift_z in range(3):
                portion = patches[:, :, :, 4 * shift_x:4 * shift_x + 4, 4 * shift_y:4 * shift_y + 4, 2 * shift_z:2 * shift_z + 2]
                portion = jnp.transpose(portion, (0, 3, 1, 4, 2, 5)).reshape(4 * nbins_x, 4 * nbins_y, 2 * nbins_z)
                summed = summed + jnp.pad(portion, ((4 * shift_x, 4 - 4 * shift_x), (4 * shift_y, 4 - 4 * shift_y), (2 * shift_z, 4 - 2 * shift_z)))
    return summed


def collect_patches(padded, nbins_x, nbins_y, nbins_z):
    blocks = padded.reshape(nbins_x + 1, 4, nbins_y + 1, 4, nbins_z + 2, 2)
    rows_x = []
    for shift_x in range(2):
        rows_y = []
        for shift_y in range(2):
            rows_z = []
            for shift_z in range(3):
                piece = blocks[shift_x:shift_x + nbins_x, :, shift_y:shift_y + nbins_y, :, shift_z:shift_z + nbins_z, :]
                rows_z.append(jnp.transpose(piece, (0, 2, 4, 1, 3, 5)))
            rows_y.append(jnp.concatenate(rows_z, axis=5))
        rows_x.append(jnp.concatenate(rows_y, axis=4))
    return jnp.concatenate(rows_x, axis=3)


def interpolate(patches, offset_x, offset_y, offset_z):
    def one_slab(items):
        slab_values, slab_x, slab_y, slab_z = items
        weight_x, weight_y, weight_z = spline_weights(slab_x, slab_y, slab_z)
        partial_sum = jnp.einsum('bcxyz,bcsz->bcsxy', slab_values, weight_z, precision=highest)
        return jnp.einsum('bcsxy,bcsx,bcsy->bcs', partial_sum, weight_x, weight_y, precision=highest)
    return lax.map(one_slab, (patches, offset_x, offset_y, offset_z))


def pad_last(moved, before, after):
    return jnp.pad(moved, [(0, 0)] * (moved.ndim - 1) + [(before, after)])


def conv_axis(values, axis_index, family):
    moved = jnp.moveaxis(values, axis_index, -1)
    length = moved.shape[-1]
    padded = pad_last(moved, R, R)
    summed = jnp.zeros(moved.shape, jnp.float32)
    for offset in range(-R, R + 1):
        summed = summed + profile_value(family, float(offset), R) * padded[..., R + offset:R + offset + length]
    return jnp.moveaxis(summed, -1, axis_index)


def level_stencil(values, scale):
    result = jnp.zeros(values.shape, jnp.float32)
    for family in (0, 1):
        term = values
        for axis_index in range(3):
            term = conv_axis(term, axis_index, family)
        result = result + (scale / norm_factor(family, R)) * term
    return result


def restrict_axis(values, axis_index):
    moved = jnp.moveaxis(values, axis_index, -1)
    length = moved.shape[-1] // 2
    padded = pad_last(moved, 3, 3)
    summed = jnp.zeros(moved.shape[:-1] + (length,), jnp.float32)
    for position, weight in enumerate(restrict_taps):
        summed = summed + weight * padded[..., position:position + 2 * length:2]
    return jnp.moveaxis(summed, -1, axis_index)


def prolong_axis(values, axis_index):
    moved = jnp.moveaxis(values, axis_index, -1)
    length = 2 * moved.shape[-1]
    upsampled = jnp.stack([moved, jnp.zeros(moved.shape, jnp.float32)], axis=-1).reshape(moved.shape[:-1] + (length,))
    padded = pad_last(upsampled, 3, 3)
    summed = jnp.zeros(upsampled.shape, jnp.float32)
    for position, weight in enumerate(restrict_taps):
        summed = summed + weight * padded[..., position:position + length]
    return jnp.moveaxis(summed, -1, axis_index)


def coarse_axis(values, axis_index):
    moved = jnp.moveaxis(values, axis_index, -1)
    grid_index = jnp.arange(moved.shape[-1])
    matrix = profile_array(2, (grid_index[None, :] - grid_index[:, None]).astype(jnp.float32), R)
    result = jnp.einsum('ij,...j->...i', matrix, moved, precision=highest)
    return jnp.moveaxis(result, -1, axis_index)


def reference(charges, offset_x, offset_y, offset_z, counts):
    slot_count = charges.shape[-1]
    present = jnp.arange(slot_count)[None, None, None, :] < counts[..., None]
    weighted = jnp.where(present, charges, 0.0)
    spread = place_patches(spread_patches(weighted, offset_x, offset_y, offset_z))
    charge_one = spread[2:2 + NX, 2:2 + NY, 2:2 + NZ]
    direct_one = level_stencil(charge_one, 1.0)
    charge_two = restrict_axis(restrict_axis(restrict_axis(charge_one, 0), 1), 2)
    direct_two = level_stencil(charge_two, 0.5)
    charge_three = restrict_axis(restrict_axis(restrict_axis(charge_two, 0), 1), 2)
    far = coarse_axis(coarse_axis(coarse_axis(charge_three, 0), 1), 2) * (0.5 / norm_factor(2, R))
    potential_two = direct_two + prolong_axis(prolong_axis(prolong_axis(far, 0), 1), 2)
    fine_potential = direct_one + prolong_axis(prolong_axis(prolong_axis(potential_two, 0), 1), 2)
    padded = jnp.pad(fine_potential, 2)
    patches = collect_patches(padded, NBX, NBY, NBZ)
    atom_potential = jnp.where(present, interpolate(patches, offset_x, offset_y, offset_z), 0.0)
    return fine_potential, atom_potential
```

```python
import functools
import math

import jax
import jax.numpy as jnp
import numpy as np
from jax import lax
from jax.experimental import pallas as pl
from jax.experimental.pallas import tpu as pltpu
from jax.sharding import PartitionSpec as P

R = 8
LANES = 128
TERMS = 5
SLOT = LANES // TERMS
RIM = 4
TAPS = (-0.0625, 0.0, 0.5625, 1.0, 0.5625, 0.0, -0.0625)
highest = lax.Precision.HIGHEST


def profile(family, offset):
    if family == 0:
        return math.exp(-((offset / (0.4 * R)) ** 2))
    if family == 1:
        return math.exp(-((offset / (0.8 * R)) ** 2))
    return 1.0 / (1.0 + (offset / R) ** 2)


def norm_factor(family):
    return sum(profile(family, float(o)) ** 2 for o in range(-R, R + 1)) ** 1.5


def stencil(points, family):
    matrix = np.zeros((points, points))
    for i in range(points):
        for k in range(max(0, i - R), min(points, i + R + 1)):
            matrix[i, k] = profile(family, float(k - i))
    return matrix


def restriction(points):
    matrix = np.zeros((points // 2, points))
    for i in range(points // 2):
        for k, tap in enumerate(TAPS):
            if 0 <= 2 * i + k - 3 < points:
                matrix[i, 2 * i + k - 3] += tap
    return matrix


def term_matrices(points):
    q_one = restriction(points)
    q_two = restriction(points // 2)
    coarse = points // 4
    far = np.array([[profile(2, float(k - i)) for k in range(coarse)] for i in range(coarse)])
    down = q_two @ q_one
    return [
        stencil(points, 0),
        stencil(points, 1),
        q_one.T @ stencil(points // 2, 0) @ q_one,
        q_one.T @ stencil(points // 2, 1) @ q_one,
        down.T @ far @ down,
    ]


def term_scales():
    n = [norm_factor(f) for f in range(3)]
    return [1.0 / n[0], 1.0 / n[1], 0.5 / n[0], 0.5 / n[1], 0.5 / n[2]]


def windowed(points, count):
    local = points // count
    width = local + RIM
    index = np.arange(count)[:, None] * local + np.arange(width)[None, :] - RIM // 2
    inside = (index >= 0) & (index < points)
    clipped = np.clip(index, 0, points - 1)
    both = inside[:, :, None, None] & inside[None, None]
    return np.stack(
        [np.where(both, m[clipped[:, :, None, None], clipped[None, None]], 0.0) for m in term_matrices(points)]
    )


def round_up(value, step):
    return -(-value // step) * step


class Plan:
    def __init__(self, nbins, counts):
        self.nbins = nbins
        self.counts = counts
        self.local = (4 * nbins[0], 4 * nbins[1], 2 * nbins[2])
        self.width = tuple(v + RIM for v in self.local)
        self.points = tuple(v * c for v, c in zip(self.local, counts))
        self.xp = round_up(self.width[0], 8)
        self.zp = round_up(self.width[2], 16)
        if self.zp - self.width[2] >= 8 and self.width[2] % 2 == 0:
            self.zp = round_up(self.width[2], 8)
        self.chunks = -(-self.width[1] // TERMS)
        self.lanes_in = round_up(self.width[1] * self.xp, LANES)
        self.lanes_out = self.chunks * LANES
        self.columns = nbins[0] * nbins[1]
        assert self.columns * nbins[2] == LANES and nbins[2] == 8
        assert self.width[2] <= SLOT and self.columns % 2 == 0

    def place_matrix(self):
        nbx, nby, _ = self.nbins
        m = np.zeros((self.columns * 64, self.lanes_in), np.float32)
        for a in range(nbx):
            for b in range(nby):
                for i in range(8):
                    for j in range(8):
                        m[(a * nby + b) * 64 + i * 8 + j, (4 * b + j) * self.xp + 4 * a + i] = 1.0
        return jnp.asarray(m, jnp.bfloat16)

    def z_table(self):
        nz, width = self.counts[2], self.width[2]
        m = windowed(self.points[2], nz)
        table = np.zeros((nz, nz * self.zp, LANES), np.float32)
        for d in range(nz):
            for o in range(nz):
                for w in range(width):
                    row = o * self.zp + (w % 2) * (self.zp // 2) + w // 2
                    for t in range(TERMS):
                        table[d, row, t * SLOT : t * SLOT + width] = m[t, d, :, (d - o) % nz, w]
        return jnp.asarray(table)

    def y_table(self):
        ny, width = self.counts[1], self.width[1]
        m = windowed(self.points[1], ny)
        table = np.zeros((ny, ny * width, self.chunks * TERMS, LANES), np.float32)
        for d in range(ny):
            for o in range(ny):
                for t in range(TERMS):
                    block = m[t, d, :, (d - o) % ny, :]
                    table[d, o * width : (o + 1) * width, :width, t * SLOT : (t + 1) * SLOT] = block.T[:, :, None]
        return jnp.asarray(table.reshape(ny, ny * width * self.chunks * TERMS, LANES))

    def x_table(self):
        nx, width = self.counts[0], self.width[0]
        m = windowed(self.points[0], nx)
        scales = term_scales()
        table = np.zeros((nx, nx * self.xp, TERMS * self.xp), np.float32)
        for d in range(nx):
            for o in range(nx):
                for t in range(TERMS):
                    table[d, o * self.xp : o * self.xp + width, t * self.xp : t * self.xp + width] = (
                        scales[t] * m[t, (d + o) % nx, :, d, :]
                    )
        return jnp.asarray(table)


def bspline(spacing):
    a = jnp.abs(spacing)
    u = jnp.maximum(2.0 - a, 0.0)
    v = jnp.maximum(1.0 - a, 0.0)
    return u * u * u * (1.0 / 6.0) - v * v * v * (2.0 / 3.0)


def counts_row(counts, nbins):
    nbx, nby, nbz = nbins
    rows = jnp.concatenate([counts[a].astype(jnp.float32) for a in range(nbx)], axis=0)
    spread = lax.broadcasted_iota(jnp.int32, (nbz, LANES), 1) % nbz == lax.broadcasted_iota(
        jnp.int32, (nbz, LANES), 0
    )
    tiled = jnp.dot(rows, spread.astype(jnp.float32), precision=highest)
    own = lax.broadcasted_iota(jnp.int32, tiled.shape, 1) // nbz == lax.broadcasted_iota(
        jnp.int32, tiled.shape, 0
    )
    return jnp.sum(jnp.where(own, tiled, 0.0), axis=0, keepdims=True)


def split_two(value):
    high = value.astype(jnp.bfloat16)
    low = (value - high.astype(jnp.float32)).astype(jnp.bfloat16)
    return high, low


def spread_kernel(plan, counts_ref, charge_ref, x_ref, y_ref, z_ref, place_ref, out_ref,
                  bx_s, by_s, bz_s, patch_s, turned_s, column_s):
    slots = charge_ref.shape[1]
    row = counts_row(counts_ref, plan.nbins)
    slot = lax.broadcasted_iota(jnp.int32, (slots, LANES), 0).astype(jnp.float32)
    weighted = jnp.where(slot < row, charge_ref[...].T, 0.0)
    along = x_ref[...].T
    for i in range(8):
        bx_s[i] = weighted * bspline(along + (2.0 - i))
    along = y_ref[...].T
    for i in range(8):
        by_s[i] = bspline(along + (2.0 - i))
    along = z_ref[...].T
    for i in range(6):
        bz_s[i] = bspline(along + (2.0 - i))

    def one_x(i, carry):
        weight_x = bx_s[i]
        rows = [[] for _ in range(6)]
        for j in range(8):
            product = weight_x * by_s[j]
            for k in range(6):
                rows[k].append(jnp.sum(product * bz_s[k], axis=0, keepdims=True))
        for k in range(6):
            patch_s[pl.ds(pl.multiple_of(k * 64 + i * 8, 8), 8), :] = jnp.concatenate(rows[k], axis=0)
        return carry

    lax.fori_loop(0, 8, one_x, 0)
    for h in range(3):
        turned_s[:, h * LANES : (h + 1) * LANES] = patch_s[h * LANES : (h + 1) * LANES, :].T
    column_s[...] = jnp.zeros_like(column_s)
    nbz = plan.nbins[2]
    half = plan.zp // 2
    lane = lax.broadcasted_iota(jnp.int32, (nbz, LANES), 1)
    for pair in range(plan.columns // 2):
        for s in range(3):
            left = turned_s[2 * pair * nbz : (2 * pair + 1) * nbz, s * LANES : (s + 1) * LANES]
            right = turned_s[(2 * pair + 1) * nbz : (2 * pair + 2) * nbz, s * LANES : (s + 1) * LANES]
            even = jnp.where(lane < 64, left, pltpu.roll(right, 64, 1))
            odd = jnp.where(lane < 64, pltpu.roll(left, 64, 1), right)
            for c, piece in enumerate((even, odd)):
                at = (pl.ds(c * half + s, nbz), pl.ds(pair * LANES, LANES))
                column_s[at] = column_s[at] + piece
    high, low = split_two(column_s[...])
    place = place_ref[...]
    out_ref[...] = jnp.dot(high, place, preferred_element_type=jnp.float32) + jnp.dot(
        low, place, preferred_element_type=jnp.float32
    )


def solve_kernel(plan, *refs):
    ny, nz = plan.counts[1:]
    nx = plan.counts[0]
    blocks = refs[: ny * nz]
    ztab_ref, ytab_ref, xtab_ref = refs[ny * nz : ny * nz + 3]
    outs = refs[ny * nz + 3 : ny * nz + 3 + nx]
    mid_s, term_s = refs[ny * nz + 3 + nx :]
    wy = plan.width[1]
    xp = plan.xp
    span = plan.chunks * TERMS
    for oy in range(ny):
        gathered = jnp.concatenate([blocks[oy * nz + oz][...] for oz in range(nz)], axis=0)
        done = lax.dot_general(
            gathered, ztab_ref[0], (((0,), (0,)), ((), ())), precision=highest,
            preferred_element_type=jnp.float32,
        )
        mid_s[oy * wy * xp : (oy + 1) * wy * xp, :] = done[: wy * xp, :]
    slot = lax.broadcasted_iota(jnp.int32, (xp, LANES), 1) // SLOT

    for chunk in range(plan.chunks):
        def one_y(y, sums):
            value = mid_s[pl.ds(pl.multiple_of(y * xp, 8), xp), :]
            return tuple(
                acc + value * ytab_ref[0, pl.ds(y * span + chunk * TERMS + b, 1), :]
                for b, acc in enumerate(sums)
            )

        sums = lax.fori_loop(
            0, ny * wy, one_y, tuple(jnp.zeros((xp, LANES), jnp.float32) for _ in range(TERMS)), unroll=8
        )
        for t in range(TERMS):
            merged = jnp.zeros((xp, LANES), jnp.float32)
            for b in range(TERMS):
                shift = (SLOT * (b - t)) % LANES
                moved = pltpu.roll(sums[b], shift, 1) if shift else sums[b]
                merged = jnp.where(slot == b, moved, merged)
            term_s[t * xp : (t + 1) * xp, chunk * LANES : (chunk + 1) * LANES] = merged
    result = jnp.dot(xtab_ref[0], term_s[...], precision=highest, preferred_element_type=jnp.float32)
    for o in range(nx):
        outs[o][...] = result[o * xp : (o + 1) * xp, :]


def gather_kernel(plan, *refs):
    nx = plan.counts[0]
    parts = refs[:nx]
    counts_ref, x_ref, y_ref, z_ref, place_ref, fine_ref, atom_ref = refs[nx : nx + 7]
    bx_s, by_s, bz_s, field_s, column_s, turned_s, patch_s = refs[nx + 7 :]
    xp = plan.xp
    wx, wy, wz = plan.width
    lx, ly, lz = plan.local
    total = parts[0][...]
    for part in parts[1:]:
        total = total + part[...]
    field_s[...] = jnp.zeros_like(field_s)
    for y in range(wy):
        chunk, b = divmod(y, TERMS)
        piece = total[:, chunk * LANES : (chunk + 1) * LANES]
        field_s[y * xp : (y + 1) * xp, :] = pltpu.roll(piece, LANES - SLOT * b, 1) if b else piece
    for x in range(lx):
        fine_ref[x] = field_s[pl.ds(2 * xp + x + 2, ly, stride=xp), :][:, 2 : 2 + lz]
    high, low = split_two(field_s[...].T[: plan.zp, :])
    place = place_ref[...]
    columns = lax.dot_general(
        high, place, (((1,), (1,)), ((), ())), preferred_element_type=jnp.float32
    ) + lax.dot_general(low, place, (((1,), (1,)), ((), ())), preferred_element_type=jnp.float32)
    for pair in range(plan.columns // 2):
        column_s[pair * plan.zp : (pair + 1) * plan.zp, :] = columns[:, pair * LANES : (pair + 1) * LANES]
    nbz = plan.nbins[2]
    lane = lax.broadcasted_iota(jnp.int32, (nbz, LANES), 1)
    for pair in range(plan.columns // 2):
        for s in range(3):
            even = column_s[pl.ds(pair * plan.zp + 2 * s, nbz, stride=2), :]
            odd = column_s[pl.ds(pair * plan.zp + 2 * s + 1, nbz, stride=2), :]
            turned_s[2 * pair * nbz : (2 * pair + 1) * nbz, s * LANES : (s + 1) * LANES] = jnp.where(
                lane < 64, even, pltpu.roll(odd, 64, 1)
            )
            turned_s[(2 * pair + 1) * nbz : (2 * pair + 2) * nbz, s * LANES : (s + 1) * LANES] = jnp.where(
                lane < 64, pltpu.roll(even, 64, 1), odd
            )
    for h in range(3):
        patch_s[h * LANES : (h + 1) * LANES, :] = turned_s[:, h * LANES : (h + 1) * LANES].T
    slots = x_ref.shape[1]
    along = x_ref[...].T
    for i in range(8):
        bx_s[i] = bspline(along + (2.0 - i))
    along = y_ref[...].T
    for i in range(8):
        by_s[i] = bspline(along + (2.0 - i))
    along = z_ref[...].T
    for i in range(6):
        bz_s[i] = bspline(along + (2.0 - i))

    def one_x(i, result):
        inner = jnp.zeros((slots, LANES), jnp.float32)
        rows = [patch_s[pl.ds(pl.multiple_of(k * 64 + i * 8, 8), 8), :] for k in range(6)]
        for j in range(8):
            along_z = rows[0][j : j + 1, :] * bz_s[0]
            for k in range(1, 6):
                along_z = along_z + rows[k][j : j + 1, :] * bz_s[k]
            inner = inner + along_z * by_s[j]
        return result + inner * bx_s[i]

    result = lax.fori_loop(0, 8, one_x, jnp.zeros((slots, LANES), jnp.float32))
    row = counts_row(counts_ref, plan.nbins)
    slot = lax.broadcasted_iota(jnp.int32, (slots, LANES), 0).astype(jnp.float32)
    atom_ref[...] = jnp.where(slot < row, result, 0.0).T


def body(charges, offset_x, offset_y, offset_z, counts):
    nbins = charges.shape[:3]
    slots = charges.shape[3]
    sizes = tuple(lax.axis_size(a) for a in ("gx", "gy", "gz"))
    nx, ny, nz = sizes
    plan = Plan(nbins, sizes)
    flat = [v.reshape(LANES, slots) for v in (charges, offset_x, offset_y, offset_z)]
    place = plan.place_matrix()
    vmem = pl.BlockSpec(memory_space=pltpu.VMEM)
    f32 = jnp.float32
    params = pltpu.CompilerParams(vmem_limit_bytes=56 << 20)

    weights = [
        pltpu.VMEM((8, slots, LANES), f32),
        pltpu.VMEM((8, slots, LANES), f32),
        pltpu.VMEM((6, slots, LANES), f32),
    ]
    spread = pl.pallas_call(
        functools.partial(spread_kernel, plan),
        out_shape=jax.ShapeDtypeStruct((plan.zp, plan.lanes_in), f32),
        in_specs=[vmem] * 6,
        out_specs=vmem,
        scratch_shapes=weights
        + [
            pltpu.VMEM((384, LANES), f32),
            pltpu.VMEM((LANES, 384), f32),
            pltpu.VMEM((plan.zp, plan.columns * 64), f32),
        ],
        compiler_params=params,
        name="spread",
    )(counts, *flat, place)

    def shifted(value, oy, oz):
        pairs = [
            (sy * nz + sz, ((sy + oy) % ny) * nz + (sz + oz) % nz) for sy in range(ny) for sz in range(nz)
        ]
        return lax.ppermute(value, ("gy", "gz"), pairs)

    blocks = [
        spread if oy == 0 and oz == 0 else shifted(spread, oy, oz) for oy in range(ny) for oz in range(nz)
    ]
    tables = (plan.z_table(), plan.y_table(), plan.x_table())
    axes = ("gz", "gy", "gx")

    def picked(table, axis):
        return pl.BlockSpec((1,) + table.shape[1:], lambda _, axis=axis: (lax.axis_index(axis), 0, 0))

    outs = pl.pallas_call(
        functools.partial(solve_kernel, plan),
        out_shape=[jax.ShapeDtypeStruct((plan.xp, plan.lanes_out), f32)] * nx,
        grid=(1,),
        in_specs=[vmem] * (ny * nz) + [picked(t, a) for t, a in zip(tables, axes)],
        out_specs=[vmem] * nx,
        scratch_shapes=[
            pltpu.VMEM((ny * plan.width[1] * plan.xp, LANES), f32),
            pltpu.VMEM((TERMS * plan.xp, plan.lanes_out), f32),
        ],
        compiler_params=params,
        name="solve",
    )(*blocks, *tables)
    parts = [
        outs[o] if o == 0 else lax.ppermute(outs[o], "gx", [(s, (s + o) % nx) for s in range(nx)])
        for o in range(nx)
    ]
    fine, atom = pl.pallas_call(
        functools.partial(gather_kernel, plan),
        out_shape=[
            jax.ShapeDtypeStruct(plan.local, f32),
            jax.ShapeDtypeStruct((LANES, slots), f32),
        ],
        in_specs=[vmem] * (nx + 5),
        out_specs=[vmem, vmem],
        scratch_shapes=weights
        + [
            pltpu.VMEM((plan.lanes_in, LANES), f32),
            pltpu.VMEM((plan.columns // 2 * plan.zp, LANES), f32),
            pltpu.VMEM((LANES, 384), f32),
            pltpu.VMEM((384, LANES), f32),
        ],
        compiler_params=params,
        name="gather",
    )(*parts, counts, *flat[1:], place)
    return fine, atom.reshape(charges.shape)


def solution(mesh):
    in_specs = (
        P("gx", "gy", "gz", None),
        P("gx", "gy", "gz", None),
        P("gx", "gy", "gz", None),
        P("gx", "gy", "gz", None),
        P("gx", "gy", "gz"),
    )
    out_specs = (P("gx", "gy", "gz"), P("gx", "gy", "gz", None))
    return jax.shard_map(body, mesh=mesh, in_specs=in_specs, out_specs=out_specs, check_vma=False)
```

```python
import functools
import math

import jax
import jax.numpy as jnp
import numpy as np
from jax import lax
from jax.experimental import pallas as pl
from jax.experimental.pallas import tpu as pltpu
from jax.sharding import PartitionSpec as P

R = 8
LANES = 128
TERMS = 5
SLOT = LANES // TERMS
RIM = 4
TAPS = (-0.0625, 0.0, 0.5625, 1.0, 0.5625, 0.0, -0.0625)
highest = lax.Precision.HIGHEST


def profile(family, offset):
    if family == 0:
        return math.exp(-((offset / (0.4 * R)) ** 2))
    if family == 1:
        return math.exp(-((offset / (0.8 * R)) ** 2))
    return 1.0 / (1.0 + (offset / R) ** 2)


def norm_factor(family):
    return sum(profile(family, float(o)) ** 2 for o in range(-R, R + 1)) ** 1.5


def stencil(points, family):
    matrix = np.zeros((points, points))
    for i in range(points):
        for k in range(max(0, i - R), min(points, i + R + 1)):
            matrix[i, k] = profile(family, float(k - i))
    return matrix


def restriction(points):
    matrix = np.zeros((points // 2, points))
    for i in range(points // 2):
        for k, tap in enumerate(TAPS):
            if 0 <= 2 * i + k - 3 < points:
                matrix[i, 2 * i + k - 3] += tap
    return matrix


def term_matrices(points):
    q_one = restriction(points)
    q_two = restriction(points // 2)
    coarse = points // 4
    far = np.array([[profile(2, float(k - i)) for k in range(coarse)] for i in range(coarse)])
    down = q_two @ q_one
    return [
        stencil(points, 0),
        stencil(points, 1),
        q_one.T @ stencil(points // 2, 0) @ q_one,
        q_one.T @ stencil(points // 2, 1) @ q_one,
        down.T @ far @ down,
    ]


def term_scales():
    n = [norm_factor(f) for f in range(3)]
    return [1.0 / n[0], 1.0 / n[1], 0.5 / n[0], 0.5 / n[1], 0.5 / n[2]]


def windowed(points, count):
    local = points // count
    width = local + RIM
    index = np.arange(count)[:, None] * local + np.arange(width)[None, :] - RIM // 2
    inside = (index >= 0) & (index < points)
    clipped = np.clip(index, 0, points - 1)
    both = inside[:, :, None, None] & inside[None, None]
    return np.stack(
        [np.where(both, m[clipped[:, :, None, None], clipped[None, None]], 0.0) for m in term_matrices(points)]
    )


def round_up(value, step):
    return -(-value // step) * step


class Plan:
    def __init__(self, nbins, counts):
        self.nbins = nbins
        self.counts = counts
        self.local = (4 * nbins[0], 4 * nbins[1], 2 * nbins[2])
        self.width = tuple(v + RIM for v in self.local)
        self.points = tuple(v * c for v, c in zip(self.local, counts))
        self.xp = round_up(self.width[0], 8)
        self.zp = round_up(self.width[2], 8)
        self.chunks = -(-self.width[1] // TERMS)
        self.lanes = self.chunks * LANES
        self.columns = nbins[0] * nbins[1]
        self.mid = self.counts[1] * self.lanes
        self.pair = 2 if counts[0] % 2 == 0 else 1
        assert self.columns * nbins[2] == LANES and nbins[2] == 8 and self.columns % 2 == 0
        assert TERMS * self.zp <= LANES and self.width[0] <= SLOT

    def place_matrix(self):
        nbx, nby, _ = self.nbins
        m = np.zeros((self.width[1] * self.xp, self.columns * 64), np.float32)
        for a in range(nbx):
            for b in range(nby):
                for i in range(8):
                    for j in range(8):
                        m[(4 * b + j) * self.xp + 4 * a + i, (a * nby + b) * 64 + i * 8 + j] = 1.0
        return jnp.asarray(m, jnp.bfloat16)

    def pick_matrix(self):
        nbx, nby, _ = self.nbins
        m = np.zeros((self.columns * 64, self.lanes), np.float32)
        for a in range(nbx):
            for b in range(nby):
                for i in range(8):
                    for j in range(8):
                        chunk, part = divmod(4 * b + j, TERMS)
                        m[(a * nby + b) * 64 + i * 8 + j, chunk * LANES + part * SLOT + 4 * a + i] = 1.0
        return jnp.asarray(m, jnp.bfloat16)

    def x_table(self):
        nx, width = self.counts[0], self.width[0]
        m = windowed(self.points[0], nx)
        table = np.zeros((nx, nx * self.xp, LANES), np.float32)
        for d in range(nx):
            for o in range(nx):
                source = self.x_source(d, o)
                for t in range(TERMS):
                    table[d, o * self.xp : o * self.xp + width, t * SLOT : t * SLOT + width] = (
                        m[t, d, :, source, :].T
                    )
        return jnp.asarray(table)

    def x_source(self, device, order):
        pair = self.pair
        shift, other = divmod(order, pair)
        return (device // pair - shift) % (self.counts[0] // pair) * pair + (device % pair ^ other)

    def y_table(self):
        ny, width = self.counts[1], self.width[1]
        m = windowed(self.points[1], ny)
        table = np.zeros((ny, ny * width, self.chunks * TERMS, LANES), np.float32)
        for d in range(ny):
            for o in range(ny):
                for t in range(TERMS):
                    block = m[t, d, :, (d - o) % ny, :]
                    table[d, o * width : (o + 1) * width, :width, t * SLOT : (t + 1) * SLOT] = block.T[:, :, None]
        return jnp.asarray(table.reshape(ny, ny * width * self.chunks * TERMS, LANES))

    def z_table(self):
        nz, width = self.counts[2], self.width[2]
        m = windowed(self.points[2], nz)
        scales = term_scales()
        table = np.zeros((nz, nz * self.zp, TERMS * self.zp), np.float32)
        for d in range(nz):
            for o in range(nz):
                for t in range(TERMS):
                    table[d, o * self.zp : o * self.zp + width, t * self.zp : t * self.zp + width] = (
                        scales[t] * m[t, (d + o) % nz, :, d, :]
                    )
        return jnp.asarray(table)


def bspline(spacing):
    a = jnp.abs(spacing)
    u = jnp.maximum(2.0 - a, 0.0)
    v = jnp.maximum(1.0 - a, 0.0)
    return u * u * u * (1.0 / 6.0) - v * v * v * (2.0 / 3.0)


def counts_row(counts, nbins):
    nbx, nby, nbz = nbins
    rows = jnp.concatenate([counts[a].astype(jnp.float32) for a in range(nbx)], axis=0)
    spread = lax.broadcasted_iota(jnp.int32, (nbz, LANES), 1) % nbz == lax.broadcasted_iota(
        jnp.int32, (nbz, LANES), 0
    )
    tiled = jnp.dot(rows, spread.astype(jnp.float32), precision=highest)
    own = lax.broadcasted_iota(jnp.int32, tiled.shape, 1) // nbz == lax.broadcasted_iota(
        jnp.int32, tiled.shape, 0
    )
    return jnp.sum(jnp.where(own, tiled, 0.0), axis=0, keepdims=True)


def split_two(value):
    high = value.astype(jnp.bfloat16)
    low = (value - high.astype(jnp.float32)).astype(jnp.bfloat16)
    return high, low


def spread_kernel(plan, *refs):
    hbm, (out_ref, bx_s, by_s, bz_s, row_ref) = refs[:6], refs[6:11]
    local, (patch_s, turned_s, column_s, sems) = refs[11:17], refs[17:]
    copies = [pltpu.make_async_copy(a, b, sems.at[n]) for n, (a, b) in enumerate(zip(hbm, local))]
    for copy in copies:
        copy.start()
    x_ref, y_ref, z_ref, counts_ref, charge_ref, place_s = local
    slots = charge_ref.shape[1]
    for n, (ref, weight, points) in enumerate(((x_ref, bx_s, 8), (y_ref, by_s, 8), (z_ref, bz_s, 6))):
        copies[n].wait()
        along = ref[...].T
        for i in range(points):
            weight[i] = bspline(along + (2.0 - i))
    copies[3].wait()
    row = counts_row(counts_ref, plan.nbins)
    row_ref[...] = jnp.broadcast_to(row, row_ref.shape)
    slot = lax.broadcasted_iota(jnp.int32, (slots, LANES), 0).astype(jnp.float32)
    copies[4].wait()
    weighted = jnp.where(slot < row, charge_ref[...].T, 0.0)

    def one_x(i, carry):
        weight_x = bx_s[i] * weighted
        rows = [[] for _ in range(6)]
        for j in range(8):
            product = weight_x * by_s[j]
            for k in range(6):
                rows[k].append(jnp.sum(product * bz_s[k], axis=0, keepdims=True))
        for k in range(6):
            patch_s[pl.ds(pl.multiple_of(k * 64 + i * 8, 8), 8), :] = jnp.concatenate(rows[k], axis=0)
        return carry

    lax.fori_loop(0, 8, one_x, 0)
    for h in range(3):
        turned_s[:, h * LANES : (h + 1) * LANES] = patch_s[h * LANES : (h + 1) * LANES, :].T
    column_s[...] = jnp.zeros_like(column_s)
    nbz = plan.nbins[2]
    half = plan.zp // 2
    lane = lax.broadcasted_iota(jnp.int32, (nbz, LANES), 1)
    for pair in range(plan.columns // 2):
        for s in range(3):
            left = turned_s[2 * pair * nbz : (2 * pair + 1) * nbz, s * LANES : (s + 1) * LANES]
            right = turned_s[(2 * pair + 1) * nbz : (2 * pair + 2) * nbz, s * LANES : (s + 1) * LANES]
            even = jnp.where(lane < 64, left, pltpu.roll(right, 64, 1))
            odd = jnp.where(lane < 64, pltpu.roll(left, 64, 1), right)
            for c, piece in enumerate((even, odd)):
                at = (pl.ds(pair * plan.zp + 2 * s + c, nbz, stride=2), slice(None))
                column_s[at] = column_s[at] + piece
    columns = jnp.concatenate(
        [column_s[p * plan.zp : (p + 1) * plan.zp, :] for p in range(plan.columns // 2)], axis=1
    )
    high, low = split_two(columns)
    copies[5].wait()
    place = place_s[...]
    contract = (((1,), (1,)), ((), ()))
    grid = lax.dot_general(place, high, contract, preferred_element_type=jnp.float32) + lax.dot_general(
        place, low, contract, preferred_element_type=jnp.float32
    )
    grid = jnp.concatenate([grid, jnp.zeros((grid.shape[0], LANES - plan.zp), jnp.float32)], axis=1)
    xp = plan.xp
    group = lax.broadcasted_iota(jnp.int32, (xp, LANES), 1) // plan.zp
    for chunk in range(plan.chunks):
        merged = jnp.zeros((xp, LANES), jnp.float32)
        for b in range(TERMS):
            y = chunk * TERMS + b
            if y < plan.width[1]:
                piece = grid[y * xp : (y + 1) * xp, :]
                moved = pltpu.roll(piece, b * plan.zp, 1) if b else piece
                merged = jnp.where(group == b, moved, merged)
        out_ref[:, chunk * LANES : (chunk + 1) * LANES] = merged


def solve_kernel(plan, *refs):
    nx, ny, nz = plan.counts
    blocks = refs[: nx * ny]
    tables = refs[nx * ny : nx * ny + 3]
    outs = refs[nx * ny + 3 : nx * ny + 3 + nz]
    mid_s, term_s, ytab_s, sem = refs[nx * ny + 3 + nz :]
    copy = pltpu.make_async_copy(tables[1].at[lax.axis_index("gy")], ytab_s, sem)
    copy.start()
    x_matrix = tables[0][lax.axis_index("gx")]
    wy = plan.width[1]
    zp = plan.zp
    span = plan.chunks * TERMS
    for oy in range(ny):
        gathered = jnp.concatenate([blocks[ox * ny + oy][...] for ox in range(nx)], axis=0)
        mid_s[oy * plan.lanes : (oy + 1) * plan.lanes, :] = lax.dot_general(
            gathered, x_matrix, (((0,), (0,)), ((), ())), precision=highest,
            preferred_element_type=jnp.float32,
        )
    slot = lax.broadcasted_iota(jnp.int32, (zp, LANES), 1) // SLOT
    copy.wait()
    for chunk in range(plan.chunks):
        sums = [jnp.zeros((zp, LANES), jnp.float32) for _ in range(TERMS)]
        for oy in range(ny):
            for y in range(wy):
                at = oy * plan.lanes + (y // TERMS) * LANES + (y % TERMS) * zp
                value = mid_s[at : at + zp, :]
                for b in range(TERMS):
                    row = (oy * wy + y) * span + chunk * TERMS + b
                    sums[b] = sums[b] + value * ytab_s[row : row + 1, :]
        for t in range(TERMS):
            merged = jnp.zeros((zp, LANES), jnp.float32)
            for b in range(TERMS):
                shift = (SLOT * (b - t)) % LANES
                moved = pltpu.roll(sums[b], shift, 1) if shift else sums[b]
                merged = jnp.where(slot == b, moved, merged)
            term_s[t * zp : (t + 1) * zp, chunk * LANES : (chunk + 1) * LANES] = merged
    z_matrix = tables[2][lax.axis_index("gz")]
    result = jnp.dot(z_matrix, term_s[...], precision=highest, preferred_element_type=jnp.float32)
    for o in range(nz):
        outs[o][...] = result[o * zp : (o + 1) * zp, :]


def gather_kernel(plan, *refs):
    nz = plan.counts[2]
    parts = refs[:nz]
    bx_s, by_s, bz_s, row_ref, pick_ref, fine_ref, atom_ref = refs[nz : nz + 7]
    field_s, column_s, turned_s, patch_s = refs[nz + 7 :]
    zp = plan.zp
    lx, ly, lz = plan.local
    total = parts[0][...]
    for part in parts[1:]:
        total = total + part[...]
    high, low = split_two(total)
    pick = pick_ref[...]
    contract = (((1,), (1,)), ((), ()))
    columns = lax.dot_general(high, pick, contract, preferred_element_type=jnp.float32) + lax.dot_general(
        low, pick, contract, preferred_element_type=jnp.float32
    )
    for pair in range(plan.columns // 2):
        column_s[pair * zp : (pair + 1) * zp, :] = columns[:, pair * LANES : (pair + 1) * LANES]
    for chunk in range(plan.chunks):
        turned = total[:, chunk * LANES : (chunk + 1) * LANES].T
        field_s[chunk * LANES : (chunk + 1) * LANES, :zp] = turned
    for y in range(ly):
        chunk, b = divmod(y + 2, TERMS)
        at = chunk * LANES + b * SLOT + 2
        fine_ref[:, y, :] = field_s[at : at + lx, 2 : 2 + lz]
    nbz = plan.nbins[2]
    lane = lax.broadcasted_iota(jnp.int32, (nbz, LANES), 1)
    for pair in range(plan.columns // 2):
        for s in range(3):
            even = column_s[pl.ds(pair * zp + 2 * s, nbz, stride=2), :]
            odd = column_s[pl.ds(pair * zp + 2 * s + 1, nbz, stride=2), :]
            turned_s[2 * pair * nbz : (2 * pair + 1) * nbz, s * LANES : (s + 1) * LANES] = jnp.where(
                lane < 64, even, pltpu.roll(odd, 64, 1)
            )
            turned_s[(2 * pair + 1) * nbz : (2 * pair + 2) * nbz, s * LANES : (s + 1) * LANES] = jnp.where(
                lane < 64, pltpu.roll(even, 64, 1), odd
            )
    for h in range(3):
        patch_s[h * LANES : (h + 1) * LANES, :] = turned_s[:, h * LANES : (h + 1) * LANES].T
    slots = atom_ref.shape[1]

    def one_x(i, result):
        inner = jnp.zeros((slots, LANES), jnp.float32)
        rows = [patch_s[pl.ds(pl.multiple_of(k * 64 + i * 8, 8), 8), :] for k in range(6)]
        for j in range(8):
            along_z = rows[0][j : j + 1, :] * bz_s[0]
            for k in range(1, 6):
                along_z = along_z + rows[k][j : j + 1, :] * bz_s[k]
            inner = inner + along_z * by_s[j]
        return result + inner * bx_s[i]

    result = lax.fori_loop(0, 8, one_x, jnp.zeros((slots, LANES), jnp.float32))
    row = row_ref[0:1, :]
    slot = lax.broadcasted_iota(jnp.int32, (slots, LANES), 0).astype(jnp.float32)
    atom_ref[...] = jnp.where(slot < row, result, 0.0).T


def body(charges, offset_x, offset_y, offset_z, counts):
    nbins = charges.shape[:3]
    slots = charges.shape[3]
    sizes = tuple(lax.axis_size(a) for a in ("gx", "gy", "gz"))
    nx, ny, nz = sizes
    plan = Plan(nbins, sizes)
    flat = [v.reshape(LANES, slots) for v in (charges, offset_x, offset_y, offset_z)]
    vmem = pl.BlockSpec(memory_space=pltpu.VMEM)
    hbm = pl.BlockSpec(memory_space=pl.ANY)
    f32 = jnp.float32
    params = pltpu.CompilerParams(vmem_limit_bytes=40 << 20)
    place, pick = plan.place_matrix(), plan.pick_matrix()

    spread, *weights = pl.pallas_call(
        functools.partial(spread_kernel, plan),
        out_shape=[
            pltpu.VMEM((plan.xp, plan.lanes), f32),
            pltpu.VMEM((8, slots, LANES), f32),
            pltpu.VMEM((8, slots, LANES), f32),
            pltpu.VMEM((6, slots, LANES), f32),
            pltpu.VMEM((8, LANES), f32),
        ],
        in_specs=[pl.BlockSpec(memory_space=pltpu.HBM)] * 6,
        out_specs=[vmem] * 5,
        scratch_shapes=[
            pltpu.VMEM((LANES, slots), f32),
            pltpu.VMEM((LANES, slots), f32),
            pltpu.VMEM((LANES, slots), f32),
            pltpu.VMEM(nbins, jnp.int32),
            pltpu.VMEM((LANES, slots), f32),
            pltpu.VMEM(place.shape, place.dtype),
            pltpu.VMEM((384, LANES), f32),
            pltpu.VMEM((LANES, 384), f32),
            pltpu.VMEM((plan.columns // 2 * plan.zp, LANES), f32),
            pltpu.SemaphoreType.DMA((6,)),
        ],
        compiler_params=params,
        name="spread",
    )(*(pltpu.with_memory_space_constraint(v, pltpu.HBM) for v in (*flat[1:], counts, flat[0], place)))

    def near(value):
        return pltpu.with_memory_space_constraint(value, pltpu.VMEM)

    def moved(value, axis, pairs):
        return near(lax.ppermute(value, axis, pairs))

    def from_chip(shift, oy):
        if shift == 0 and oy == 0:
            return spread
        pairs = [
            (sx * ny + sy, (sx // pair + shift) % (nx // pair) * pair * ny + sx % pair * ny + (sy + oy) % ny)
            for sx in range(nx)
            for sy in range(ny)
        ]
        return moved(spread, ("gx", "gy"), pairs)

    pair = plan.pair
    blocks = []
    for shift in range(nx // pair):
        own = [from_chip(shift, oy) for oy in range(ny)]
        blocks += own
        if pair == 2:
            blocks += [moved(v, "gx", [(s, s ^ 1) for s in range(nx)]) for v in own]
    tables = (plan.x_table(), plan.y_table(), plan.z_table())
    outs = pl.pallas_call(
        functools.partial(solve_kernel, plan),
        out_shape=[pltpu.VMEM((plan.zp, plan.lanes), f32)] * nz,
        in_specs=[vmem] * (nx * ny) + [vmem, hbm, vmem],
        out_specs=[vmem] * nz,
        scratch_shapes=[
            pltpu.VMEM((plan.mid, LANES), f32),
            pltpu.VMEM((TERMS * plan.zp, plan.lanes), f32),
            pltpu.VMEM(tables[1].shape[1:], f32),
            pltpu.SemaphoreType.DMA(()),
        ],
        compiler_params=params,
        name="solve",
    )(*blocks, *tables)
    parts = [outs[0]] + [
        moved(outs[o], "gz", [(s, (s + o) % nz) for s in range(nz)]) for o in range(1, nz)
    ]
    fine, atom = pl.pallas_call(
        functools.partial(gather_kernel, plan),
        out_shape=[
            jax.ShapeDtypeStruct(plan.local, f32),
            jax.ShapeDtypeStruct((LANES, slots), f32),
        ],
        in_specs=[vmem] * (nz + 5),
        out_specs=[vmem, vmem],
        scratch_shapes=[
            pltpu.VMEM((plan.lanes, LANES), f32),
            pltpu.VMEM((plan.columns // 2 * plan.zp, LANES), f32),
            pltpu.VMEM((LANES, 384), f32),
            pltpu.VMEM((384, LANES), f32),
        ],
        compiler_params=params,
        name="gather",
    )(*parts, *weights, pick)
    return fine, atom.reshape(charges.shape)


def solution(mesh):
    in_specs = (
        P("gx", "gy", "gz", None),
        P("gx", "gy", "gz", None),
        P("gx", "gy", "gz", None),
        P("gx", "gy", "gz", None),
        P("gx", "gy", "gz"),
    )
    out_specs = (P("gx", "gy", "gz"), P("gx", "gy", "gz", None))
    return jax.shard_map(body, mesh=mesh, in_specs=in_specs, out_specs=out_specs, check_vma=False)
```

```python
import functools
import math

import jax
import jax.numpy as jnp
import numpy as np
from jax import lax
from jax.experimental import pallas as pl
from jax.experimental.pallas import tpu as pltpu
from jax.sharding import PartitionSpec as P

R = 8
LANES = 128
TERMS = 5
SLOT = LANES // TERMS
GROUP = 2
RIM = 4
TAPS = (-0.0625, 0.0, 0.5625, 1.0, 0.5625, 0.0, -0.0625)
highest = lax.Precision.HIGHEST


def profile(family, offset):
    if family == 0:
        return math.exp(-((offset / (0.4 * R)) ** 2))
    if family == 1:
        return math.exp(-((offset / (0.8 * R)) ** 2))
    return 1.0 / (1.0 + (offset / R) ** 2)


def norm_factor(family):
    return sum(profile(family, float(o)) ** 2 for o in range(-R, R + 1)) ** 1.5


def stencil(points, family):
    matrix = np.zeros((points, points))
    for i in range(points):
        for k in range(max(0, i - R), min(points, i + R + 1)):
            matrix[i, k] = profile(family, float(k - i))
    return matrix


def restriction(points):
    matrix = np.zeros((points // 2, points))
    for i in range(points // 2):
        for k, tap in enumerate(TAPS):
            if 0 <= 2 * i + k - 3 < points:
                matrix[i, 2 * i + k - 3] += tap
    return matrix


def term_matrices(points):
    q_one = restriction(points)
    q_two = restriction(points // 2)
    coarse = points // 4
    far = np.array([[profile(2, float(k - i)) for k in range(coarse)] for i in range(coarse)])
    down = q_two @ q_one
    return [
        stencil(points, 0),
        stencil(points, 1),
        q_one.T @ stencil(points // 2, 0) @ q_one,
        q_one.T @ stencil(points // 2, 1) @ q_one,
        down.T @ far @ down,
    ]


def term_scales():
    n = [norm_factor(f) for f in range(3)]
    return [1.0 / n[0], 1.0 / n[1], 0.5 / n[0], 0.5 / n[1], 0.5 / n[2]]


def windowed(points, count):
    local = points // count
    width = local + RIM
    index = np.arange(count)[:, None] * local + np.arange(width)[None, :] - RIM // 2
    inside = (index >= 0) & (index < points)
    clipped = np.clip(index, 0, points - 1)
    both = inside[:, :, None, None] & inside[None, None]
    return np.stack(
        [np.where(both, m[clipped[:, :, None, None], clipped[None, None]], 0.0) for m in term_matrices(points)]
    )


def round_up(value, step):
    return -(-value // step) * step


class Plan:
    def __init__(self, nbins, counts):
        self.nbins = nbins
        self.counts = counts
        self.local = (4 * nbins[0], 4 * nbins[1], 2 * nbins[2])
        self.width = tuple(v + RIM for v in self.local)
        self.points = tuple(v * c for v, c in zip(self.local, counts))
        self.xp = round_up(self.width[0], 8)
        self.zp = round_up(self.width[2], 8)
        self.chunks = -(-self.width[1] // TERMS)
        self.lanes = self.chunks * LANES
        self.columns = nbins[0] * nbins[1]
        self.mid = self.counts[1] * self.lanes
        self.pair = 2 if counts[0] % 2 == 0 else 1
        assert self.columns * nbins[2] == LANES and nbins[2] == 8 and self.columns % 2 == 0
        assert TERMS * self.zp <= LANES and self.width[0] <= SLOT

    def place_matrix(self):
        nbx, nby, _ = self.nbins
        m = np.zeros((self.width[1] * self.xp, self.columns * 64), np.float32)
        for a in range(nbx):
            for b in range(nby):
                for i in range(8):
                    for j in range(8):
                        m[(4 * b + j) * self.xp + 4 * a + i, (a * nby + b) * 64 + i * 8 + j] = 1.0
        return jnp.asarray(m, jnp.bfloat16)

    def pick_matrix(self):
        nbx, nby, _ = self.nbins
        m = np.zeros((self.columns * 64, self.lanes), np.float32)
        for a in range(nbx):
            for b in range(nby):
                for i in range(8):
                    for j in range(8):
                        chunk, part = divmod(4 * b + j, TERMS)
                        m[(a * nby + b) * 64 + i * 8 + j, chunk * LANES + part * SLOT + 4 * a + i] = 1.0
        return jnp.asarray(m, jnp.bfloat16)

    def x_table(self):
        nx, width = self.counts[0], self.width[0]
        m = windowed(self.points[0], nx)
        table = np.zeros((nx, nx * self.xp, LANES), np.float32)
        for d in range(nx):
            for o in range(nx):
                source = self.x_source(d, o)
                for t in range(TERMS):
                    table[d, o * self.xp : o * self.xp + width, t * SLOT : t * SLOT + width] = (
                        m[t, d, :, source, :].T
                    )
        return jnp.asarray(table)

    def x_source(self, device, order):
        pair = self.pair
        shift, other = divmod(order, pair)
        return (device // pair - shift) % (self.counts[0] // pair) * pair + (device % pair ^ other)

    def y_table(self):
        ny, width = self.counts[1], self.width[1]
        m = windowed(self.points[1], ny)
        table = np.zeros((ny, ny * width, self.chunks * TERMS, LANES), np.float32)
        for d in range(ny):
            for o in range(ny):
                for t in range(TERMS):
                    block = m[t, d, :, (d - o) % ny, :]
                    table[d, o * width : (o + 1) * width, :width, t * SLOT : (t + 1) * SLOT] = block.T[:, :, None]
        return jnp.asarray(table.reshape(ny, ny * width * self.chunks * TERMS, LANES))

    def z_table(self):
        nz, width = self.counts[2], self.width[2]
        m = windowed(self.points[2], nz)
        scales = term_scales()
        table = np.zeros((nz, nz * self.zp, TERMS * self.zp), np.float32)
        for d in range(nz):
            for o in range(nz):
                for t in range(TERMS):
                    table[d, o * self.zp : o * self.zp + width, t * self.zp : t * self.zp + width] = (
                        scales[t] * m[t, (d + o) % nz, :, d, :]
                    )
        return jnp.asarray(table)


def bspline(spacing):
    a = jnp.abs(spacing)
    u = jnp.maximum(2.0 - a, 0.0)
    v = jnp.maximum(1.0 - a, 0.0)
    return u * u * u * (1.0 / 6.0) - v * v * v * (2.0 / 3.0)


def split_two(value):
    high = value.astype(jnp.bfloat16)
    low = (value - high.astype(jnp.float32)).astype(jnp.bfloat16)
    return high, low


def split_rows(value):
    high = value.astype(jnp.bfloat16).astype(jnp.float32)
    return jnp.concatenate([high, value - high], axis=0).astype(jnp.bfloat16)


def spread_kernel(plan, *refs):
    hbm, tables, (out_ref, outer_s, along_z_s) = refs[:6], refs[6:10], refs[10:13]
    tables_out, local, (column_s, sems) = refs[13:17], refs[17:23], refs[23:]
    copies = [pltpu.make_async_copy(a, b, sems.at[n]) for n, (a, b) in enumerate(zip(hbm, local))]
    for n, (table, target, axis) in enumerate(zip(tables, tables_out, ("gx", "gy", "gz", None))):
        source = table if axis is None else table.at[lax.axis_index(axis)]
        copies.append(pltpu.make_async_copy(source, target, sems.at[6 + n]))
    for copy in copies:
        copy.start()
    x_ref, y_ref, z_ref, charge_ref, counts_ref, place_s = local
    slots = charge_ref.shape[1]
    nbx, nby, nbz = plan.nbins
    zp = plan.zp
    node = 2.0 - lax.broadcasted_iota(jnp.int32, (8, slots), 0).astype(jnp.float32)
    slot = lax.broadcasted_iota(jnp.int32, (1, slots), 1)
    rank = lax.broadcasted_iota(jnp.int32, (8, LANES), 0)
    for copy in copies[:5]:
        copy.wait()

    def one_column(p):
        sums = [jnp.zeros((8, LANES), jnp.float32) for _ in range(zp // 8)]
        for c in range(nbz):
            r = p * nbz + c
            weight_x = bspline(x_ref[pl.ds(r, 1), :] + node)
            weight_y = bspline(y_ref[pl.ds(r, 1), :] + node)
            weight_z = bspline(z_ref[pl.ds(r, 1), :] + node)
            outer = split_rows(
                jnp.concatenate([weight_x[i : i + 1, :] * weight_y for i in range(8)], axis=0)
            )
            outer_s[r] = outer
            along_z_s[r] = weight_z
            weighted = jnp.where(slot < counts_ref[p // nby, p % nby, c], charge_ref[pl.ds(r, 1), :], 0.0)
            both = lax.dot_general(
                split_rows(weight_z * weighted), outer, (((1,), (1,)), ((), ())),
                preferred_element_type=jnp.float32,
            )
            part = both[:8, :] + both[8:, :]
            at, shift = divmod(2 * c, 8)
            if shift:
                part = pltpu.roll(part, shift, 0)
                sums[at] = sums[at] + jnp.where(rank >= shift, part, 0.0)
                sums[at + 1] = sums[at + 1] + jnp.where(rank < shift, part, 0.0)
            else:
                sums[at] = sums[at] + part
        return [v + pltpu.roll(v, 64, 1) for v in sums]

    left = lax.broadcasted_iota(jnp.int32, (8, LANES), 1) < 64

    def one_group(g, carry):
        for q in range(GROUP):
            pair = g * GROUP + q
            even = one_column(2 * pair)
            odd = one_column(2 * pair + 1)
            for n, (a, b) in enumerate(zip(even, odd)):
                column_s[pl.ds(pl.multiple_of(pair * zp, 8) + 8 * n, 8), :] = jnp.where(left, a, b)
        return carry

    lax.fori_loop(0, plan.columns // 2 // GROUP, one_group, 0)
    columns = jnp.concatenate(
        [column_s[p * plan.zp : (p + 1) * plan.zp, :] for p in range(plan.columns // 2)], axis=1
    )
    pad = jnp.zeros((LANES - 2 * zp, columns.shape[1]), jnp.bfloat16)
    copies[5].wait()
    grid = lax.dot_general(
        place_s[...], jnp.concatenate([split_rows(columns), pad], axis=0), (((1,), (1,)), ((), ())),
        preferred_element_type=jnp.float32,
    )
    grid = grid + pltpu.roll(grid, LANES - zp, 1)
    xp = plan.xp
    group = lax.broadcasted_iota(jnp.int32, (xp, LANES), 1) // plan.zp
    for chunk in range(plan.chunks):
        merged = jnp.zeros((xp, LANES), jnp.float32)
        for b in range(TERMS):
            y = chunk * TERMS + b
            if y < plan.width[1]:
                piece = grid[y * xp : (y + 1) * xp, :]
                moved = pltpu.roll(piece, b * plan.zp, 1) if b else piece
                merged = jnp.where(group == b, moved, merged)
        out_ref[:, chunk * LANES : (chunk + 1) * LANES] = merged
    for copy in copies[6:]:
        copy.wait()


def solve_kernel(plan, *refs):
    nx, ny, nz = plan.counts
    blocks = refs[: nx * ny]
    tables = refs[nx * ny : nx * ny + 3]
    outs = refs[nx * ny + 3 : nx * ny + 3 + nz]
    mid_s, term_s = refs[nx * ny + 3 + nz :]
    ytab_s = tables[1]
    x_matrix = tables[0][...]
    wy = plan.width[1]
    zp = plan.zp
    span = plan.chunks * TERMS
    for oy in range(ny):
        gathered = jnp.concatenate([blocks[ox * ny + oy][...] for ox in range(nx)], axis=0)
        mid_s[oy * plan.lanes : (oy + 1) * plan.lanes, :] = lax.dot_general(
            gathered, x_matrix, (((0,), (0,)), ((), ())), precision=highest,
            preferred_element_type=jnp.float32,
        )
    slot = lax.broadcasted_iota(jnp.int32, (zp, LANES), 1) // SLOT
    for chunk in range(plan.chunks):
        sums = [jnp.zeros((zp, LANES), jnp.float32) for _ in range(TERMS)]
        for oy in range(ny):
            for y in range(wy):
                at = oy * plan.lanes + (y // TERMS) * LANES + (y % TERMS) * zp
                value = mid_s[at : at + zp, :]
                for b in range(TERMS):
                    row = (oy * wy + y) * span + chunk * TERMS + b
                    sums[b] = sums[b] + value * ytab_s[row : row + 1, :]
        for t in range(TERMS):
            merged = jnp.zeros((zp, LANES), jnp.float32)
            for b in range(TERMS):
                shift = (SLOT * (b - t)) % LANES
                moved = pltpu.roll(sums[b], shift, 1) if shift else sums[b]
                merged = jnp.where(slot == b, moved, merged)
            term_s[t * zp : (t + 1) * zp, chunk * LANES : (chunk + 1) * LANES] = merged
    result = jnp.dot(tables[2][...], term_s[...], precision=highest, preferred_element_type=jnp.float32)
    for o in range(nz):
        outs[o][...] = result[o * zp : (o + 1) * zp, :]


def gather_kernel(plan, *refs):
    nz = plan.counts[2]
    parts = refs[:nz]
    outer_s, along_z_s, counts_hbm, pick_ref, fine_ref, atom_ref = refs[nz : nz + 6]
    field_s, column_s, counts_ref, sem = refs[nz + 6 :]
    copy = pltpu.make_async_copy(counts_hbm, counts_ref, sem)
    copy.start()
    nbx, nby, nbz = plan.nbins
    zp = plan.zp
    lx, ly, lz = plan.local
    total = parts[0][...]
    for part in parts[1:]:
        total = total + part[...]
    columns = lax.dot_general(
        split_rows(total), pick_ref[...], (((1,), (1,)), ((), ())), preferred_element_type=jnp.float32
    )
    columns = columns[:zp, :] + columns[zp:, :]
    left = lax.broadcasted_iota(jnp.int32, (zp, LANES), 1) < 64
    for pair in range(plan.columns // 2):
        both = columns[:, pair * LANES : (pair + 1) * LANES]
        turned = pltpu.roll(both, 64, 1)
        column_s[2 * pair * zp : (2 * pair + 1) * zp, :] = jnp.where(left, both, turned)
        column_s[(2 * pair + 1) * zp : (2 * pair + 2) * zp, :] = jnp.where(left, turned, both)
    for chunk in range(plan.chunks):
        turned = total[:, chunk * LANES : (chunk + 1) * LANES].T
        field_s[chunk * LANES : (chunk + 1) * LANES, :zp] = turned
    for y in range(ly):
        chunk, b = divmod(y + 2, TERMS)
        at = chunk * LANES + b * SLOT + 2
        fine_ref[:, y, :] = field_s[at : at + lx, 2 : 2 + lz]
    slots = atom_ref.shape[1]
    slot = lax.broadcasted_iota(jnp.int32, (1, slots), 1)
    copy.wait()

    def one_column(p):
        rows = []
        for c in range(nbz):
            r = p * nbz + c
            patch = column_s[pl.ds(p * zp + 2 * c, 8), :]
            both = jnp.dot(split_rows(patch), outer_s[r], preferred_element_type=jnp.float32)
            value = jnp.sum((both[:8, :] + both[8:, :]) * along_z_s[r], axis=0, keepdims=True)
            rows.append(jnp.where(slot < counts_ref[p // nby, p % nby, c], value, 0.0))
        atom_ref[pl.ds(pl.multiple_of(p * nbz, 8), nbz), :] = jnp.concatenate(rows, axis=0)

    def one_group(g, carry):
        for q in range(2 * GROUP):
            one_column(g * 2 * GROUP + q)
        return carry

    lax.fori_loop(0, plan.columns // 2 // GROUP, one_group, 0)


def body(charges, offset_x, offset_y, offset_z, counts):
    nbins = charges.shape[:3]
    slots = charges.shape[3]
    sizes = tuple(lax.axis_size(a) for a in ("gx", "gy", "gz"))
    nx, ny, nz = sizes
    plan = Plan(nbins, sizes)
    flat = [v.reshape(LANES, slots) for v in (charges, offset_x, offset_y, offset_z)]
    vmem = pl.BlockSpec(memory_space=pltpu.VMEM)
    hbm = pl.BlockSpec(memory_space=pltpu.HBM)
    f32 = jnp.float32
    params = pltpu.CompilerParams(vmem_limit_bytes=12 << 20)
    place, pick = plan.place_matrix(), plan.pick_matrix()

    def far(value):
        return pltpu.with_memory_space_constraint(value, pltpu.HBM)

    tables = (plan.x_table(), plan.y_table(), plan.z_table(), pick)
    spread, *weights = pl.pallas_call(
        functools.partial(spread_kernel, plan),
        out_shape=[
            pltpu.VMEM((plan.xp, plan.lanes), f32),
            pltpu.VMEM((LANES, LANES, slots), jnp.bfloat16),
            pltpu.VMEM((LANES, 8, slots), f32),
        ]
        + [pltpu.VMEM(t.shape[1:], t.dtype) for t in tables[:3]]
        + [pltpu.VMEM(pick.shape, pick.dtype)],
        in_specs=[hbm] * 10,
        out_specs=[vmem] * 7,
        scratch_shapes=[pltpu.VMEM((LANES, slots), f32)] * 4
        + [
            pltpu.SMEM(nbins, jnp.int32),
            pltpu.VMEM(place.shape, place.dtype),
            pltpu.VMEM((plan.columns // 2 * plan.zp, LANES), f32),
            pltpu.SemaphoreType.DMA((10,)),
        ],
        compiler_params=params,
        name="spread",
    )(*(far(v) for v in (*flat[1:], flat[0], counts, place, *tables)))
    weights, tables, pick = weights[:2], weights[2:5], weights[5]

    def near(value):
        return pltpu.with_memory_space_constraint(value, pltpu.VMEM)

    def moved(value, axis, pairs):
        return near(lax.ppermute(value, axis, pairs))

    def from_chip(shift, oy):
        if shift == 0 and oy == 0:
            return spread
        pairs = [
            (sx * ny + sy, (sx // pair + shift) % (nx // pair) * pair * ny + sx % pair * ny + (sy + oy) % ny)
            for sx in range(nx)
            for sy in range(ny)
        ]
        return moved(spread, ("gx", "gy"), pairs)

    pair = plan.pair
    blocks = []
    for shift in range(nx // pair):
        own = [from_chip(shift, oy) for oy in range(ny)]
        blocks += own
        if pair == 2:
            blocks += [moved(v, "gx", [(s, s ^ 1) for s in range(nx)]) for v in own]
    outs = pl.pallas_call(
        functools.partial(solve_kernel, plan),
        out_shape=[pltpu.VMEM((plan.zp, plan.lanes), f32)] * nz,
        in_specs=[vmem] * (nx * ny + 3),
        out_specs=[vmem] * nz,
        scratch_shapes=[
            pltpu.VMEM((plan.mid, LANES), f32),
            pltpu.VMEM((TERMS * plan.zp, plan.lanes), f32),
        ],
        compiler_params=params,
        name="solve",
    )(*blocks, *tables)
    parts = [outs[0]] + [
        moved(outs[o], "gz", [(s, (s + o) % nz) for s in range(nz)]) for o in range(1, nz)
    ]
    fine, atom = pl.pallas_call(
        functools.partial(gather_kernel, plan),
        out_shape=[
            jax.ShapeDtypeStruct(plan.local, f32),
            jax.ShapeDtypeStruct((LANES, slots), f32),
        ],
        in_specs=[vmem] * (nz + 2) + [hbm, vmem],
        out_specs=[vmem, vmem],
        scratch_shapes=[
            pltpu.VMEM((plan.lanes, LANES), f32),
            pltpu.VMEM((plan.columns * plan.zp, LANES), f32),
            pltpu.SMEM(nbins, jnp.int32),
            pltpu.SemaphoreType.DMA(()),
        ],
        compiler_params=params,
        name="gather",
    )(*parts, *weights, far(counts), pick)
    return fine, atom.reshape(charges.shape)


def solution(mesh):
    in_specs = (
        P("gx", "gy", "gz", None),
        P("gx", "gy", "gz", None),
        P("gx", "gy", "gz", None),
        P("gx", "gy", "gz", None),
        P("gx", "gy", "gz"),
    )
    out_specs = (P("gx", "gy", "gz"), P("gx", "gy", "gz", None))
    return jax.shard_map(body, mesh=mesh, in_specs=in_specs, out_specs=out_specs, check_vma=False)
```

```python
import functools
import math

import jax
import jax.numpy as jnp
import numpy as np
from jax import lax
from jax.experimental import pallas as pl
from jax.experimental.pallas import tpu as pltpu
from jax.sharding import PartitionSpec as P

R = 8
LANES = 128
TERMS = 5
SLOT = LANES // TERMS
PARTS = 4
GROUP = 8
RIM = 4
TAPS = (-0.0625, 0.0, 0.5625, 1.0, 0.5625, 0.0, -0.0625)
highest = lax.Precision.HIGHEST


def profile(family, offset):
    if family == 0:
        return math.exp(-((offset / (0.4 * R)) ** 2))
    if family == 1:
        return math.exp(-((offset / (0.8 * R)) ** 2))
    return 1.0 / (1.0 + (offset / R) ** 2)


def norm_factor(family):
    return sum(profile(family, float(o)) ** 2 for o in range(-R, R + 1)) ** 1.5


def stencil(points, family):
    matrix = np.zeros((points, points))
    for i in range(points):
        for k in range(max(0, i - R), min(points, i + R + 1)):
            matrix[i, k] = profile(family, float(k - i))
    return matrix


def restriction(points):
    matrix = np.zeros((points // 2, points))
    for i in range(points // 2):
        for k, tap in enumerate(TAPS):
            if 0 <= 2 * i + k - 3 < points:
                matrix[i, 2 * i + k - 3] += tap
    return matrix


def term_matrices(points):
    q_one = restriction(points)
    q_two = restriction(points // 2)
    coarse = points // 4
    far = np.array([[profile(2, float(k - i)) for k in range(coarse)] for i in range(coarse)])
    down = q_two @ q_one
    return [
        stencil(points, 0),
        stencil(points, 1),
        q_one.T @ stencil(points // 2, 0) @ q_one,
        q_one.T @ stencil(points // 2, 1) @ q_one,
        down.T @ far @ down,
    ]


def term_scales():
    n = [norm_factor(f) for f in range(3)]
    return [1.0 / n[0], 1.0 / n[1], 0.5 / n[0], 0.5 / n[1], 0.5 / n[2]]


def windowed(points, count):
    local = points // count
    width = local + RIM
    index = np.arange(count)[:, None] * local + np.arange(width)[None, :] - RIM // 2
    inside = (index >= 0) & (index < points)
    clipped = np.clip(index, 0, points - 1)
    both = inside[:, :, None, None] & inside[None, None]
    return np.stack(
        [np.where(both, m[clipped[:, :, None, None], clipped[None, None]], 0.0) for m in term_matrices(points)]
    )


def round_up(value, step):
    return -(-value // step) * step


def partner(device, order, count):
    return (device + order) % count


class Plan:
    def __init__(self, nbins, counts):
        self.nbins = nbins
        self.counts = counts
        self.local = (4 * nbins[0], 4 * nbins[1], 2 * nbins[2])
        self.width = tuple(v + RIM for v in self.local)
        self.points = tuple(v * c for v, c in zip(self.local, counts))
        self.xp = round_up(self.width[0], 8)
        self.zp = round_up(self.width[2], 8)
        self.chunks = -(-self.width[1] // TERMS)
        self.lanes = self.chunks * LANES
        self.columns = nbins[0] * nbins[1]
        self.mid = self.counts[1] * self.lanes
        self.pair = 2 if counts[0] % 2 == 0 else 1
        assert self.columns * nbins[2] == LANES and nbins[2] == 8 and self.columns % 2 == 0
        assert TERMS * self.zp <= LANES and self.width[0] <= SLOT

    def place_matrix(self):
        nbx, nby, _ = self.nbins
        m = np.zeros((self.width[1] * self.xp, self.columns * 64), np.float32)
        for a in range(nbx):
            for b in range(nby):
                for i in range(8):
                    for j in range(8):
                        m[(4 * b + j) * self.xp + 4 * a + i, (a * nby + b) * 64 + i * 8 + j] = 1.0
        return jnp.asarray(m, jnp.bfloat16)

    def pick_matrix(self):
        nbx, nby, _ = self.nbins
        m = np.zeros((self.columns * 64, self.lanes), np.float32)
        for a in range(nbx):
            for b in range(nby):
                for i in range(8):
                    for j in range(8):
                        chunk, part = divmod(4 * b + j, TERMS)
                        m[(a * nby + b) * 64 + i * 8 + j, chunk * LANES + part * SLOT + 4 * a + i] = 1.0
        return jnp.asarray(m, jnp.bfloat16)

    def x_table(self):
        nx, width = self.counts[0], self.width[0]
        m = windowed(self.points[0], nx)
        table = np.zeros((nx, nx * self.xp, LANES), np.float32)
        for d in range(nx):
            for o in range(nx):
                source = self.x_source(d, o)
                for t in range(TERMS):
                    table[d, o * self.xp : o * self.xp + width, t * SLOT : t * SLOT + width] = (
                        m[t, d, :, source, :].T
                    )
        return jnp.asarray(table)

    def x_source(self, device, order):
        pair = self.pair
        shift, other = divmod(order, pair)
        return (device // pair - shift) % (self.counts[0] // pair) * pair + (device % pair ^ other)

    def y_table(self):
        ny, width = self.counts[1], self.width[1]
        m = windowed(self.points[1], ny)
        table = np.zeros((ny, ny * width, self.chunks * TERMS, LANES), np.float32)
        for d in range(ny):
            for o in range(ny):
                for t in range(TERMS):
                    block = m[t, d, :, (d - o) % ny, :]
                    table[d, o * width : (o + 1) * width, :width, t * SLOT : (t + 1) * SLOT] = block.T[:, :, None]
        return jnp.asarray(table.reshape(ny, ny * width * self.chunks * TERMS, LANES))

    def z_table(self):
        nz, width = self.counts[2], self.width[2]
        m = windowed(self.points[2], nz)
        scales = term_scales()
        table = np.zeros((nz, nz * self.zp, TERMS * self.zp), np.float32)
        for d in range(nz):
            for o in range(nz):
                for t in range(TERMS):
                    table[d, o * self.zp : o * self.zp + width, t * self.zp : t * self.zp + width] = (
                        scales[t] * m[t, partner(d, o, nz), :, d, :]
                    )
        return jnp.asarray(table)


SCALE = (1.0 / 6.0) ** (1.0 / 3.0)


def bspline(scaled):
    a = jnp.abs(scaled)
    u = jnp.maximum(2.0 * SCALE - a, 0.0)
    v = jnp.maximum(SCALE - a, 0.0)
    return u * u * u - v * v * (4.0 * v)


def split_rows(value):
    high = value.astype(jnp.bfloat16).astype(jnp.float32)
    return jnp.concatenate([high, value - high], axis=0).astype(jnp.bfloat16)


def spread_kernel(plan, *refs):
    hbm, tables, (out_ref, outer_s, along_z_s) = refs[:6], refs[6:10], refs[10:13]
    tables_out, local, (column_s, sems) = refs[13:17], refs[17:23], refs[23:]
    copies = [pltpu.make_async_copy(a, b, sems.at[n]) for n, (a, b) in enumerate(zip(hbm, local))]
    for n, (table, target, axis) in enumerate(zip(tables, tables_out, ("gx", "gy", "gz", None))):
        source = table if axis is None else table.at[lax.axis_index(axis)]
        copies.append(pltpu.make_async_copy(source, target, sems.at[6 + n]))
    for copy in copies:
        copy.start()
    x_ref, y_ref, z_ref, charge_ref, counts_ref, place_s = local
    slots = charge_ref.shape[1]
    nbx, nby, nbz = plan.nbins
    zp = plan.zp
    node = (2.0 - lax.broadcasted_iota(jnp.int32, (8, slots), 0).astype(jnp.float32)) * SCALE
    slot = lax.broadcasted_iota(jnp.int32, (8, slots), 1)
    rank = lax.broadcasted_iota(jnp.int32, (8, LANES), 0)
    for copy in copies[:5]:
        copy.wait()
    for ref in (x_ref, y_ref, z_ref):
        ref[...] = ref[...] * SCALE

    def one_bin(p, c):
        r = p * nbz + c
        weight_x = bspline(x_ref[pl.ds(r, 1), :] + node)
        weight_y = bspline(y_ref[pl.ds(r, 1), :] + node)
        weight_z = bspline(z_ref[pl.ds(r, 1), :] + node)
        weight_z = jnp.where(slot < counts_ref[p // nby, p % nby, c], weight_z, 0.0)
        outer = split_rows(jnp.concatenate([weight_x[i : i + 1, :] * weight_y for i in range(8)], axis=0))
        outer_s[r // 2, :, (c % 2) * slots : (c % 2 + 1) * slots] = outer
        along_z_s[r] = weight_z
        return outer, split_rows(weight_z * charge_ref[pl.ds(r, 1), :])

    def one_column(p):
        sums = [jnp.zeros((8, LANES), jnp.float32) for _ in range(zp // 8)]
        for c in range(0, nbz, 2):
            (outer_a, z_a), (outer_b, z_b) = one_bin(p, c), one_bin(p, c + 1)
            none = jnp.zeros_like(z_a)
            both = lax.dot_general(
                jnp.concatenate(
                    [jnp.concatenate([z_a, none], axis=1), jnp.concatenate([none, z_b], axis=1)], axis=0
                ),
                jnp.concatenate([outer_a, outer_b], axis=1),
                (((1,), (1,)), ((), ())),
                preferred_element_type=jnp.float32,
            )
            for n in range(2):
                part = both[16 * n : 16 * n + 8, :] + both[16 * n + 8 : 16 * n + 16, :]
                at, shift = divmod(2 * (c + n), 8)
                if shift:
                    part = pltpu.roll(part, shift, 0)
                    sums[at] = sums[at] + jnp.where(rank >= shift, part, 0.0)
                    sums[at + 1] = sums[at + 1] + jnp.where(rank < shift, part, 0.0)
                else:
                    sums[at] = sums[at] + part
        return [v + pltpu.roll(v, 64, 1) for v in sums]

    left = lax.broadcasted_iota(jnp.int32, (8, LANES), 1) < 64

    def one_group(g, carry):
        for q in range(GROUP):
            pair = g * GROUP + q
            even = one_column(2 * pair)
            odd = one_column(2 * pair + 1)
            for n, (a, b) in enumerate(zip(even, odd)):
                column_s[pl.ds(pl.multiple_of(pair * zp, 8) + 8 * n, 8), :] = jnp.where(left, a, b)
        return carry

    lax.fori_loop(0, plan.columns // 2 // GROUP, one_group, 0)
    columns = jnp.concatenate(
        [column_s[p * plan.zp : (p + 1) * plan.zp, :] for p in range(plan.columns // 2)], axis=1
    )
    pad = jnp.zeros((LANES - 2 * zp, columns.shape[1]), jnp.bfloat16)
    copies[5].wait()
    grid = lax.dot_general(
        place_s[...], jnp.concatenate([split_rows(columns), pad], axis=0), (((1,), (1,)), ((), ())),
        preferred_element_type=jnp.float32,
    )
    grid = grid + pltpu.roll(grid, LANES - zp, 1)
    xp = plan.xp
    group = lax.broadcasted_iota(jnp.int32, (xp, LANES), 1) // plan.zp
    for chunk in range(plan.chunks):
        merged = jnp.zeros((xp, LANES), jnp.float32)
        for b in range(TERMS):
            y = chunk * TERMS + b
            if y < plan.width[1]:
                piece = grid[y * xp : (y + 1) * xp, :]
                moved = pltpu.roll(piece, b * plan.zp, 1) if b else piece
                merged = jnp.where(group == b, moved, merged)
        out_ref[:, chunk * LANES : (chunk + 1) * LANES] = merged
    for copy in copies[6:]:
        copy.wait()


def solve_kernel(plan, *refs):
    nx, ny, nz = plan.counts
    blocks = refs[: nx * ny]
    tables = refs[nx * ny : nx * ny + 3]
    outs = refs[nx * ny + 3 : nx * ny + 3 + nz]
    mid_s, term_s = refs[nx * ny + 3 + nz :]
    ytab_s = tables[1]
    x_matrix = tables[0][...]
    wy = plan.width[1]
    zp = plan.zp
    span = plan.chunks * TERMS
    for oy in range(ny):
        gathered = jnp.concatenate([blocks[ox * ny + oy][...] for ox in range(nx)], axis=0)
        mid_s[oy * plan.lanes : (oy + 1) * plan.lanes, :] = lax.dot_general(
            gathered, x_matrix, (((0,), (0,)), ((), ())), precision=highest,
            preferred_element_type=jnp.float32,
        )
    slot = lax.broadcasted_iota(jnp.int32, (zp, LANES), 1) // SLOT
    for chunk in range(plan.chunks):
        sums = [jnp.zeros((zp, LANES), jnp.float32) for _ in range(TERMS)]
        for oy in range(ny):
            for y in range(wy):
                at = oy * plan.lanes + (y // TERMS) * LANES + (y % TERMS) * zp
                value = mid_s[at : at + zp, :]
                for b in range(TERMS):
                    row = (oy * wy + y) * span + chunk * TERMS + b
                    sums[b] = sums[b] + value * ytab_s[row : row + 1, :]
        for t in range(TERMS):
            merged = jnp.zeros((zp, LANES), jnp.float32)
            for b in range(TERMS):
                shift = (SLOT * (b - t)) % LANES
                moved = pltpu.roll(sums[b], shift, 1) if shift else sums[b]
                merged = jnp.where(slot == b, moved, merged)
            term_s[t * zp : (t + 1) * zp, chunk * LANES : (chunk + 1) * LANES] = merged
    result = jnp.dot(tables[2][...], term_s[...], precision=highest, preferred_element_type=jnp.float32)
    for o in range(nz):
        outs[o][...] = result[o * zp : (o + 1) * zp, :]


def gather_kernel(plan, *refs):
    nz = plan.counts[2]
    parts = refs[:nz]
    outer_s, along_z_s, pick_ref, fine_hbm, atom_hbm = refs[nz : nz + 5]
    field_s, column_s, fine_ref, atom_ref, sems = refs[nz + 5 :]
    nbx, nby, nbz = plan.nbins
    zp = plan.zp
    lx, ly, lz = plan.local
    total = parts[0][...]
    for part in parts[1:]:
        total = total + part[...]
    columns = lax.dot_general(
        split_rows(total), pick_ref[...], (((1,), (1,)), ((), ())), preferred_element_type=jnp.float32
    )
    columns = columns[:zp, :] + columns[zp:, :]
    left = lax.broadcasted_iota(jnp.int32, (zp, LANES), 1) < 64
    for pair in range(plan.columns // 2):
        both = columns[:, pair * LANES : (pair + 1) * LANES]
        turned = pltpu.roll(both, 64, 1)
        column_s[2 * pair * zp : (2 * pair + 1) * zp, :] = jnp.where(left, both, turned)
        column_s[(2 * pair + 1) * zp : (2 * pair + 2) * zp, :] = jnp.where(left, turned, both)
    for chunk in range(plan.chunks):
        turned = total[:, chunk * LANES : (chunk + 1) * LANES].T
        field_s[chunk * LANES : (chunk + 1) * LANES, :zp] = turned
    for y in range(ly):
        chunk, b = divmod(y + 2, TERMS)
        at = chunk * LANES + b * SLOT + 2
        fine_ref[:, y, :] = field_s[at : at + lx, 2 : 2 + lz]
    copies = [pltpu.make_async_copy(fine_ref, fine_hbm, sems.at[0])]
    copies[0].start()
    slots = atom_ref.shape[1]

    def one_column(p):
        rows = []
        for c in range(0, nbz, 2):
            patches = [
                split_rows(column_s[p * zp + 2 * n : p * zp + 2 * n + 8, :]) for n in (c, c + 1)
            ]
            both = jnp.dot(
                jnp.concatenate(patches, axis=0), outer_s[(p * nbz + c) // 2],
                preferred_element_type=jnp.float32,
            )
            for n in range(2):
                field = both[16 * n : 16 * n + 8, n * slots : (n + 1) * slots]
                field = field + both[16 * n + 8 : 16 * n + 16, n * slots : (n + 1) * slots]
                rows.append(jnp.sum(field * along_z_s[p * nbz + c + n], axis=0, keepdims=True))
        atom_ref[p * nbz : (p + 1) * nbz, :] = jnp.concatenate(rows, axis=0)

    for part in range(PARTS):
        span = LANES // PARTS
        for p in range(part * span // nbz, (part + 1) * span // nbz):
            one_column(p)
        rows = pl.ds(part * span, span)
        copies.append(pltpu.make_async_copy(atom_ref.at[rows], atom_hbm.at[rows], sems.at[1 + part]))
        copies[-1].start()
    for copy in copies:
        copy.wait()


def body(charges, offset_x, offset_y, offset_z, counts):
    nbins = charges.shape[:3]
    slots = charges.shape[3]
    sizes = tuple(lax.axis_size(a) for a in ("gx", "gy", "gz"))
    nx, ny, nz = sizes
    plan = Plan(nbins, sizes)
    flat = [v.reshape(LANES, slots) for v in (charges, offset_x, offset_y, offset_z)]
    vmem = pl.BlockSpec(memory_space=pltpu.VMEM)
    hbm = pl.BlockSpec(memory_space=pltpu.HBM)
    f32 = jnp.float32
    params = pltpu.CompilerParams(vmem_limit_bytes=12 << 20)
    place, pick = plan.place_matrix(), plan.pick_matrix()

    def far(value):
        return pltpu.with_memory_space_constraint(value, pltpu.HBM)

    tables = (plan.x_table(), plan.y_table(), plan.z_table(), pick)
    spread, *weights = pl.pallas_call(
        functools.partial(spread_kernel, plan),
        out_shape=[
            pltpu.VMEM((plan.xp, plan.lanes), f32),
            pltpu.VMEM((LANES // 2, LANES, 2 * slots), jnp.bfloat16),
            pltpu.VMEM((LANES, 8, slots), f32),
        ]
        + [pltpu.VMEM(t.shape[1:], t.dtype) for t in tables[:3]]
        + [pltpu.VMEM(pick.shape, pick.dtype)],
        in_specs=[hbm] * 10,
        out_specs=[vmem] * 7,
        scratch_shapes=[pltpu.VMEM((LANES, slots), f32)] * 4
        + [
            pltpu.SMEM(nbins, jnp.int32),
            pltpu.VMEM(place.shape, place.dtype),
            pltpu.VMEM((plan.columns // 2 * plan.zp, LANES), f32),
            pltpu.SemaphoreType.DMA((10,)),
        ],
        compiler_params=params,
        name="spread",
    )(*(far(v) for v in (*flat[1:], flat[0], counts, place, *tables)))
    weights, tables, pick = weights[:2], weights[2:5], weights[5]

    def near(value):
        return pltpu.with_memory_space_constraint(value, pltpu.VMEM)

    def moved(value, axis, pairs):
        return near(lax.ppermute(value, axis, pairs))

    def from_chip(shift, oy):
        if shift == 0 and oy == 0:
            return spread
        pairs = [
            (sx * ny + sy, (sx // pair + shift) % (nx // pair) * pair * ny + sx % pair * ny + (sy + oy) % ny)
            for sx in range(nx)
            for sy in range(ny)
        ]
        return moved(spread, ("gx", "gy"), pairs)

    pair = plan.pair
    blocks = []
    for shift in range(nx // pair):
        own = [from_chip(shift, oy) for oy in range(ny)]
        blocks += own
        if pair == 2:
            blocks += [moved(v, "gx", [(s, s ^ 1) for s in range(nx)]) for v in own]
    outs = pl.pallas_call(
        functools.partial(solve_kernel, plan),
        out_shape=[pltpu.VMEM((plan.zp, plan.lanes), f32)] * nz,
        in_specs=[vmem] * (nx * ny + 3),
        out_specs=[vmem] * nz,
        scratch_shapes=[
            pltpu.VMEM((plan.mid, LANES), f32),
            pltpu.VMEM((TERMS * plan.zp, plan.lanes), f32),
        ],
        compiler_params=params,
        name="solve",
    )(*blocks, *tables)
    parts = [outs[0]] + [
        moved(outs[o], "gz", [(s, partner(s, o, nz)) for s in range(nz)]) for o in range(1, nz)
    ]
    fine, atom = pl.pallas_call(
        functools.partial(gather_kernel, plan),
        out_shape=[
            jax.ShapeDtypeStruct(plan.local, f32),
            jax.ShapeDtypeStruct((LANES, slots), f32),
        ],
        in_specs=[vmem] * (nz + 3),
        out_specs=[hbm, hbm],
        scratch_shapes=[
            pltpu.VMEM((plan.lanes, LANES), f32),
            pltpu.VMEM((plan.columns * plan.zp, LANES), f32),
            pltpu.VMEM(plan.local, f32),
            pltpu.VMEM((LANES, slots), f32),
            pltpu.SemaphoreType.DMA((1 + PARTS,)),
        ],
        compiler_params=params,
        name="gather",
    )(*parts, *weights, pick)
    return fine, atom.reshape(charges.shape)


def solution(mesh):
    in_specs = (
        P("gx", "gy", "gz", None),
        P("gx", "gy", "gz", None),
        P("gx", "gy", "gz", None),
        P("gx", "gy", "gz", None),
        P("gx", "gy", "gz"),
    )
    out_specs = (P("gx", "gy", "gz"), P("gx", "gy", "gz", None))
    return jax.shard_map(body, mesh=mesh, in_specs=in_specs, out_specs=out_specs, check_vma=False)
```

```python
import functools
import math

import jax
import jax.numpy as jnp
import numpy as np
from jax import lax
from jax.experimental import pallas as pl
from jax.experimental.pallas import tpu as pltpu
from jax.sharding import PartitionSpec as P

R = 8
LANES = 128
TERMS = 5
SLOT = LANES // TERMS
PARTS = 4
RIM = 4
TAPS = (-0.0625, 0.0, 0.5625, 1.0, 0.5625, 0.0, -0.0625)
highest = lax.Precision.HIGHEST


def profile(family, offset):
    if family == 0:
        return math.exp(-((offset / (0.4 * R)) ** 2))
    if family == 1:
        return math.exp(-((offset / (0.8 * R)) ** 2))
    return 1.0 / (1.0 + (offset / R) ** 2)


def norm_factor(family):
    return sum(profile(family, float(o)) ** 2 for o in range(-R, R + 1)) ** 1.5


def stencil(points, family):
    matrix = np.zeros((points, points))
    for i in range(points):
        for k in range(max(0, i - R), min(points, i + R + 1)):
            matrix[i, k] = profile(family, float(k - i))
    return matrix


def restriction(points):
    matrix = np.zeros((points // 2, points))
    for i in range(points // 2):
        for k, tap in enumerate(TAPS):
            if 0 <= 2 * i + k - 3 < points:
                matrix[i, 2 * i + k - 3] += tap
    return matrix


def term_matrices(points):
    q_one = restriction(points)
    q_two = restriction(points // 2)
    coarse = points // 4
    far = np.array([[profile(2, float(k - i)) for k in range(coarse)] for i in range(coarse)])
    down = q_two @ q_one
    return [
        stencil(points, 0),
        stencil(points, 1),
        q_one.T @ stencil(points // 2, 0) @ q_one,
        q_one.T @ stencil(points // 2, 1) @ q_one,
        down.T @ far @ down,
    ]


def term_scales():
    n = [norm_factor(f) for f in range(3)]
    return [1.0 / n[0], 1.0 / n[1], 0.5 / n[0], 0.5 / n[1], 0.5 / n[2]]


def windowed(points, count):
    local = points // count
    width = local + RIM
    index = np.arange(count)[:, None] * local + np.arange(width)[None, :] - RIM // 2
    inside = (index >= 0) & (index < points)
    clipped = np.clip(index, 0, points - 1)
    both = inside[:, :, None, None] & inside[None, None]
    return np.stack(
        [np.where(both, m[clipped[:, :, None, None], clipped[None, None]], 0.0) for m in term_matrices(points)]
    )


def round_up(value, step):
    return -(-value // step) * step


def halves(table):
    high = table.astype(jnp.bfloat16)
    return high, (table - high.astype(np.float32)).astype(jnp.bfloat16)


def partner(device, order, count):
    return (device + order) % count


class Plan:
    def __init__(self, nbins, counts):
        self.nbins = nbins
        self.counts = counts
        self.local = (4 * nbins[0], 4 * nbins[1], 2 * nbins[2])
        self.width = tuple(v + RIM for v in self.local)
        self.points = tuple(v * c for v, c in zip(self.local, counts))
        self.xp = round_up(self.width[0], 8)
        self.zp = round_up(self.width[2], 8)
        self.chunks = -(-self.width[1] // TERMS)
        self.lanes = self.chunks * LANES
        self.columns = nbins[0] * nbins[1]
        self.mid = self.counts[1] * self.lanes
        self.pair = 2 if counts[0] % 2 == 0 else 1
        assert self.columns * nbins[2] == LANES and nbins[2] == 8 and self.columns % 2 == 0
        assert TERMS * self.zp <= LANES and self.width[0] <= SLOT

    def x_table(self):
        nx, width = self.counts[0], self.width[0]
        m = windowed(self.points[0], nx)
        table = np.zeros((nx, nx * self.xp, LANES), np.float32)
        for d in range(nx):
            for o in range(nx):
                source = self.x_source(d, o)
                for t in range(TERMS):
                    table[d, o * self.xp : o * self.xp + width, t * SLOT : t * SLOT + width] = (
                        m[t, d, :, source, :].T
                    )
        high, low = halves(table)
        upper = np.concatenate([high, low], axis=2)
        lower = np.concatenate([high, np.zeros_like(low)], axis=2)
        return jnp.asarray(np.concatenate([upper, lower], axis=1))

    def x_source(self, device, order):
        pair = self.pair
        shift, other = divmod(order, pair)
        return (device // pair - shift) % (self.counts[0] // pair) * pair + (device % pair ^ other)

    def y_table(self):
        ny, width = self.counts[1], self.width[1]
        m = windowed(self.points[1], ny)
        table = np.zeros((ny, ny * width, self.chunks * TERMS, LANES), np.float32)
        for d in range(ny):
            for o in range(ny):
                for t in range(TERMS):
                    block = m[t, d, :, (d - o) % ny, :]
                    table[d, o * width : (o + 1) * width, :width, t * SLOT : (t + 1) * SLOT] = block.T[:, :, None]
        return jnp.asarray(table.reshape(ny, ny * width * self.chunks * TERMS, LANES))

    def z_table(self):
        nz, width = self.counts[2], self.width[2]
        m = windowed(self.points[2], nz)
        scales = term_scales()
        table = np.zeros((nz, nz * self.zp, TERMS * self.zp), np.float32)
        for d in range(nz):
            for o in range(nz):
                for t in range(TERMS):
                    table[d, o * self.zp : o * self.zp + width, t * self.zp : t * self.zp + width] = (
                        scales[t] * m[t, partner(d, o, nz), :, d, :]
                    )
        high, low = halves(table)
        upper = np.concatenate([high, high], axis=2)
        lower = np.concatenate([low, np.zeros_like(low)], axis=2)
        return jnp.asarray(np.concatenate([upper, lower], axis=1))


SCALE = (1.0 / 6.0) ** (1.0 / 3.0)


def bspline(scaled):
    a = jnp.abs(scaled)
    u = jnp.maximum(2.0 * SCALE - a, 0.0)
    v = jnp.maximum(SCALE - a, 0.0)
    return u * u * u - v * v * (4.0 * v)


def split_rows(value):
    high = value.astype(jnp.bfloat16).astype(jnp.float32)
    return jnp.concatenate([high, value - high], axis=0).astype(jnp.bfloat16)


def spread_kernel(plan, *refs):
    hbm, tables, (out_ref, outer_s, along_z_s) = refs[:5], refs[5:8], refs[8:11]
    tables_out, local, (column_s, turned_s, grid_s, sems) = refs[11:14], refs[14:19], refs[19:]
    copies = [pltpu.make_async_copy(a, b, sems.at[n]) for n, (a, b) in enumerate(zip(hbm, local))]
    for n, (table, target, axis) in enumerate(zip(tables, tables_out, ("gx", "gy", "gz"))):
        copies.append(pltpu.make_async_copy(table.at[lax.axis_index(axis)], target, sems.at[5 + n]))
    for copy in copies:
        copy.start()
    x_ref, y_ref, z_ref, charge_ref, counts_ref = local
    slots = charge_ref.shape[1]
    nbx, nby, nbz = plan.nbins
    zp = plan.zp
    node = (2.0 - lax.broadcasted_iota(jnp.int32, (8, slots), 0).astype(jnp.float32)) * SCALE
    slot = lax.broadcasted_iota(jnp.int32, (8, slots), 1)
    rank = lax.broadcasted_iota(jnp.int32, (8, LANES), 0)
    for copy in copies[:5]:
        copy.wait()
    for ref in (x_ref, y_ref, z_ref):
        ref[...] = ref[...] * SCALE

    def one_bin(p, c):
        r = p * nbz + c
        weight_x = bspline(x_ref[pl.ds(r, 1), :] + node)
        weight_y = bspline(y_ref[pl.ds(r, 1), :] + node)
        weight_z = bspline(z_ref[pl.ds(r, 1), :] + node)
        weight_z = jnp.where(slot < counts_ref[p // nby, p % nby, c], weight_z, 0.0)
        outer = split_rows(
            jnp.concatenate([weight_y[j : j + 1, :] * weight_x for j in range(8)], axis=0)
        )
        outer_s[r // 2, :, (c % 2) * slots : (c % 2 + 1) * slots] = outer
        along_z_s[r] = weight_z
        return outer, split_rows(weight_z * charge_ref[pl.ds(r, 1), :])

    def one_column(p):
        sums = [jnp.zeros((8, LANES), jnp.float32) for _ in range(zp // 8)]
        for c in range(0, nbz, 2):
            (outer_a, z_a), (outer_b, z_b) = one_bin(p, c), one_bin(p, c + 1)
            none = jnp.zeros_like(z_a)
            both = lax.dot_general(
                jnp.concatenate(
                    [jnp.concatenate([z_a, none], axis=1), jnp.concatenate([none, z_b], axis=1)], axis=0
                ),
                jnp.concatenate([outer_a, outer_b], axis=1),
                (((1,), (1,)), ((), ())),
                preferred_element_type=jnp.float32,
            )
            for n in range(2):
                part = both[16 * n : 16 * n + 8, :] + both[16 * n + 8 : 16 * n + 16, :]
                at, shift = divmod(2 * (c + n), 8)
                if shift:
                    part = pltpu.roll(part, shift, 0)
                    sums[at] = sums[at] + jnp.where(rank >= shift, part, 0.0)
                    sums[at + 1] = sums[at + 1] + jnp.where(rank < shift, part, 0.0)
                else:
                    sums[at] = sums[at] + part
        return [v + pltpu.roll(v, 64, 1) for v in sums]

    left = lax.broadcasted_iota(jnp.int32, (8, LANES), 1) < 64

    for pair in range(plan.columns // 2):
        even = one_column(2 * pair)
        odd = one_column(2 * pair + 1)
        for n, (a, b) in enumerate(zip(even, odd)):
            at = pair * zp + 8 * n
            column_s[at : at + 8, :] = jnp.where(left, a, b)
    xp = plan.xp
    for pair in range(plan.columns // 2):
        turned_s[pair * LANES : (pair + 1) * LANES, :zp] = column_s[pair * zp : (pair + 1) * zp, :].T

    def folded(a, y):
        total = None
        for b in range(nby):
            j = y - 4 * b
            if 0 <= j < 8:
                at = (a * nby + b) * 64 + j * 8
                piece = turned_s[at : at + 8, :]
                total = piece if total is None else total + piece
        return total

    for y in range(plan.width[1]):
        for a in range(0, nbx, 2):
            grid_s[y * xp + 4 * a : y * xp + 4 * a + 8, :] = folded(a, y)
        rest = xp - 4 * nbx
        grid_s[(y + 1) * xp - rest : (y + 1) * xp, :] = jnp.zeros((rest, LANES), jnp.float32)
        for a in range(1, nbx, 2):
            at = slice(y * xp + 4 * a, y * xp + 4 * a + 8)
            grid_s[at, :] = grid_s[at, :] + folded(a, y)
    group = lax.broadcasted_iota(jnp.int32, (xp, LANES), 1) // plan.zp
    for chunk in range(plan.chunks):
        merged = jnp.zeros((xp, LANES), jnp.float32)
        for b in range(TERMS):
            y = chunk * TERMS + b
            if y < plan.width[1]:
                piece = grid_s[y * xp : (y + 1) * xp, :]
                moved = pltpu.roll(piece, b * plan.zp, 1) if b else piece
                merged = jnp.where(group == b, moved, merged)
        out_ref[:, chunk * LANES : (chunk + 1) * LANES] = merged
    for copy in copies[5:]:
        copy.wait()


def solve_kernel(plan, *refs):
    nx, ny, nz = plan.counts
    blocks = refs[: nx * ny]
    tables = refs[nx * ny : nx * ny + 3]
    outs = refs[nx * ny + 3 : nx * ny + 3 + nz]
    mid_s, term_s = refs[nx * ny + 3 + nz :]
    ytab_s = tables[1]
    x_matrix = tables[0][...]
    wy = plan.width[1]
    zp = plan.zp
    span = plan.chunks * TERMS
    for oy in range(ny):
        gathered = jnp.concatenate([blocks[ox * ny + oy][...] for ox in range(nx)], axis=0)
        both = lax.dot_general(
            split_rows(gathered), x_matrix, (((0,), (0,)), ((), ())), preferred_element_type=jnp.float32
        )
        mid_s[oy * plan.lanes : (oy + 1) * plan.lanes, :] = both[:, :LANES] + both[:, LANES:]
    slot = lax.broadcasted_iota(jnp.int32, (zp, LANES), 1) // SLOT
    for chunk in range(plan.chunks):
        sums = [jnp.zeros((zp, LANES), jnp.float32) for _ in range(TERMS)]
        for oy in range(ny):
            for y in range(wy):
                at = oy * plan.lanes + (y // TERMS) * LANES + (y % TERMS) * zp
                value = mid_s[at : at + zp, :]
                for b in range(TERMS):
                    row = (oy * wy + y) * span + chunk * TERMS + b
                    sums[b] = sums[b] + value * ytab_s[row : row + 1, :]
        for t in range(TERMS):
            merged = jnp.zeros((zp, LANES), jnp.float32)
            for b in range(TERMS):
                shift = (SLOT * (b - t)) % LANES
                moved = pltpu.roll(sums[b], shift, 1) if shift else sums[b]
                merged = jnp.where(slot == b, moved, merged)
            term_s[t * zp : (t + 1) * zp, chunk * LANES : (chunk + 1) * LANES] = merged
    both = jnp.dot(tables[2][...], split_rows(term_s[...]), preferred_element_type=jnp.float32)
    result = both[: nz * zp, :] + both[nz * zp :, :]
    for o in range(nz):
        outs[o][...] = result[o * zp : (o + 1) * zp, :]


def gather_kernel(plan, *refs):
    nz = plan.counts[2]
    parts = refs[:nz]
    outer_s, along_z_s, fine_hbm, atom_hbm = refs[nz : nz + 4]
    field_s, column_s, turned_s, inner_s, order_s, fine_ref, atom_ref, sems = refs[nz + 4 :]
    nbx, nby, nbz = plan.nbins
    zp = plan.zp
    lx, ly, lz = plan.local
    total = parts[0][...]
    for part in parts[1:]:
        total = total + part[...]
    for chunk in range(plan.chunks):
        field_s[chunk * LANES : (chunk + 1) * LANES, :zp] = total[:, chunk * LANES : (chunk + 1) * LANES].T
    left = lax.broadcasted_iota(jnp.int32, (zp, LANES), 1) < 64
    for pair in range(plan.columns // 2):
        for half in range(2):
            a, b = divmod(2 * pair + half, nby)
            for j in range(8):
                chunk, part = divmod(4 * b + j, TERMS)
                at = chunk * LANES + part * SLOT + 4 * a
                to = pair * LANES + half * 64 + j * 8
                turned_s[to : to + 8, :] = field_s[at : at + 8, :]
        both = turned_s[pair * LANES : (pair + 1) * LANES, :zp].T
        turned = pltpu.roll(both, 64, 1)
        column_s[2 * pair * zp : (2 * pair + 1) * zp, :] = jnp.where(left, both, turned)
        column_s[(2 * pair + 1) * zp : (2 * pair + 2) * zp, :] = jnp.where(left, turned, both)
    for chunk in range(plan.chunks):
        inner_s[chunk * LANES : (chunk + 1) * LANES, :lz] = total[
            2 : 2 + lz, chunk * LANES : (chunk + 1) * LANES
        ].T
    for y in range(ly):
        chunk, b = divmod(y + 2, TERMS)
        at = chunk * LANES + b * SLOT + 2
        order_s[pl.ds(y, lx, stride=ly), :] = inner_s[at : at + lx, :]
    for x in range(lx):
        fine_ref[x] = order_s[x * ly : (x + 1) * ly, :lz]
    copies = [pltpu.make_async_copy(fine_ref, fine_hbm, sems.at[0])]
    copies[0].start()
    slots = atom_ref.shape[1]

    def one_column(p):
        rows = []
        for c in range(0, nbz, 2):
            patches = [
                split_rows(column_s[p * zp + 2 * n : p * zp + 2 * n + 8, :]) for n in (c, c + 1)
            ]
            both = jnp.dot(
                jnp.concatenate(patches, axis=0), outer_s[(p * nbz + c) // 2],
                preferred_element_type=jnp.float32,
            )
            for n in range(2):
                field = both[16 * n : 16 * n + 8, n * slots : (n + 1) * slots]
                field = field + both[16 * n + 8 : 16 * n + 16, n * slots : (n + 1) * slots]
                rows.append(jnp.sum(field * along_z_s[p * nbz + c + n], axis=0, keepdims=True))
        atom_ref[p * nbz : (p + 1) * nbz, :] = jnp.concatenate(rows, axis=0)

    for part in range(PARTS):
        span = LANES // PARTS
        for p in range(part * span // nbz, (part + 1) * span // nbz):
            one_column(p)
        rows = pl.ds(part * span, span)
        copies.append(pltpu.make_async_copy(atom_ref.at[rows], atom_hbm.at[rows], sems.at[1 + part]))
        copies[-1].start()
    for copy in copies:
        copy.wait()


def body(charges, offset_x, offset_y, offset_z, counts):
    nbins = charges.shape[:3]
    slots = charges.shape[3]
    sizes = tuple(lax.axis_size(a) for a in ("gx", "gy", "gz"))
    nx, ny, nz = sizes
    plan = Plan(nbins, sizes)
    flat = [v.reshape(LANES, slots) for v in (charges, offset_x, offset_y, offset_z)]
    vmem = pl.BlockSpec(memory_space=pltpu.VMEM)
    hbm = pl.BlockSpec(memory_space=pltpu.HBM)
    f32 = jnp.float32
    params = pltpu.CompilerParams(vmem_limit_bytes=12 << 20)

    def far(value):
        return pltpu.with_memory_space_constraint(value, pltpu.HBM)

    tables = (plan.x_table(), plan.y_table(), plan.z_table())
    spread, *weights = pl.pallas_call(
        functools.partial(spread_kernel, plan),
        out_shape=[
            pltpu.VMEM((plan.xp, plan.lanes), f32),
            pltpu.VMEM((LANES // 2, LANES, 2 * slots), jnp.bfloat16),
            pltpu.VMEM((LANES, 8, slots), f32),
        ]
        + [pltpu.VMEM(t.shape[1:], t.dtype) for t in tables],
        in_specs=[hbm] * 8,
        out_specs=[vmem] * 6,
        scratch_shapes=[pltpu.VMEM((LANES, slots), f32)] * 4
        + [
            pltpu.SMEM(nbins, jnp.int32),
            pltpu.VMEM((plan.columns // 2 * plan.zp, LANES), f32),
            pltpu.VMEM((plan.columns * 64, LANES), f32),
            pltpu.VMEM((plan.width[1] * plan.xp, LANES), f32),
            pltpu.SemaphoreType.DMA((8,)),
        ],
        compiler_params=params,
        name="spread",
    )(*(far(v) for v in (*flat[1:], flat[0], counts, *tables)))
    weights, tables = weights[:2], weights[2:]

    def near(value):
        return pltpu.with_memory_space_constraint(value, pltpu.VMEM)

    def moved(value, axis, pairs):
        return near(lax.ppermute(value, axis, pairs))

    def from_chip(shift, oy):
        if shift == 0 and oy == 0:
            return spread
        pairs = [
            (sx * ny + sy, (sx // pair + shift) % (nx // pair) * pair * ny + sx % pair * ny + (sy + oy) % ny)
            for sx in range(nx)
            for sy in range(ny)
        ]
        return moved(spread, ("gx", "gy"), pairs)

    pair = plan.pair
    blocks = []
    for shift in range(nx // pair):
        own = [from_chip(shift, oy) for oy in range(ny)]
        blocks += own
        if pair == 2:
            blocks += [moved(v, "gx", [(s, s ^ 1) for s in range(nx)]) for v in own]
    outs = pl.pallas_call(
        functools.partial(solve_kernel, plan),
        out_shape=[pltpu.VMEM((plan.zp, plan.lanes), f32)] * nz,
        in_specs=[vmem] * (nx * ny + 3),
        out_specs=[vmem] * nz,
        scratch_shapes=[
            pltpu.VMEM((plan.mid, LANES), f32),
            pltpu.VMEM((TERMS * plan.zp, plan.lanes), f32),
        ],
        compiler_params=params,
        name="solve",
    )(*blocks, *tables)
    parts = [outs[0]] + [
        moved(outs[o], "gz", [(s, partner(s, o, nz)) for s in range(nz)]) for o in range(1, nz)
    ]
    fine, atom = pl.pallas_call(
        functools.partial(gather_kernel, plan),
        out_shape=[
            jax.ShapeDtypeStruct(plan.local, f32),
            jax.ShapeDtypeStruct((LANES, slots), f32),
        ],
        in_specs=[vmem] * (nz + 2),
        out_specs=[hbm, hbm],
        scratch_shapes=[
            pltpu.VMEM((plan.lanes, LANES), f32),
            pltpu.VMEM((plan.columns * plan.zp, LANES), f32),
            pltpu.VMEM((plan.columns * 64, LANES), f32),
            pltpu.VMEM((plan.lanes, LANES), f32),
            pltpu.VMEM((plan.local[0] * plan.local[1], LANES), f32),
            pltpu.VMEM(plan.local, f32),
            pltpu.VMEM((LANES, slots), f32),
            pltpu.SemaphoreType.DMA((1 + PARTS,)),
        ],
        compiler_params=params,
        name="gather",
    )(*parts, *weights)
    return fine, atom.reshape(charges.shape)


def solution(mesh):
    in_specs = (
        P("gx", "gy", "gz", None),
        P("gx", "gy", "gz", None),
        P("gx", "gy", "gz", None),
        P("gx", "gy", "gz", None),
        P("gx", "gy", "gz"),
    )
    out_specs = (P("gx", "gy", "gz"), P("gx", "gy", "gz", None))
    return jax.shard_map(body, mesh=mesh, in_specs=in_specs, out_specs=out_specs, check_vma=False)
```

```python
import functools
import math

import jax
import jax.numpy as jnp
import numpy as np
from jax import lax
from jax.experimental import pallas as pl
from jax.experimental.pallas import tpu as pltpu
from jax.sharding import PartitionSpec as P

R = 8
LANES = 128
TERMS = 5
SLOT = LANES // TERMS
PARTS = 4
RIM = 4
TAPS = (-0.0625, 0.0, 0.5625, 1.0, 0.5625, 0.0, -0.0625)
highest = lax.Precision.HIGHEST


def profile(family, offset):
    if family == 0:
        return math.exp(-((offset / (0.4 * R)) ** 2))
    if family == 1:
        return math.exp(-((offset / (0.8 * R)) ** 2))
    return 1.0 / (1.0 + (offset / R) ** 2)


def norm_factor(family):
    return sum(profile(family, float(o)) ** 2 for o in range(-R, R + 1)) ** 1.5


def stencil(points, family):
    matrix = np.zeros((points, points))
    for i in range(points):
        for k in range(max(0, i - R), min(points, i + R + 1)):
            matrix[i, k] = profile(family, float(k - i))
    return matrix


def restriction(points):
    matrix = np.zeros((points // 2, points))
    for i in range(points // 2):
        for k, tap in enumerate(TAPS):
            if 0 <= 2 * i + k - 3 < points:
                matrix[i, 2 * i + k - 3] += tap
    return matrix


def term_matrices(points):
    q_one = restriction(points)
    q_two = restriction(points // 2)
    coarse = points // 4
    far = np.array([[profile(2, float(k - i)) for k in range(coarse)] for i in range(coarse)])
    down = q_two @ q_one
    return [
        stencil(points, 0),
        stencil(points, 1),
        q_one.T @ stencil(points // 2, 0) @ q_one,
        q_one.T @ stencil(points // 2, 1) @ q_one,
        down.T @ far @ down,
    ]


def term_scales():
    n = [norm_factor(f) for f in range(3)]
    return [1.0 / n[0], 1.0 / n[1], 0.5 / n[0], 0.5 / n[1], 0.5 / n[2]]


def windowed(points, count):
    local = points // count
    width = local + RIM
    index = np.arange(count)[:, None] * local + np.arange(width)[None, :] - RIM // 2
    inside = (index >= 0) & (index < points)
    clipped = np.clip(index, 0, points - 1)
    both = inside[:, :, None, None] & inside[None, None]
    return np.stack(
        [np.where(both, m[clipped[:, :, None, None], clipped[None, None]], 0.0) for m in term_matrices(points)]
    )


def round_up(value, step):
    return -(-value // step) * step


def halves(table):
    high = table.astype(jnp.bfloat16)
    return high, (table - high.astype(np.float32)).astype(jnp.bfloat16)


def partner(device, order, count):
    return (device + order) % count


class Plan:
    def __init__(self, nbins, counts):
        self.nbins = nbins
        self.counts = counts
        self.local = (4 * nbins[0], 4 * nbins[1], 2 * nbins[2])
        self.width = tuple(v + RIM for v in self.local)
        self.points = tuple(v * c for v, c in zip(self.local, counts))
        self.xp = round_up(self.width[0], 8)
        self.zp = round_up(self.width[2], 8)
        self.kept = self.width[1] - RIM // 2 if counts[1] <= 2 else self.width[1]
        self.per = LANES // max(self.width[0], self.width[2])
        self.step = LANES // self.per
        self.chunks = -(-self.kept // self.per)
        self.lanes = self.chunks * LANES
        self.columns = nbins[0] * nbins[1]
        self.mid = self.counts[1] * self.lanes
        self.pair = 2 if counts[0] % 2 == 0 else 1
        assert self.columns * nbins[2] == LANES and nbins[2] == 8 and self.columns % 2 == 0
        assert self.width[0] <= SLOT and max(self.width[0], self.width[2]) <= self.step

    def first(self, device):
        return RIM // 2 if self.counts[1] <= 2 and device == 0 else 0

    def first_here(self):
        if self.counts[1] > 2:
            return 0
        return jnp.where(lax.axis_index("gy") == 0, RIM // 2, 0)

    def row(self, y):
        return y // self.per * LANES + y % self.per * self.step

    def x_table(self):
        nx, width = self.counts[0], self.width[0]
        m = windowed(self.points[0], nx)
        table = np.zeros((nx, nx * self.xp, LANES), np.float32)
        for d in range(nx):
            for o in range(nx):
                source = self.x_source(d, o)
                for t in range(TERMS):
                    table[d, o * self.xp : o * self.xp + width, t * SLOT : t * SLOT + width] = (
                        m[t, d, :, source, :].T
                    )
        high, low = halves(table)
        upper = np.concatenate([high, low], axis=2)
        lower = np.concatenate([high, np.zeros_like(low)], axis=2)
        return jnp.asarray(np.concatenate([upper, lower], axis=1))

    def x_source(self, device, order):
        pair = self.pair
        shift, other = divmod(order, pair)
        return (device // pair - shift) % (self.counts[0] // pair) * pair + (device % pair ^ other)

    def y_table(self):
        ny, kept = self.counts[1], self.kept
        m = windowed(self.points[1], ny)
        table = np.zeros((ny, ny * kept, self.chunks * self.per, LANES), np.float32)
        for d in range(ny):
            for o in range(ny):
                source = (d - o) % ny
                target_at, source_at = self.first(d), self.first(source)
                for t in range(TERMS):
                    block = m[t, d, target_at : target_at + kept, source, source_at : source_at + kept]
                    table[d, o * kept : (o + 1) * kept, :kept, t * SLOT : (t + 1) * SLOT] = block.T[:, :, None]
        return jnp.asarray(table.reshape(ny, ny * kept * self.chunks * self.per, LANES))

    def z_table(self):
        nz, width = self.counts[2], self.width[2]
        m = windowed(self.points[2], nz)
        scales = term_scales()
        table = np.zeros((nz, nz * self.zp, TERMS * self.zp), np.float32)
        for d in range(nz):
            for o in range(nz):
                for t in range(TERMS):
                    table[d, o * self.zp : o * self.zp + width, t * self.zp : t * self.zp + width] = (
                        scales[t] * m[t, partner(d, o, nz), :, d, :]
                    )
        high, low = halves(table)
        upper = np.concatenate([high, high], axis=2)
        lower = np.concatenate([low, np.zeros_like(low)], axis=2)
        return jnp.asarray(np.concatenate([upper, lower], axis=1))


SCALE = (1.0 / 6.0) ** (1.0 / 3.0)


def bspline(scaled):
    a = jnp.abs(scaled)
    u = jnp.maximum(2.0 * SCALE - a, 0.0)
    v = jnp.maximum(SCALE - a, 0.0)
    return u * u * u - v * v * (4.0 * v)


def split_rows(value):
    high = value.astype(jnp.bfloat16).astype(jnp.float32)
    return jnp.concatenate([high, value - high], axis=0).astype(jnp.bfloat16)


def spread_kernel(plan, *refs):
    hbm, tables, (out_ref, outer_s, along_z_s) = refs[:5], refs[5:8], refs[8:11]
    tables_out, local, (column_s, turned_s, grid_s, sems) = refs[11:14], refs[14:19], refs[19:]
    copies = [pltpu.make_async_copy(a, b, sems.at[n]) for n, (a, b) in enumerate(zip(hbm, local))]
    for n, (table, target, axis) in enumerate(zip(tables, tables_out, ("gx", "gy", "gz"))):
        copies.append(pltpu.make_async_copy(table.at[lax.axis_index(axis)], target, sems.at[5 + n]))
    for copy in copies:
        copy.start()
    x_ref, y_ref, z_ref, charge_ref, counts_ref = local
    slots = charge_ref.shape[1]
    nbx, nby, nbz = plan.nbins
    zp = plan.zp
    node = (2.0 - lax.broadcasted_iota(jnp.int32, (8, slots), 0).astype(jnp.float32)) * SCALE
    slot = lax.broadcasted_iota(jnp.int32, (8, slots), 1)
    rank = lax.broadcasted_iota(jnp.int32, (8, LANES), 0)
    for copy in copies[:5]:
        copy.wait()
    for ref in (x_ref, y_ref, z_ref):
        ref[...] = ref[...] * SCALE

    def one_bin(p, c):
        r = p * nbz + c
        weight_x = bspline(x_ref[pl.ds(r, 1), :] + node)
        weight_y = bspline(y_ref[pl.ds(r, 1), :] + node)
        weight_z = bspline(z_ref[pl.ds(r, 1), :] + node)
        weight_z = jnp.where(slot < counts_ref[p // nby, p % nby, c], weight_z, 0.0)
        outer = split_rows(
            jnp.concatenate([weight_y[j : j + 1, :] * weight_x for j in range(8)], axis=0)
        )
        outer_s[r // 2, :, (c % 2) * slots : (c % 2 + 1) * slots] = outer
        along_z_s[r] = weight_z
        return outer, split_rows(weight_z * charge_ref[pl.ds(r, 1), :])

    def one_column(p):
        sums = [jnp.zeros((8, LANES), jnp.float32) for _ in range(zp // 8)]
        for c in range(0, nbz, 2):
            (outer_a, z_a), (outer_b, z_b) = one_bin(p, c), one_bin(p, c + 1)
            none = jnp.zeros_like(z_a)
            both = lax.dot_general(
                jnp.concatenate(
                    [jnp.concatenate([z_a, none], axis=1), jnp.concatenate([none, z_b], axis=1)], axis=0
                ),
                jnp.concatenate([outer_a, outer_b], axis=1),
                (((1,), (1,)), ((), ())),
                preferred_element_type=jnp.float32,
            )
            for n in range(2):
                part = both[16 * n : 16 * n + 8, :] + both[16 * n + 8 : 16 * n + 16, :]
                at, shift = divmod(2 * (c + n), 8)
                if shift:
                    part = pltpu.roll(part, shift, 0)
                    sums[at] = sums[at] + jnp.where(rank >= shift, part, 0.0)
                    sums[at + 1] = sums[at + 1] + jnp.where(rank < shift, part, 0.0)
                else:
                    sums[at] = sums[at] + part
        return [v + pltpu.roll(v, 64, 1) for v in sums]

    left = lax.broadcasted_iota(jnp.int32, (8, LANES), 1) < 64

    for pair in range(plan.columns // 2):
        even = one_column(2 * pair)
        odd = one_column(2 * pair + 1)
        for n, (a, b) in enumerate(zip(even, odd)):
            at = pair * zp + 8 * n
            column_s[at : at + 8, :] = jnp.where(left, a, b)
    xp = plan.xp
    for pair in range(plan.columns // 2):
        turned_s[pair * LANES : (pair + 1) * LANES, :zp] = column_s[pair * zp : (pair + 1) * zp, :].T

    def folded(a, y):
        total = None
        for b in range(nby):
            j = y - 4 * b
            if 0 <= j < 8:
                at = (a * nby + b) * 64 + j * 8
                piece = turned_s[at : at + 8, :]
                total = piece if total is None else total + piece
        return total

    for y in range(plan.width[1]):
        for a in range(0, nbx, 2):
            grid_s[y * xp + 4 * a : y * xp + 4 * a + 8, :] = folded(a, y)
        rest = xp - 4 * nbx
        grid_s[(y + 1) * xp - rest : (y + 1) * xp, :] = jnp.zeros((rest, LANES), jnp.float32)
        for a in range(1, nbx, 2):
            at = slice(y * xp + 4 * a, y * xp + 4 * a + 8)
            grid_s[at, :] = grid_s[at, :] + folded(a, y)
    group = lax.broadcasted_iota(jnp.int32, (xp, LANES), 1) // plan.step
    first = plan.first_here()
    for chunk in range(plan.chunks):
        merged = jnp.zeros((xp, LANES), jnp.float32)
        for b in range(plan.per):
            y = chunk * plan.per + b
            if y < plan.kept:
                piece = grid_s[pl.ds(pl.multiple_of((y + first) * xp, 8), xp), :]
                moved = pltpu.roll(piece, b * plan.step, 1) if b else piece
                merged = jnp.where(group == b, moved, merged)
        out_ref[:, chunk * LANES : (chunk + 1) * LANES] = merged
    for copy in copies[5:]:
        copy.wait()


def solve_kernel(plan, *refs):
    nx, ny, nz = plan.counts
    blocks = refs[: nx * ny]
    tables = refs[nx * ny : nx * ny + 3]
    outs = refs[nx * ny + 3 : nx * ny + 3 + nz]
    mid_s, term_s = refs[nx * ny + 3 + nz :]
    ytab_s = tables[1]
    x_matrix = tables[0][...]
    kept, per, zp = plan.kept, plan.per, plan.zp
    span = plan.chunks * per
    mid_s[plan.mid : plan.mid + 8, :] = jnp.zeros((8, LANES), jnp.float32)
    for oy in range(ny):
        gathered = jnp.concatenate([blocks[ox * ny + oy][...] for ox in range(nx)], axis=0)
        both = lax.dot_general(
            split_rows(gathered), x_matrix, (((0,), (0,)), ((), ())), preferred_element_type=jnp.float32
        )
        mid_s[oy * plan.lanes : (oy + 1) * plan.lanes, :] = both[:, :LANES] + both[:, LANES:]
    group = lax.broadcasted_iota(jnp.int32, (zp, LANES), 1) // plan.step
    for chunk in range(plan.chunks):
        sums = [jnp.zeros((zp, LANES), jnp.float32) for _ in range(per)]
        for oy in range(ny):
            for y in range(kept):
                at = oy * plan.lanes + plan.row(y)
                value = mid_s[at : at + zp, :]
                for b in range(per):
                    row = (oy * kept + y) * span + chunk * per + b
                    sums[b] = sums[b] + value * ytab_s[row : row + 1, :]
        for t in range(TERMS):
            merged = jnp.zeros((zp, LANES), jnp.float32)
            for b in range(per):
                shift = (plan.step * b - SLOT * t) % LANES
                moved = pltpu.roll(sums[b], shift, 1) if shift else sums[b]
                merged = jnp.where(group == b, moved, merged)
            term_s[t * zp : (t + 1) * zp, chunk * LANES : (chunk + 1) * LANES] = merged
    both = jnp.dot(tables[2][...], split_rows(term_s[...]), preferred_element_type=jnp.float32)
    result = both[: nz * zp, :] + both[nz * zp :, :]
    for o in range(nz):
        outs[o][...] = result[o * zp : (o + 1) * zp, :]


def gather_kernel(plan, *refs):
    nz = plan.counts[2]
    parts = refs[:nz]
    outer_s, along_z_s, fine_hbm, atom_hbm = refs[nz : nz + 4]
    field_s, column_s, turned_s, inner_s, order_s, fine_ref, atom_ref, sems = refs[nz + 4 :]
    nbx, nby, nbz = plan.nbins
    zp = plan.zp
    lx, ly, lz = plan.local
    total = parts[0][...]
    for part in parts[1:]:
        total = total + part[...]
    for chunk in range(plan.chunks):
        field_s[chunk * LANES : (chunk + 1) * LANES, :zp] = total[:, chunk * LANES : (chunk + 1) * LANES].T
    nothing = plan.lanes
    field_s[nothing:, :] = jnp.zeros((field_s.shape[0] - nothing, LANES), jnp.float32)
    first = plan.first_here()

    def row_of(y):
        if plan.counts[1] > 2:
            return plan.row(y)
        at_start = plan.row(y - RIM // 2) if y >= RIM // 2 else nothing
        at_end = plan.row(y) if y < plan.kept else nothing
        return jnp.where(first == 0, at_end, at_start)

    rows_of = [row_of(y) for y in range(plan.width[1])]
    left = lax.broadcasted_iota(jnp.int32, (zp, LANES), 1) < 64
    for pair in range(plan.columns // 2):
        for half in range(2):
            a, b = divmod(2 * pair + half, nby)
            for j in range(8):
                to = pair * LANES + half * 64 + j * 8
                turned_s[to : to + 8, :] = field_s[pl.ds(rows_of[4 * b + j] + 4 * a, 8), :]
        both = turned_s[pair * LANES : (pair + 1) * LANES, :zp].T
        turned = pltpu.roll(both, 64, 1)
        column_s[2 * pair * zp : (2 * pair + 1) * zp, :] = jnp.where(left, both, turned)
        column_s[(2 * pair + 1) * zp : (2 * pair + 2) * zp, :] = jnp.where(left, turned, both)
    for chunk in range(plan.chunks):
        inner_s[chunk * LANES : (chunk + 1) * LANES, :lz] = total[
            2 : 2 + lz, chunk * LANES : (chunk + 1) * LANES
        ].T
    for y in range(ly):
        order_s[pl.ds(y, lx, stride=ly), :] = inner_s[pl.ds(rows_of[y + 2] + 2, lx), :]
    for x in range(lx):
        fine_ref[x] = order_s[x * ly : (x + 1) * ly, :lz]
    copies = [pltpu.make_async_copy(fine_ref, fine_hbm, sems.at[0])]
    copies[0].start()
    slots = atom_ref.shape[1]

    def one_column(p):
        rows = []
        for c in range(0, nbz, 2):
            patches = [
                split_rows(column_s[p * zp + 2 * n : p * zp + 2 * n + 8, :]) for n in (c, c + 1)
            ]
            both = jnp.dot(
                jnp.concatenate(patches, axis=0), outer_s[(p * nbz + c) // 2],
                preferred_element_type=jnp.float32,
            )
            for n in range(2):
                field = both[16 * n : 16 * n + 8, n * slots : (n + 1) * slots]
                field = field + both[16 * n + 8 : 16 * n + 16, n * slots : (n + 1) * slots]
                rows.append(jnp.sum(field * along_z_s[p * nbz + c + n], axis=0, keepdims=True))
        atom_ref[p * nbz : (p + 1) * nbz, :] = jnp.concatenate(rows, axis=0)

    for part in range(PARTS):
        span = LANES // PARTS
        for p in range(part * span // nbz, (part + 1) * span // nbz):
            one_column(p)
        rows = pl.ds(part * span, span)
        copies.append(pltpu.make_async_copy(atom_ref.at[rows], atom_hbm.at[rows], sems.at[1 + part]))
        copies[-1].start()
    for copy in copies:
        copy.wait()


def body(charges, offset_x, offset_y, offset_z, counts):
    nbins = charges.shape[:3]
    slots = charges.shape[3]
    sizes = tuple(lax.axis_size(a) for a in ("gx", "gy", "gz"))
    nx, ny, nz = sizes
    plan = Plan(nbins, sizes)
    flat = [v.reshape(LANES, slots) for v in (charges, offset_x, offset_y, offset_z)]
    vmem = pl.BlockSpec(memory_space=pltpu.VMEM)
    hbm = pl.BlockSpec(memory_space=pltpu.HBM)
    f32 = jnp.float32
    params = pltpu.CompilerParams(vmem_limit_bytes=12 << 20)

    def far(value):
        return pltpu.with_memory_space_constraint(value, pltpu.HBM)

    tables = (plan.x_table(), plan.y_table(), plan.z_table())
    spread, *weights = pl.pallas_call(
        functools.partial(spread_kernel, plan),
        out_shape=[
            pltpu.VMEM((plan.xp, plan.lanes), f32),
            pltpu.VMEM((LANES // 2, LANES, 2 * slots), jnp.bfloat16),
            pltpu.VMEM((LANES, 8, slots), f32),
        ]
        + [pltpu.VMEM(t.shape[1:], t.dtype) for t in tables],
        in_specs=[hbm] * 8,
        out_specs=[vmem] * 6,
        scratch_shapes=[pltpu.VMEM((LANES, slots), f32)] * 4
        + [
            pltpu.SMEM(nbins, jnp.int32),
            pltpu.VMEM((plan.columns // 2 * plan.zp, LANES), f32),
            pltpu.VMEM((plan.columns * 64, LANES), f32),
            pltpu.VMEM((plan.width[1] * plan.xp, LANES), f32),
            pltpu.SemaphoreType.DMA((8,)),
        ],
        compiler_params=params,
        name="spread",
    )(*(far(v) for v in (*flat[1:], flat[0], counts, *tables)))
    weights, tables = weights[:2], weights[2:]

    def near(value):
        return pltpu.with_memory_space_constraint(value, pltpu.VMEM)

    def moved(value, axis, pairs):
        return near(lax.ppermute(value, axis, pairs))

    def from_chip(shift, oy):
        if shift == 0 and oy == 0:
            return spread
        pairs = [
            (sx * ny + sy, (sx // pair + shift) % (nx // pair) * pair * ny + sx % pair * ny + (sy + oy) % ny)
            for sx in range(nx)
            for sy in range(ny)
        ]
        return moved(spread, ("gx", "gy"), pairs)

    pair = plan.pair
    blocks = []
    for shift in range(nx // pair):
        own = [from_chip(shift, oy) for oy in range(ny)]
        blocks += own
        if pair == 2:
            blocks += [moved(v, "gx", [(s, s ^ 1) for s in range(nx)]) for v in own]
    outs = pl.pallas_call(
        functools.partial(solve_kernel, plan),
        out_shape=[pltpu.VMEM((plan.zp, plan.lanes), f32)] * nz,
        in_specs=[vmem] * (nx * ny + 3),
        out_specs=[vmem] * nz,
        scratch_shapes=[
            pltpu.VMEM((plan.mid + 8, LANES), f32),
            pltpu.VMEM((TERMS * plan.zp, plan.lanes), f32),
        ],
        compiler_params=params,
        name="solve",
    )(*blocks, *tables)
    parts = [outs[0]] + [
        moved(outs[o], "gz", [(s, partner(s, o, nz)) for s in range(nz)]) for o in range(1, nz)
    ]
    fine, atom = pl.pallas_call(
        functools.partial(gather_kernel, plan),
        out_shape=[
            jax.ShapeDtypeStruct(plan.local, f32),
            jax.ShapeDtypeStruct((LANES, slots), f32),
        ],
        in_specs=[vmem] * (nz + 2),
        out_specs=[hbm, hbm],
        scratch_shapes=[
            pltpu.VMEM((plan.lanes + plan.xp, LANES), f32),
            pltpu.VMEM((plan.columns * plan.zp, LANES), f32),
            pltpu.VMEM((plan.columns * 64, LANES), f32),
            pltpu.VMEM((plan.lanes, LANES), f32),
            pltpu.VMEM((plan.local[0] * plan.local[1], LANES), f32),
            pltpu.VMEM(plan.local, f32),
            pltpu.VMEM((LANES, slots), f32),
            pltpu.SemaphoreType.DMA((1 + PARTS,)),
        ],
        compiler_params=params,
        name="gather",
    )(*parts, *weights)
    return fine, atom.reshape(charges.shape)


def solution(mesh):
    in_specs = (
        P("gx", "gy", "gz", None),
        P("gx", "gy", "gz", None),
        P("gx", "gy", "gz", None),
        P("gx", "gy", "gz", None),
        P("gx", "gy", "gz"),
    )
    out_specs = (P("gx", "gy", "gz"), P("gx", "gy", "gz", None))
    return jax.shard_map(body, mesh=mesh, in_specs=in_specs, out_specs=out_specs, check_vma=False)
```

```python
import functools
import math

import jax
import jax.numpy as jnp
import numpy as np
from jax import lax
from jax.experimental import pallas as pl
from jax.experimental.pallas import tpu as pltpu
from jax.sharding import PartitionSpec as P

R = 8
LANES = 128
TERMS = 5
SLOT = LANES // TERMS
PARTS = 4
RIM = 4
TAPS = (-0.0625, 0.0, 0.5625, 1.0, 0.5625, 0.0, -0.0625)
highest = lax.Precision.HIGHEST


def profile(family, offset):
    if family == 0:
        return math.exp(-((offset / (0.4 * R)) ** 2))
    if family == 1:
        return math.exp(-((offset / (0.8 * R)) ** 2))
    return 1.0 / (1.0 + (offset / R) ** 2)


def norm_factor(family):
    return sum(profile(family, float(o)) ** 2 for o in range(-R, R + 1)) ** 1.5


def stencil(points, family):
    matrix = np.zeros((points, points))
    for i in range(points):
        for k in range(max(0, i - R), min(points, i + R + 1)):
            matrix[i, k] = profile(family, float(k - i))
    return matrix


def restriction(points):
    matrix = np.zeros((points // 2, points))
    for i in range(points // 2):
        for k, tap in enumerate(TAPS):
            if 0 <= 2 * i + k - 3 < points:
                matrix[i, 2 * i + k - 3] += tap
    return matrix


def term_matrices(points):
    q_one = restriction(points)
    q_two = restriction(points // 2)
    coarse = points // 4
    far = np.array([[profile(2, float(k - i)) for k in range(coarse)] for i in range(coarse)])
    down = q_two @ q_one
    return [
        stencil(points, 0),
        stencil(points, 1),
        q_one.T @ stencil(points // 2, 0) @ q_one,
        q_one.T @ stencil(points // 2, 1) @ q_one,
        down.T @ far @ down,
    ]


def term_scales():
    n = [norm_factor(f) for f in range(3)]
    return [1.0 / n[0], 1.0 / n[1], 0.5 / n[0], 0.5 / n[1], 0.5 / n[2]]


def windowed(points, count):
    local = points // count
    width = local + RIM
    index = np.arange(count)[:, None] * local + np.arange(width)[None, :] - RIM // 2
    inside = (index >= 0) & (index < points)
    clipped = np.clip(index, 0, points - 1)
    both = inside[:, :, None, None] & inside[None, None]
    return np.stack(
        [np.where(both, m[clipped[:, :, None, None], clipped[None, None]], 0.0) for m in term_matrices(points)]
    )


def round_up(value, step):
    return -(-value // step) * step


def halves(table):
    high = table.astype(jnp.bfloat16)
    return high, (table - high.astype(np.float32)).astype(jnp.bfloat16)


def partner(device, order, count):
    return (device + order) % count


class Plan:
    def __init__(self, nbins, counts):
        self.nbins = nbins
        self.counts = counts
        self.local = (4 * nbins[0], 4 * nbins[1], 2 * nbins[2])
        self.width = tuple(v + RIM for v in self.local)
        self.points = tuple(v * c for v, c in zip(self.local, counts))
        self.xp = round_up(self.width[0], 8)
        self.zp = round_up(self.width[2], 8)
        self.kept = self.width[1] - RIM // 2 if counts[1] <= 2 else self.width[1]
        self.per = LANES // max(self.width[0], self.width[2])
        self.step = LANES // self.per
        self.chunks = -(-self.kept // self.per)
        self.lanes = self.chunks * LANES
        self.columns = nbins[0] * nbins[1]
        self.mid = self.counts[1] * self.lanes
        self.pair = 2 if counts[0] % 2 == 0 else 1
        assert self.columns * nbins[2] == LANES and nbins[2] == 8 and self.columns % 2 == 0
        assert self.width[0] <= SLOT and max(self.width[0], self.width[2]) <= self.step

    def first(self, device):
        return RIM // 2 if self.counts[1] <= 2 and device == 0 else 0

    def first_here(self):
        if self.counts[1] > 2:
            return 0
        return jnp.where(lax.axis_index("gy") == 0, RIM // 2, 0)

    def row(self, y):
        return y // self.per * LANES + y % self.per * self.step

    def x_table(self):
        nx, width = self.counts[0], self.width[0]
        m = windowed(self.points[0], nx)
        table = np.zeros((nx, nx * self.xp, LANES), np.float32)
        for d in range(nx):
            for o in range(nx):
                source = self.x_source(d, o)
                for t in range(TERMS):
                    table[d, o * self.xp : o * self.xp + width, t * SLOT : t * SLOT + width] = (
                        m[t, d, :, source, :].T
                    )
        high, low = halves(table)
        upper = np.concatenate([high, low], axis=2)
        lower = np.concatenate([high, np.zeros_like(low)], axis=2)
        return jnp.asarray(np.concatenate([upper, lower], axis=1))

    def x_source(self, device, order):
        pair = self.pair
        shift, other = divmod(order, pair)
        return (device // pair - shift) % (self.counts[0] // pair) * pair + (device % pair ^ other)

    def y_table(self):
        ny, kept = self.counts[1], self.kept
        m = windowed(self.points[1], ny)
        table = np.zeros((ny, ny * kept, self.chunks * self.per, LANES), np.float32)
        for d in range(ny):
            for o in range(ny):
                source = (d - o) % ny
                target_at, source_at = self.first(d), self.first(source)
                for t in range(TERMS):
                    block = m[t, d, target_at : target_at + kept, source, source_at : source_at + kept]
                    table[d, o * kept : (o + 1) * kept, :kept, t * SLOT : (t + 1) * SLOT] = block.T[:, :, None]
        return jnp.asarray(table.reshape(ny, ny * kept * self.chunks * self.per, LANES))

    def z_table(self):
        nz, width = self.counts[2], self.width[2]
        m = windowed(self.points[2], nz)
        scales = term_scales()
        table = np.zeros((nz, nz * self.zp, TERMS * self.zp), np.float32)
        for d in range(nz):
            for o in range(nz):
                for t in range(TERMS):
                    table[d, o * self.zp : o * self.zp + width, t * self.zp : t * self.zp + width] = (
                        scales[t] * m[t, partner(d, o, nz), :, d, :]
                    )
        high, low = halves(table)
        upper = np.concatenate([high, high], axis=2)
        lower = np.concatenate([low, np.zeros_like(low)], axis=2)
        return jnp.asarray(np.concatenate([upper, lower], axis=1))


SCALE = (1.0 / 6.0) ** (1.0 / 3.0)


def bspline(scaled):
    a = jnp.abs(scaled)
    u = jnp.maximum(2.0 * SCALE - a, 0.0)
    v = jnp.maximum(SCALE - a, 0.0)
    return u * u * u - v * v * (4.0 * v)


def split_rows(value):
    high = value.astype(jnp.bfloat16).astype(jnp.float32)
    return jnp.concatenate([high, value - high], axis=0).astype(jnp.bfloat16)


def spread_kernel(plan, *refs):
    hbm, tables, (out_ref, outer_s, along_z_s) = refs[:5], refs[5:8], refs[8:11]
    tables_out, local, (column_s, turned_s, grid_s, sems) = refs[11:14], refs[14:19], refs[19:]
    copies = [pltpu.make_async_copy(a, b, sems.at[n]) for n, (a, b) in enumerate(zip(hbm, local))]
    for n, (table, target, axis) in enumerate(zip(tables, tables_out, ("gx", "gy", "gz"))):
        copies.append(pltpu.make_async_copy(table.at[lax.axis_index(axis)], target, sems.at[5 + n]))
    for copy in copies:
        copy.start()
    x_ref, y_ref, z_ref, charge_ref, counts_ref = local
    slots = charge_ref.shape[1]
    nbx, nby, nbz = plan.nbins
    zp = plan.zp
    node = (2.0 - lax.broadcasted_iota(jnp.int32, (8, slots), 0).astype(jnp.float32)) * SCALE
    slot = lax.broadcasted_iota(jnp.int32, (8, slots), 1)
    rank = lax.broadcasted_iota(jnp.int32, (8, LANES), 0)
    for copy in copies[:5]:
        copy.wait()
    for ref in (x_ref, y_ref, z_ref):
        ref[...] = ref[...] * SCALE

    def one_bin(p, c):
        r = p * nbz + c
        weight_x = bspline(x_ref[pl.ds(r, 1), :] + node)
        weight_y = bspline(y_ref[pl.ds(r, 1), :] + node)
        weight_z = bspline(z_ref[pl.ds(r, 1), :] + node)
        weight_z = jnp.where(slot < counts_ref[p // nby, p % nby, c], weight_z, 0.0)
        outer = jnp.concatenate([weight_y[j : j + 1, :] * weight_x for j in range(8)], axis=0)
        outer_s[r // 2, :, (c % 2) * slots : (c % 2 + 1) * slots] = outer
        along_z_s[r] = weight_z
        return split_rows(outer), split_rows(weight_z * charge_ref[pl.ds(r, 1), :])

    def one_column(p):
        sums = [jnp.zeros((8, LANES), jnp.float32) for _ in range(zp // 8)]
        for c in range(0, nbz, 2):
            (outer_a, z_a), (outer_b, z_b) = one_bin(p, c), one_bin(p, c + 1)
            none = jnp.zeros_like(z_a)
            both = lax.dot_general(
                jnp.concatenate(
                    [jnp.concatenate([z_a, none], axis=1), jnp.concatenate([none, z_b], axis=1)], axis=0
                ),
                jnp.concatenate([outer_a, outer_b], axis=1),
                (((1,), (1,)), ((), ())),
                preferred_element_type=jnp.float32,
            )
            for n in range(2):
                part = both[16 * n : 16 * n + 8, :] + both[16 * n + 8 : 16 * n + 16, :]
                at, shift = divmod(2 * (c + n), 8)
                if shift:
                    part = pltpu.roll(part, shift, 0)
                    sums[at] = sums[at] + jnp.where(rank >= shift, part, 0.0)
                    sums[at + 1] = sums[at + 1] + jnp.where(rank < shift, part, 0.0)
                else:
                    sums[at] = sums[at] + part
        return [v + pltpu.roll(v, 64, 1) for v in sums]

    left = lax.broadcasted_iota(jnp.int32, (8, LANES), 1) < 64

    for pair in range(plan.columns // 2):
        even = one_column(2 * pair)
        odd = one_column(2 * pair + 1)
        for n, (a, b) in enumerate(zip(even, odd)):
            at = pair * zp + 8 * n
            column_s[at : at + 8, :] = jnp.where(left, a, b)
    xp = plan.xp
    for pair in range(plan.columns // 2):
        turned_s[pair * LANES : (pair + 1) * LANES, :zp] = column_s[pair * zp : (pair + 1) * zp, :].T

    def folded(a, y):
        total = None
        for b in range(nby):
            j = y - 4 * b
            if 0 <= j < 8:
                at = (a * nby + b) * 64 + j * 8
                piece = turned_s[at : at + 8, :]
                total = piece if total is None else total + piece
        return total

    for y in range(plan.width[1]):
        for a in range(0, nbx, 2):
            grid_s[y * xp + 4 * a : y * xp + 4 * a + 8, :] = folded(a, y)
        rest = xp - 4 * nbx
        grid_s[(y + 1) * xp - rest : (y + 1) * xp, :] = jnp.zeros((rest, LANES), jnp.float32)
        for a in range(1, nbx, 2):
            at = slice(y * xp + 4 * a, y * xp + 4 * a + 8)
            grid_s[at, :] = grid_s[at, :] + folded(a, y)
    group = lax.broadcasted_iota(jnp.int32, (xp, LANES), 1) // plan.step
    first = plan.first_here()
    for chunk in range(plan.chunks):
        merged = jnp.zeros((xp, LANES), jnp.float32)
        for b in range(plan.per):
            y = chunk * plan.per + b
            if y < plan.kept:
                piece = grid_s[pl.ds(pl.multiple_of((y + first) * xp, 8), xp), :]
                moved = pltpu.roll(piece, b * plan.step, 1) if b else piece
                merged = jnp.where(group == b, moved, merged)
        out_ref[:, chunk * LANES : (chunk + 1) * LANES] = merged
    for copy in copies[5:]:
        copy.wait()


def solve_kernel(plan, *refs):
    nx, ny, nz = plan.counts
    blocks = refs[: nx * ny]
    tables = refs[nx * ny : nx * ny + 3]
    outs = refs[nx * ny + 3 : nx * ny + 3 + nz]
    mid_s, term_s = refs[nx * ny + 3 + nz :]
    ytab_s = tables[1]
    x_matrix = tables[0][...]
    kept, per, zp = plan.kept, plan.per, plan.zp
    span = plan.chunks * per
    mid_s[plan.mid : plan.mid + 8, :] = jnp.zeros((8, LANES), jnp.float32)
    for oy in range(ny):
        gathered = jnp.concatenate([blocks[ox * ny + oy][...] for ox in range(nx)], axis=0)
        both = lax.dot_general(
            split_rows(gathered), x_matrix, (((0,), (0,)), ((), ())), preferred_element_type=jnp.float32
        )
        mid_s[oy * plan.lanes : (oy + 1) * plan.lanes, :] = both[:, :LANES] + both[:, LANES:]
    group = lax.broadcasted_iota(jnp.int32, (zp, LANES), 1) // plan.step
    for chunk in range(plan.chunks):
        sums = [jnp.zeros((zp, LANES), jnp.float32) for _ in range(per)]
        for oy in range(ny):
            for y in range(kept):
                at = oy * plan.lanes + plan.row(y)
                value = mid_s[at : at + zp, :]
                for b in range(per):
                    row = (oy * kept + y) * span + chunk * per + b
                    sums[b] = sums[b] + value * ytab_s[row : row + 1, :]
        for t in range(TERMS):
            merged = jnp.zeros((zp, LANES), jnp.float32)
            for b in range(per):
                shift = (plan.step * b - SLOT * t) % LANES
                moved = pltpu.roll(sums[b], shift, 1) if shift else sums[b]
                merged = jnp.where(group == b, moved, merged)
            term_s[t * zp : (t + 1) * zp, chunk * LANES : (chunk + 1) * LANES] = merged
    both = jnp.dot(tables[2][...], split_rows(term_s[...]), preferred_element_type=jnp.float32)
    result = both[: nz * zp, :] + both[nz * zp :, :]
    for o in range(nz):
        outs[o][...] = result[o * zp : (o + 1) * zp, :]


def gather_kernel(plan, *refs):
    nz = plan.counts[2]
    parts = refs[:nz]
    outer_s, along_z_s, fine_hbm, atom_hbm = refs[nz : nz + 4]
    field_s, column_s, turned_s, inner_s, order_s, fine_ref, atom_ref, sems = refs[nz + 4 :]
    nbx, nby, nbz = plan.nbins
    zp = plan.zp
    lx, ly, lz = plan.local
    total = parts[0][...]
    for part in parts[1:]:
        total = total + part[...]
    for chunk in range(plan.chunks):
        field_s[chunk * LANES : (chunk + 1) * LANES, :zp] = total[:, chunk * LANES : (chunk + 1) * LANES].T
    nothing = plan.lanes
    field_s[nothing:, :] = jnp.zeros((field_s.shape[0] - nothing, LANES), jnp.float32)
    first = plan.first_here()

    def row_of(y):
        if plan.counts[1] > 2:
            return plan.row(y)
        at_start = plan.row(y - RIM // 2) if y >= RIM // 2 else nothing
        at_end = plan.row(y) if y < plan.kept else nothing
        return jnp.where(first == 0, at_end, at_start)

    rows_of = [row_of(y) for y in range(plan.width[1])]
    left = lax.broadcasted_iota(jnp.int32, (zp, LANES), 1) < 64
    for pair in range(plan.columns // 2):
        for half in range(2):
            a, b = divmod(2 * pair + half, nby)
            for j in range(8):
                to = pair * LANES + half * 64 + j * 8
                turned_s[to : to + 8, :] = field_s[pl.ds(rows_of[4 * b + j] + 4 * a, 8), :]
        both = turned_s[pair * LANES : (pair + 1) * LANES, :zp].T
        turned = pltpu.roll(both, 64, 1)
        column_s[2 * pair * zp : (2 * pair + 1) * zp, :] = jnp.where(left, both, turned)
        column_s[(2 * pair + 1) * zp : (2 * pair + 2) * zp, :] = jnp.where(left, turned, both)
    for chunk in range(plan.chunks):
        inner_s[chunk * LANES : (chunk + 1) * LANES, :lz] = total[
            2 : 2 + lz, chunk * LANES : (chunk + 1) * LANES
        ].T
    for y in range(ly):
        order_s[pl.ds(y, lx, stride=ly), :] = inner_s[pl.ds(rows_of[y + 2] + 2, lx), :]
    for x in range(lx):
        fine_ref[x] = order_s[x * ly : (x + 1) * ly, :lz]
    copies = [pltpu.make_async_copy(fine_ref, fine_hbm, sems.at[0])]
    copies[0].start()
    slots = atom_ref.shape[1]

    def one_column(p):
        rows = []
        for c in range(0, nbz, 2):
            patches = [
                split_rows(column_s[p * zp + 2 * n : p * zp + 2 * n + 8, :]) for n in (c, c + 1)
            ]
            both = jnp.dot(
                jnp.concatenate(patches, axis=0), split_rows(outer_s[(p * nbz + c) // 2]),
                preferred_element_type=jnp.float32,
            )
            for n in range(2):
                field = both[16 * n : 16 * n + 8, n * slots : (n + 1) * slots]
                field = field + both[16 * n + 8 : 16 * n + 16, n * slots : (n + 1) * slots]
                rows.append(jnp.sum(field * along_z_s[p * nbz + c + n], axis=0, keepdims=True))
        atom_ref[p * nbz : (p + 1) * nbz, :] = jnp.concatenate(rows, axis=0)

    for part in range(PARTS):
        span = LANES // PARTS
        for p in range(part * span // nbz, (part + 1) * span // nbz):
            one_column(p)
        rows = pl.ds(part * span, span)
        copies.append(pltpu.make_async_copy(atom_ref.at[rows], atom_hbm.at[rows], sems.at[1 + part]))
        copies[-1].start()
    for copy in copies:
        copy.wait()


def body(charges, offset_x, offset_y, offset_z, counts):
    nbins = charges.shape[:3]
    slots = charges.shape[3]
    sizes = tuple(lax.axis_size(a) for a in ("gx", "gy", "gz"))
    nx, ny, nz = sizes
    plan = Plan(nbins, sizes)
    flat = [v.reshape(LANES, slots) for v in (charges, offset_x, offset_y, offset_z)]
    vmem = pl.BlockSpec(memory_space=pltpu.VMEM)
    hbm = pl.BlockSpec(memory_space=pltpu.HBM)
    f32 = jnp.float32
    params = pltpu.CompilerParams(vmem_limit_bytes=12 << 20)

    def far(value):
        return pltpu.with_memory_space_constraint(value, pltpu.HBM)

    tables = (plan.x_table(), plan.y_table(), plan.z_table())
    spread, *weights = pl.pallas_call(
        functools.partial(spread_kernel, plan),
        out_shape=[
            pltpu.VMEM((plan.xp, plan.lanes), f32),
            pltpu.VMEM((LANES // 2, 64, 2 * slots), f32),
            pltpu.VMEM((LANES, 8, slots), f32),
        ]
        + [pltpu.VMEM(t.shape[1:], t.dtype) for t in tables],
        in_specs=[hbm] * 8,
        out_specs=[vmem] * 6,
        scratch_shapes=[pltpu.VMEM((LANES, slots), f32)] * 4
        + [
            pltpu.SMEM(nbins, jnp.int32),
            pltpu.VMEM((plan.columns // 2 * plan.zp, LANES), f32),
            pltpu.VMEM((plan.columns * 64, LANES), f32),
            pltpu.VMEM((plan.width[1] * plan.xp, LANES), f32),
            pltpu.SemaphoreType.DMA((8,)),
        ],
        compiler_params=params,
        name="spread",
    )(*(far(v) for v in (*flat[1:], flat[0], counts, *tables)))
    weights, tables = weights[:2], weights[2:]

    def near(value):
        return pltpu.with_memory_space_constraint(value, pltpu.VMEM)

    def moved(value, axis, pairs):
        return near(lax.ppermute(value, axis, pairs))

    def from_chip(shift, oy):
        if shift == 0 and oy == 0:
            return spread
        pairs = [
            (sx * ny + sy, (sx // pair + shift) % (nx // pair) * pair * ny + sx % pair * ny + (sy + oy) % ny)
            for sx in range(nx)
            for sy in range(ny)
        ]
        return moved(spread, ("gx", "gy"), pairs)

    pair = plan.pair
    blocks = []
    for shift in range(nx // pair):
        own = [from_chip(shift, oy) for oy in range(ny)]
        blocks += own
        if pair == 2:
            blocks += [moved(v, "gx", [(s, s ^ 1) for s in range(nx)]) for v in own]
    outs = pl.pallas_call(
        functools.partial(solve_kernel, plan),
        out_shape=[pltpu.VMEM((plan.zp, plan.lanes), f32)] * nz,
        in_specs=[vmem] * (nx * ny + 3),
        out_specs=[vmem] * nz,
        scratch_shapes=[
            pltpu.VMEM((plan.mid + 8, LANES), f32),
            pltpu.VMEM((TERMS * plan.zp, plan.lanes), f32),
        ],
        compiler_params=params,
        name="solve",
    )(*blocks, *tables)
    parts = [outs[0]] + [
        moved(outs[o], "gz", [(s, partner(s, o, nz)) for s in range(nz)]) for o in range(1, nz)
    ]
    fine, atom = pl.pallas_call(
        functools.partial(gather_kernel, plan),
        out_shape=[
            jax.ShapeDtypeStruct(plan.local, f32),
            jax.ShapeDtypeStruct((LANES, slots), f32),
        ],
        in_specs=[vmem] * (nz + 2),
        out_specs=[hbm, hbm],
        scratch_shapes=[
            pltpu.VMEM((plan.lanes + plan.xp, LANES), f32),
            pltpu.VMEM((plan.columns * plan.zp, LANES), f32),
            pltpu.VMEM((plan.columns * 64, LANES), f32),
            pltpu.VMEM((plan.lanes, LANES), f32),
            pltpu.VMEM((plan.local[0] * plan.local[1], LANES), f32),
            pltpu.VMEM(plan.local, f32),
            pltpu.VMEM((LANES, slots), f32),
            pltpu.SemaphoreType.DMA((1 + PARTS,)),
        ],
        compiler_params=params,
        name="gather",
    )(*parts, *weights)
    return fine, atom.reshape(charges.shape)


def solution(mesh):
    in_specs = (
        P("gx", "gy", "gz", None),
        P("gx", "gy", "gz", None),
        P("gx", "gy", "gz", None),
        P("gx", "gy", "gz", None),
        P("gx", "gy", "gz"),
    )
    out_specs = (P("gx", "gy", "gz"), P("gx", "gy", "gz", None))
    return jax.shard_map(body, mesh=mesh, in_specs=in_specs, out_specs=out_specs, check_vma=False)
```

```python
import functools
import math

import jax
import jax.numpy as jnp
import numpy as np
from jax import lax
from jax.experimental import pallas as pl
from jax.experimental.pallas import tpu as pltpu
from jax.sharding import PartitionSpec as P

R = 8
LANES = 128
TERMS = 5
SLOT = LANES // TERMS
PARTS = 2
RIM = 4
TAPS = (-0.0625, 0.0, 0.5625, 1.0, 0.5625, 0.0, -0.0625)
highest = lax.Precision.HIGHEST


def profile(family, offset):
    if family == 0:
        return math.exp(-((offset / (0.4 * R)) ** 2))
    if family == 1:
        return math.exp(-((offset / (0.8 * R)) ** 2))
    return 1.0 / (1.0 + (offset / R) ** 2)


def norm_factor(family):
    return sum(profile(family, float(o)) ** 2 for o in range(-R, R + 1)) ** 1.5


def stencil(points, family):
    matrix = np.zeros((points, points))
    for i in range(points):
        for k in range(max(0, i - R), min(points, i + R + 1)):
            matrix[i, k] = profile(family, float(k - i))
    return matrix


def restriction(points):
    matrix = np.zeros((points // 2, points))
    for i in range(points // 2):
        for k, tap in enumerate(TAPS):
            if 0 <= 2 * i + k - 3 < points:
                matrix[i, 2 * i + k - 3] += tap
    return matrix


def term_matrices(points):
    q_one = restriction(points)
    q_two = restriction(points // 2)
    coarse = points // 4
    far = np.array([[profile(2, float(k - i)) for k in range(coarse)] for i in range(coarse)])
    down = q_two @ q_one
    return [
        stencil(points, 0),
        stencil(points, 1),
        q_one.T @ stencil(points // 2, 0) @ q_one,
        q_one.T @ stencil(points // 2, 1) @ q_one,
        down.T @ far @ down,
    ]


def term_scales():
    n = [norm_factor(f) for f in range(3)]
    return [1.0 / n[0], 1.0 / n[1], 0.5 / n[0], 0.5 / n[1], 0.5 / n[2]]


def windowed(points, count):
    local = points // count
    width = local + RIM
    index = np.arange(count)[:, None] * local + np.arange(width)[None, :] - RIM // 2
    inside = (index >= 0) & (index < points)
    clipped = np.clip(index, 0, points - 1)
    both = inside[:, :, None, None] & inside[None, None]
    return np.stack(
        [np.where(both, m[clipped[:, :, None, None], clipped[None, None]], 0.0) for m in term_matrices(points)]
    )


def round_up(value, step):
    return -(-value // step) * step


def halves(table):
    high = table.astype(jnp.bfloat16)
    return high, (table - high.astype(np.float32)).astype(jnp.bfloat16)


def partner(device, order, count):
    return (device + order) % count


class Plan:
    def __init__(self, nbins, counts):
        self.nbins = nbins
        self.counts = counts
        self.local = (4 * nbins[0], 4 * nbins[1], 2 * nbins[2])
        self.width = tuple(v + RIM for v in self.local)
        self.points = tuple(v * c for v, c in zip(self.local, counts))
        self.xp = round_up(self.width[0], 8)
        self.zp = round_up(self.width[2], 8)
        self.kept = self.width[1] - RIM // 2 if counts[1] <= 2 else self.width[1]
        self.per = LANES // max(self.width[0], self.width[2])
        self.step = LANES // self.per
        self.chunks = -(-self.kept // self.per)
        self.lanes = self.chunks * LANES
        self.columns = nbins[0] * nbins[1]
        self.mid = self.counts[1] * self.lanes
        self.pair = 2 if counts[0] % 2 == 0 else 1
        assert self.columns * nbins[2] == LANES and nbins[2] == 8 and self.columns % 2 == 0
        assert self.width[0] <= SLOT and max(self.width[0], self.width[2]) <= self.step

    def first(self, device):
        return RIM // 2 if self.counts[1] <= 2 and device == 0 else 0

    def first_here(self):
        if self.counts[1] > 2:
            return 0
        return jnp.where(lax.axis_index("gy") == 0, RIM // 2, 0)

    def row(self, y):
        return y // self.per * LANES + y % self.per * self.step

    def x_table(self):
        nx, width = self.counts[0], self.width[0]
        m = windowed(self.points[0], nx)
        table = np.zeros((nx, nx * self.xp, LANES), np.float32)
        for d in range(nx):
            for o in range(nx):
                source = self.x_source(d, o)
                for t in range(TERMS):
                    table[d, o * self.xp : o * self.xp + width, t * SLOT : t * SLOT + width] = (
                        m[t, d, :, source, :].T
                    )
        high, low = halves(table)
        upper = np.concatenate([high, low], axis=2)
        lower = np.concatenate([high, np.zeros_like(low)], axis=2)
        return jnp.asarray(np.concatenate([upper, lower], axis=1))

    def x_source(self, device, order):
        pair = self.pair
        shift, other = divmod(order, pair)
        return (device // pair - shift) % (self.counts[0] // pair) * pair + (device % pair ^ other)

    def y_table(self):
        ny, kept = self.counts[1], self.kept
        m = windowed(self.points[1], ny)
        table = np.zeros((ny, ny * kept, self.chunks * self.per, LANES), np.float32)
        for d in range(ny):
            for o in range(ny):
                source = (d - o) % ny
                target_at, source_at = self.first(d), self.first(source)
                for t in range(TERMS):
                    block = m[t, d, target_at : target_at + kept, source, source_at : source_at + kept]
                    table[d, o * kept : (o + 1) * kept, :kept, t * SLOT : (t + 1) * SLOT] = block.T[:, :, None]
        return jnp.asarray(table.reshape(ny, ny * kept * self.chunks * self.per, LANES))

    def z_table(self):
        nz, width = self.counts[2], self.width[2]
        m = windowed(self.points[2], nz)
        scales = term_scales()
        table = np.zeros((nz, nz * self.zp, TERMS * self.zp), np.float32)
        for d in range(nz):
            for o in range(nz):
                for t in range(TERMS):
                    table[d, o * self.zp : o * self.zp + width, t * self.zp : t * self.zp + width] = (
                        scales[t] * m[t, partner(d, o, nz), :, d, :]
                    )
        high, low = halves(table)
        upper = np.concatenate([high, high], axis=2)
        lower = np.concatenate([low, np.zeros_like(low)], axis=2)
        return jnp.asarray(np.concatenate([upper, lower], axis=1))


SCALE = (1.0 / 6.0) ** (1.0 / 3.0)


def bspline(scaled):
    a = jnp.abs(scaled)
    u = jnp.maximum(2.0 * SCALE - a, 0.0)
    v = jnp.maximum(SCALE - a, 0.0)
    return u * u * u - v * v * (4.0 * v)


def split_rows(value):
    high = value.astype(jnp.bfloat16).astype(jnp.float32)
    return jnp.concatenate([high, value - high], axis=0).astype(jnp.bfloat16)


def spread_kernel(plan, *refs):
    hbm, tables, (out_ref, outer_s, along_z_s) = refs[:5], refs[5:8], refs[8:11]
    tables_out, local, (column_s, turned_s, grid_s, along_y_s, sems) = refs[11:14], refs[14:19], refs[19:]
    copies = [pltpu.make_async_copy(a, b, sems.at[n]) for n, (a, b) in enumerate(zip(hbm, local))]
    for n, (table, target, axis) in enumerate(zip(tables, tables_out, ("gx", "gy", "gz"))):
        copies.append(pltpu.make_async_copy(table.at[lax.axis_index(axis)], target, sems.at[5 + n]))
    for copy in copies:
        copy.start()
    x_ref, y_ref, z_ref, charge_ref, counts_ref = local
    slots = charge_ref.shape[1]
    nbx, nby, nbz = plan.nbins
    zp = plan.zp
    node = (2.0 - lax.broadcasted_iota(jnp.int32, (8, slots), 0).astype(jnp.float32)) * SCALE
    slot = lax.broadcasted_iota(jnp.int32, (8, slots), 1)
    rank = lax.broadcasted_iota(jnp.int32, (8, LANES), 0)
    for copy in copies[:5]:
        copy.wait()
    for ref in (x_ref, y_ref, z_ref):
        ref[...] = ref[...] * SCALE

    def one_bin(p, c):
        r = p * nbz + c
        weight_x = bspline(x_ref[pl.ds(r, 1), :] + node)
        weight_y = bspline(y_ref[pl.ds(r, 1), :] + node)
        weight_z = bspline(z_ref[pl.ds(r, 1), :] + node)
        weight_z = jnp.where(slot < counts_ref[p // nby, p % nby, c], weight_z, 0.0)
        along_y_s[r * 8 : (r + 1) * 8, :] = weight_y
        outer = jnp.concatenate(
            [along_y_s[pl.ds(r * 8 + j, 8, stride=0), :] * weight_x for j in range(8)], axis=0
        )
        outer_s[r // 2, :, (c % 2) * slots : (c % 2 + 1) * slots] = outer
        along_z_s[r] = weight_z
        return split_rows(outer), split_rows(weight_z * charge_ref[pl.ds(r, 1), :])

    def one_column(p):
        sums = [jnp.zeros((8, LANES), jnp.float32) for _ in range(zp // 8)]
        for c in range(0, nbz, 2):
            (outer_a, z_a), (outer_b, z_b) = one_bin(p, c), one_bin(p, c + 1)
            none = jnp.zeros_like(z_a)
            both = lax.dot_general(
                jnp.concatenate(
                    [jnp.concatenate([z_a, none], axis=1), jnp.concatenate([none, z_b], axis=1)], axis=0
                ),
                jnp.concatenate([outer_a, outer_b], axis=1),
                (((1,), (1,)), ((), ())),
                preferred_element_type=jnp.float32,
            )
            for n in range(2):
                part = both[16 * n : 16 * n + 8, :] + both[16 * n + 8 : 16 * n + 16, :]
                at, shift = divmod(2 * (c + n), 8)
                if shift:
                    part = pltpu.roll(part, shift, 0)
                    sums[at] = sums[at] + jnp.where(rank >= shift, part, 0.0)
                    sums[at + 1] = sums[at + 1] + jnp.where(rank < shift, part, 0.0)
                else:
                    sums[at] = sums[at] + part
        return [v + pltpu.roll(v, 64, 1) for v in sums]

    left = lax.broadcasted_iota(jnp.int32, (8, LANES), 1) < 64

    for pair in range(plan.columns // 2):
        even = one_column(2 * pair)
        odd = one_column(2 * pair + 1)
        for n, (a, b) in enumerate(zip(even, odd)):
            at = pair * zp + 8 * n
            column_s[at : at + 8, :] = jnp.where(left, a, b)
    xp = plan.xp
    for pair in range(plan.columns // 2):
        turned_s[pair * LANES : (pair + 1) * LANES, :zp] = column_s[pair * zp : (pair + 1) * zp, :].T

    def folded(a, y):
        total = None
        for b in range(nby):
            j = y - 4 * b
            if 0 <= j < 8:
                at = (a * nby + b) * 64 + j * 8
                piece = turned_s[at : at + 8, :]
                total = piece if total is None else total + piece
        return total

    for y in range(plan.width[1]):
        for a in range(0, nbx, 2):
            grid_s[y * xp + 4 * a : y * xp + 4 * a + 8, :] = folded(a, y)
        rest = xp - 4 * nbx
        grid_s[(y + 1) * xp - rest : (y + 1) * xp, :] = jnp.zeros((rest, LANES), jnp.float32)
        for a in range(1, nbx, 2):
            at = slice(y * xp + 4 * a, y * xp + 4 * a + 8)
            grid_s[at, :] = grid_s[at, :] + folded(a, y)
    group = lax.broadcasted_iota(jnp.int32, (xp, LANES), 1) // plan.step
    first = plan.first_here()
    for chunk in range(plan.chunks):
        merged = jnp.zeros((xp, LANES), jnp.float32)
        for b in range(plan.per):
            y = chunk * plan.per + b
            if y < plan.kept:
                piece = grid_s[pl.ds(pl.multiple_of((y + first) * xp, 8), xp), :]
                moved = pltpu.roll(piece, b * plan.step, 1) if b else piece
                merged = jnp.where(group == b, moved, merged)
        out_ref[:, chunk * LANES : (chunk + 1) * LANES] = merged
    for copy in copies[5:]:
        copy.wait()


def solve_kernel(plan, *refs):
    nx, ny, nz = plan.counts
    blocks = refs[: nx * ny]
    tables = refs[nx * ny : nx * ny + 3]
    outs = refs[nx * ny + 3 : nx * ny + 3 + nz]
    mid_s, term_s = refs[nx * ny + 3 + nz :]
    ytab_s = tables[1]
    x_matrix = tables[0][...]
    kept, per, zp = plan.kept, plan.per, plan.zp
    span = plan.chunks * per
    mid_s[plan.mid : plan.mid + 8, :] = jnp.zeros((8, LANES), jnp.float32)
    for oy in range(ny):
        gathered = jnp.concatenate([blocks[ox * ny + oy][...] for ox in range(nx)], axis=0)
        both = lax.dot_general(
            split_rows(gathered), x_matrix, (((0,), (0,)), ((), ())), preferred_element_type=jnp.float32
        )
        mid_s[oy * plan.lanes : (oy + 1) * plan.lanes, :] = both[:, :LANES] + both[:, LANES:]
    group = lax.broadcasted_iota(jnp.int32, (zp, LANES), 1) // plan.step
    for chunk in range(plan.chunks):
        sums = [jnp.zeros((zp, LANES), jnp.float32) for _ in range(per)]
        for oy in range(ny):
            for y in range(kept):
                at = oy * plan.lanes + plan.row(y)
                value = mid_s[at : at + zp, :]
                for b in range(per):
                    row = (oy * kept + y) * span + chunk * per + b
                    sums[b] = sums[b] + value * ytab_s[row : row + 1, :]
        for t in range(TERMS):
            merged = jnp.zeros((zp, LANES), jnp.float32)
            for b in range(per):
                shift = (plan.step * b - SLOT * t) % LANES
                moved = pltpu.roll(sums[b], shift, 1) if shift else sums[b]
                merged = jnp.where(group == b, moved, merged)
            term_s[t * zp : (t + 1) * zp, chunk * LANES : (chunk + 1) * LANES] = merged
    both = jnp.dot(tables[2][...], split_rows(term_s[...]), preferred_element_type=jnp.float32)
    result = both[: nz * zp, :] + both[nz * zp :, :]
    for o in range(nz):
        outs[o][...] = result[o * zp : (o + 1) * zp, :]


def gather_kernel(plan, *refs):
    nz = plan.counts[2]
    parts = refs[:nz]
    outer_s, along_z_s, fine_hbm, atom_hbm = refs[nz : nz + 4]
    field_s, column_s, turned_s, inner_s, order_s, fine_ref, atom_ref, sems = refs[nz + 4 :]
    nbx, nby, nbz = plan.nbins
    zp = plan.zp
    lx, ly, lz = plan.local
    total = parts[0][...]
    for part in parts[1:]:
        total = total + part[...]
    for chunk in range(plan.chunks):
        field_s[chunk * LANES : (chunk + 1) * LANES, :zp] = total[:, chunk * LANES : (chunk + 1) * LANES].T
    nothing = plan.lanes
    field_s[nothing:, :] = jnp.zeros((field_s.shape[0] - nothing, LANES), jnp.float32)
    first = plan.first_here()

    def row_of(y):
        if plan.counts[1] > 2:
            return plan.row(y)
        at_start = plan.row(y - RIM // 2) if y >= RIM // 2 else nothing
        at_end = plan.row(y) if y < plan.kept else nothing
        return jnp.where(first == 0, at_end, at_start)

    rows_of = [row_of(y) for y in range(plan.width[1])]
    left = lax.broadcasted_iota(jnp.int32, (zp, LANES), 1) < 64
    for pair in range(plan.columns // 2):
        for half in range(2):
            a, b = divmod(2 * pair + half, nby)
            for j in range(8):
                to = pair * LANES + half * 64 + j * 8
                turned_s[to : to + 8, :] = field_s[pl.ds(rows_of[4 * b + j] + 4 * a, 8), :]
        both = turned_s[pair * LANES : (pair + 1) * LANES, :zp].T
        turned = pltpu.roll(both, 64, 1)
        column_s[2 * pair * zp : (2 * pair + 1) * zp, :] = jnp.where(left, both, turned)
        column_s[(2 * pair + 1) * zp : (2 * pair + 2) * zp, :] = jnp.where(left, turned, both)
    for chunk in range(plan.chunks):
        inner_s[chunk * LANES : (chunk + 1) * LANES, :lz] = total[
            2 : 2 + lz, chunk * LANES : (chunk + 1) * LANES
        ].T
    for y in range(ly):
        order_s[pl.ds(y, lx, stride=ly), :] = inner_s[pl.ds(rows_of[y + 2] + 2, lx), :]
    for x in range(lx):
        fine_ref[x] = order_s[x * ly : (x + 1) * ly, :lz]
    copies = [pltpu.make_async_copy(fine_ref, fine_hbm, sems.at[0])]
    copies[0].start()
    slots = atom_ref.shape[1]

    def one_column(p):
        rows = []
        for c in range(0, nbz, 2):
            patches = [
                split_rows(column_s[p * zp + 2 * n : p * zp + 2 * n + 8, :]) for n in (c, c + 1)
            ]
            both = jnp.dot(
                jnp.concatenate(patches, axis=0), split_rows(outer_s[(p * nbz + c) // 2]),
                preferred_element_type=jnp.float32,
            )
            for n in range(2):
                field = both[16 * n : 16 * n + 8, n * slots : (n + 1) * slots]
                field = field + both[16 * n + 8 : 16 * n + 16, n * slots : (n + 1) * slots]
                rows.append(jnp.sum(field * along_z_s[p * nbz + c + n], axis=0, keepdims=True))
        atom_ref[p * nbz : (p + 1) * nbz, :] = jnp.concatenate(rows, axis=0)

    for part in range(PARTS):
        span = LANES // PARTS
        for p in range(part * span // nbz, (part + 1) * span // nbz):
            one_column(p)
        rows = pl.ds(part * span, span)
        copies.append(pltpu.make_async_copy(atom_ref.at[rows], atom_hbm.at[rows], sems.at[1 + part]))
        copies[-1].start()
    for copy in copies:
        copy.wait()


def body(charges, offset_x, offset_y, offset_z, counts):
    nbins = charges.shape[:3]
    slots = charges.shape[3]
    sizes = tuple(lax.axis_size(a) for a in ("gx", "gy", "gz"))
    nx, ny, nz = sizes
    plan = Plan(nbins, sizes)
    flat = [v.reshape(LANES, slots) for v in (charges, offset_x, offset_y, offset_z)]
    vmem = pl.BlockSpec(memory_space=pltpu.VMEM)
    hbm = pl.BlockSpec(memory_space=pltpu.HBM)
    f32 = jnp.float32
    params = pltpu.CompilerParams(vmem_limit_bytes=12 << 20)

    def far(value):
        return pltpu.with_memory_space_constraint(value, pltpu.HBM)

    tables = (plan.x_table(), plan.y_table(), plan.z_table())
    spread, *weights = pl.pallas_call(
        functools.partial(spread_kernel, plan),
        out_shape=[
            pltpu.VMEM((plan.xp, plan.lanes), f32),
            pltpu.VMEM((LANES // 2, 64, 2 * slots), f32),
            pltpu.VMEM((LANES, 8, slots), f32),
        ]
        + [pltpu.VMEM(t.shape[1:], t.dtype) for t in tables],
        in_specs=[hbm] * 8,
        out_specs=[vmem] * 6,
        scratch_shapes=[pltpu.VMEM((LANES, slots), f32)] * 4
        + [
            pltpu.SMEM(nbins, jnp.int32),
            pltpu.VMEM((plan.columns // 2 * plan.zp, LANES), f32),
            pltpu.VMEM((plan.columns * 64, LANES), f32),
            pltpu.VMEM((plan.width[1] * plan.xp, LANES), f32),
            pltpu.VMEM((LANES * 8, slots), f32),
            pltpu.SemaphoreType.DMA((8,)),
        ],
        compiler_params=params,
        name="spread",
    )(*(far(v) for v in (*flat[1:], flat[0], counts, *tables)))
    weights, tables = weights[:2], weights[2:]

    def near(value):
        return pltpu.with_memory_space_constraint(value, pltpu.VMEM)

    def moved(value, axis, pairs):
        return near(lax.ppermute(value, axis, pairs))

    def from_chip(shift, oy):
        if shift == 0 and oy == 0:
            return spread
        pairs = [
            (sx * ny + sy, (sx // pair + shift) % (nx // pair) * pair * ny + sx % pair * ny + (sy + oy) % ny)
            for sx in range(nx)
            for sy in range(ny)
        ]
        return moved(spread, ("gx", "gy"), pairs)

    pair = plan.pair
    blocks = []
    for shift in range(nx // pair):
        own = [from_chip(shift, oy) for oy in range(ny)]
        blocks += own
        if pair == 2:
            blocks += [moved(v, "gx", [(s, s ^ 1) for s in range(nx)]) for v in own]
    outs = pl.pallas_call(
        functools.partial(solve_kernel, plan),
        out_shape=[pltpu.VMEM((plan.zp, plan.lanes), f32)] * nz,
        in_specs=[vmem] * (nx * ny + 3),
        out_specs=[vmem] * nz,
        scratch_shapes=[
            pltpu.VMEM((plan.mid + 8, LANES), f32),
            pltpu.VMEM((TERMS * plan.zp, plan.lanes), f32),
        ],
        compiler_params=params,
        name="solve",
    )(*blocks, *tables)
    parts = [outs[0]] + [
        moved(outs[o], "gz", [(s, partner(s, o, nz)) for s in range(nz)]) for o in range(1, nz)
    ]
    fine, atom = pl.pallas_call(
        functools.partial(gather_kernel, plan),
        out_shape=[
            jax.ShapeDtypeStruct(plan.local, f32),
            jax.ShapeDtypeStruct((LANES, slots), f32),
        ],
        in_specs=[vmem] * (nz + 2),
        out_specs=[hbm, hbm],
        scratch_shapes=[
            pltpu.VMEM((plan.lanes + plan.xp, LANES), f32),
            pltpu.VMEM((plan.columns * plan.zp, LANES), f32),
            pltpu.VMEM((plan.columns * 64, LANES), f32),
            pltpu.VMEM((plan.lanes, LANES), f32),
            pltpu.VMEM((plan.local[0] * plan.local[1], LANES), f32),
            pltpu.VMEM(plan.local, f32),
            pltpu.VMEM((LANES, slots), f32),
            pltpu.SemaphoreType.DMA((1 + PARTS,)),
        ],
        compiler_params=params,
        name="gather",
    )(*parts, *weights)
    return fine, atom.reshape(charges.shape)


def solution(mesh):
    in_specs = (
        P("gx", "gy", "gz", None),
        P("gx", "gy", "gz", None),
        P("gx", "gy", "gz", None),
        P("gx", "gy", "gz", None),
        P("gx", "gy", "gz"),
    )
    out_specs = (P("gx", "gy", "gz"), P("gx", "gy", "gz", None))
    return jax.shard_map(body, mesh=mesh, in_specs=in_specs, out_specs=out_specs, check_vma=False)
```

```python
import functools
import math

import jax
import jax.numpy as jnp
import numpy as np
from jax import lax
from jax.experimental import pallas as pl
from jax.experimental.pallas import tpu as pltpu
from jax.sharding import PartitionSpec as P

R = 8
LANES = 128
TERMS = 5
SLOT = LANES // TERMS
PARTS = 2
RIM = 4
TAPS = (-0.0625, 0.0, 0.5625, 1.0, 0.5625, 0.0, -0.0625)
highest = lax.Precision.HIGHEST


def profile(family, offset):
    if family == 0:
        return math.exp(-((offset / (0.4 * R)) ** 2))
    if family == 1:
        return math.exp(-((offset / (0.8 * R)) ** 2))
    return 1.0 / (1.0 + (offset / R) ** 2)


def norm_factor(family):
    return sum(profile(family, float(o)) ** 2 for o in range(-R, R + 1)) ** 1.5


def stencil(points, family):
    matrix = np.zeros((points, points))
    for i in range(points):
        for k in range(max(0, i - R), min(points, i + R + 1)):
            matrix[i, k] = profile(family, float(k - i))
    return matrix


def restriction(points):
    matrix = np.zeros((points // 2, points))
    for i in range(points // 2):
        for k, tap in enumerate(TAPS):
            if 0 <= 2 * i + k - 3 < points:
                matrix[i, 2 * i + k - 3] += tap
    return matrix


def term_matrices(points):
    q_one = restriction(points)
    q_two = restriction(points // 2)
    coarse = points // 4
    far = np.array([[profile(2, float(k - i)) for k in range(coarse)] for i in range(coarse)])
    down = q_two @ q_one
    return [
        stencil(points, 0),
        stencil(points, 1),
        q_one.T @ stencil(points // 2, 0) @ q_one,
        q_one.T @ stencil(points // 2, 1) @ q_one,
        down.T @ far @ down,
    ]


def term_scales():
    n = [norm_factor(f) for f in range(3)]
    return [1.0 / n[0], 1.0 / n[1], 0.5 / n[0], 0.5 / n[1], 0.5 / n[2]]


def windowed(points, count):
    local = points // count
    width = local + RIM
    index = np.arange(count)[:, None] * local + np.arange(width)[None, :] - RIM // 2
    inside = (index >= 0) & (index < points)
    clipped = np.clip(index, 0, points - 1)
    both = inside[:, :, None, None] & inside[None, None]
    return np.stack(
        [np.where(both, m[clipped[:, :, None, None], clipped[None, None]], 0.0) for m in term_matrices(points)]
    )


def round_up(value, step):
    return -(-value // step) * step


def halves(table):
    high = table.astype(jnp.bfloat16)
    return high, (table - high.astype(np.float32)).astype(jnp.bfloat16)


def partner(device, order, count):
    return (device + order) % count


class Plan:
    def __init__(self, nbins, counts):
        self.nbins = nbins
        self.counts = counts
        self.local = (4 * nbins[0], 4 * nbins[1], 2 * nbins[2])
        self.width = tuple(v + RIM for v in self.local)
        self.points = tuple(v * c for v, c in zip(self.local, counts))
        self.xp = round_up(self.width[0], 8)
        self.zp = round_up(self.width[2], 8)
        self.kept = self.width[1] - RIM // 2 if counts[1] <= 2 else self.width[1]
        self.per = LANES // max(self.width[0], self.width[2])
        self.step = LANES // self.per
        self.chunks = -(-self.kept // self.per)
        self.lanes = self.chunks * LANES
        self.columns = nbins[0] * nbins[1]
        self.mid = self.counts[1] * self.lanes
        self.pair = 2 if counts[0] % 2 == 0 else 1
        assert self.columns * nbins[2] == LANES and nbins[2] == 8 and self.columns % 2 == 0
        assert self.width[0] <= SLOT and max(self.width[0], self.width[2]) <= self.step

    def first(self, device):
        return RIM // 2 if self.counts[1] <= 2 and device == 0 else 0

    def first_here(self):
        if self.counts[1] > 2:
            return 0
        return jnp.where(lax.axis_index("gy") == 0, RIM // 2, 0)

    def row(self, y):
        return y // self.per * LANES + y % self.per * self.step

    def x_table(self):
        nx, width = self.counts[0], self.width[0]
        m = windowed(self.points[0], nx)
        table = np.zeros((nx, nx * self.xp, LANES), np.float32)
        for d in range(nx):
            for o in range(nx):
                source = self.x_source(d, o)
                for t in range(TERMS):
                    table[d, o * self.xp : o * self.xp + width, t * SLOT : t * SLOT + width] = (
                        m[t, d, :, source, :].T
                    )
        high, low = halves(table)
        upper = np.concatenate([high, low], axis=2)
        lower = np.concatenate([high, np.zeros_like(low)], axis=2)
        return jnp.asarray(np.concatenate([upper, lower], axis=1))

    def x_source(self, device, order):
        pair = self.pair
        shift, other = divmod(order, pair)
        return (device // pair - shift) % (self.counts[0] // pair) * pair + (device % pair ^ other)

    def y_table(self):
        ny, kept = self.counts[1], self.kept
        m = windowed(self.points[1], ny)
        table = np.zeros((ny, ny * kept, self.chunks * self.per, LANES), np.float32)
        for d in range(ny):
            for o in range(ny):
                source = (d - o) % ny
                target_at, source_at = self.first(d), self.first(source)
                for t in range(TERMS):
                    block = m[t, d, target_at : target_at + kept, source, source_at : source_at + kept]
                    table[d, o * kept : (o + 1) * kept, :kept, t * SLOT : (t + 1) * SLOT] = block.T[:, :, None]
        return jnp.asarray(table.reshape(ny, ny * kept * self.chunks * self.per, LANES))

    def z_table(self):
        nz, width = self.counts[2], self.width[2]
        m = windowed(self.points[2], nz)
        scales = term_scales()
        table = np.zeros((nz, nz * self.zp, TERMS * self.zp), np.float32)
        for d in range(nz):
            for o in range(nz):
                for t in range(TERMS):
                    table[d, o * self.zp : o * self.zp + width, t * self.zp : t * self.zp + width] = (
                        scales[t] * m[t, partner(d, o, nz), :, d, :]
                    )
        high, low = halves(table)
        upper = np.concatenate([high, high], axis=2)
        lower = np.concatenate([low, np.zeros_like(low)], axis=2)
        return jnp.asarray(np.concatenate([upper, lower], axis=1))


SCALE = (1.0 / 6.0) ** (1.0 / 3.0)


def bspline(scaled):
    a = jnp.abs(scaled)
    u = jnp.maximum(2.0 * SCALE - a, 0.0)
    v = jnp.maximum(SCALE - a, 0.0)
    return u * u * u - v * v * (4.0 * v)


def split_rows(value):
    high = value.astype(jnp.bfloat16).astype(jnp.float32)
    return jnp.concatenate([high, value - high], axis=0).astype(jnp.bfloat16)


def spread_kernel(plan, *refs):
    hbm, tables, (out_ref, outer_s, along_z_s) = refs[:5], refs[5:8], refs[8:11]
    tables_out, local, (column_s, turned_s, grid_s, along_y_s, sems) = refs[11:14], refs[14:19], refs[19:]
    copies = [pltpu.make_async_copy(a, b, sems.at[n]) for n, (a, b) in enumerate(zip(hbm, local))]
    for n, (table, target, axis) in enumerate(zip(tables, tables_out, ("gx", "gy", "gz"))):
        copies.append(pltpu.make_async_copy(table.at[lax.axis_index(axis)], target, sems.at[5 + n]))
    for copy in copies:
        copy.start()
    x_ref, y_ref, z_ref, charge_ref, counts_ref = local
    slots = charge_ref.shape[1]
    nbx, nby, nbz = plan.nbins
    zp = plan.zp
    node = (2.0 - lax.broadcasted_iota(jnp.int32, (8, slots), 0).astype(jnp.float32)) * SCALE
    slot = lax.broadcasted_iota(jnp.int32, (8, slots), 1)
    rank = lax.broadcasted_iota(jnp.int32, (8, LANES), 0)
    for copy in copies[:5]:
        copy.wait()
    for ref in (x_ref, y_ref, z_ref):
        ref[...] = ref[...] * SCALE

    def one_bin(p, c):
        r = p * nbz + c
        weight_x = bspline(x_ref[pl.ds(r, 1), :] + node)
        weight_y = bspline(y_ref[pl.ds(r, 1), :] + node)
        weight_z = bspline(z_ref[pl.ds(r, 1), :] + node)
        weight_z = jnp.where(slot < counts_ref[p // nby, p % nby, c], weight_z, 0.0)
        along_y_s[r * 8 : (r + 1) * 8, :] = weight_y
        outer = jnp.concatenate(
            [along_y_s[pl.ds(r * 8 + j, 8, stride=0), :] * weight_x for j in range(8)], axis=0
        )
        outer_s[r // 2, :, (c % 2) * slots : (c % 2 + 1) * slots] = outer
        along_z_s[r] = weight_z
        return split_rows(outer), split_rows(weight_z * charge_ref[pl.ds(r, 1), :])

    def one_column(p):
        sums = [jnp.zeros((8, LANES), jnp.float32) for _ in range(zp // 8)]
        for c in range(0, nbz, 2):
            (outer_a, z_a), (outer_b, z_b) = one_bin(p, c), one_bin(p, c + 1)
            none = jnp.zeros_like(z_a)
            both = lax.dot_general(
                jnp.concatenate(
                    [jnp.concatenate([z_a, none], axis=1), jnp.concatenate([none, z_b], axis=1)], axis=0
                ),
                jnp.concatenate([outer_a, outer_b], axis=1),
                (((1,), (1,)), ((), ())),
                preferred_element_type=jnp.float32,
            )
            for n in range(2):
                part = both[16 * n : 16 * n + 8, :] + both[16 * n + 8 : 16 * n + 16, :]
                at, shift = divmod(2 * (c + n), 8)
                if shift:
                    part = pltpu.roll(part, shift, 0)
                    sums[at] = sums[at] + jnp.where(rank >= shift, part, 0.0)
                    sums[at + 1] = sums[at + 1] + jnp.where(rank < shift, part, 0.0)
                else:
                    sums[at] = sums[at] + part
        return [v + pltpu.roll(v, 64, 1) for v in sums]

    left = lax.broadcasted_iota(jnp.int32, (8, LANES), 1) < 64

    for pair in range(plan.columns // 2):
        even = one_column(2 * pair)
        odd = one_column(2 * pair + 1)
        for n, (a, b) in enumerate(zip(even, odd)):
            at = pair * zp + 8 * n
            column_s[at : at + 8, :] = jnp.where(left, a, b)
    xp = plan.xp
    for pair in range(plan.columns // 2):
        turned_s[pair * LANES : (pair + 1) * LANES, :zp] = column_s[pair * zp : (pair + 1) * zp, :].T

    def folded(a, y):
        total = None
        for b in range(nby):
            j = y - 4 * b
            if 0 <= j < 8:
                at = (a * nby + b) * 64 + j * 8
                piece = turned_s[at : at + 8, :]
                total = piece if total is None else total + piece
        return total

    for y in range(plan.width[1]):
        for a in range(0, nbx, 2):
            grid_s[y * xp + 4 * a : y * xp + 4 * a + 8, :] = folded(a, y)
        rest = xp - 4 * nbx
        grid_s[(y + 1) * xp - rest : (y + 1) * xp, :] = jnp.zeros((rest, LANES), jnp.float32)
        for a in range(1, nbx, 2):
            at = slice(y * xp + 4 * a, y * xp + 4 * a + 8)
            grid_s[at, :] = grid_s[at, :] + folded(a, y)
    group = lax.broadcasted_iota(jnp.int32, (xp, LANES), 1) // plan.step
    first = plan.first_here()
    for chunk in range(plan.chunks):
        merged = jnp.zeros((xp, LANES), jnp.float32)
        for b in range(plan.per):
            y = chunk * plan.per + b
            if y < plan.kept:
                piece = grid_s[pl.ds(pl.multiple_of((y + first) * xp, 8), xp), :]
                moved = pltpu.roll(piece, b * plan.step, 1) if b else piece
                merged = jnp.where(group == b, moved, merged)
        out_ref[:, chunk * LANES : (chunk + 1) * LANES] = merged
    for copy in copies[5:]:
        copy.wait()


def solve_kernel(plan, *refs):
    nx, ny, nz = plan.counts
    blocks = refs[: nx * ny]
    tables = refs[nx * ny : nx * ny + 3]
    outs = refs[nx * ny + 3 : nx * ny + 3 + nz]
    mid_s, term_s = refs[nx * ny + 3 + nz :]
    ytab_s = tables[1]
    x_matrix = tables[0][...]
    kept, per, zp = plan.kept, plan.per, plan.zp
    span = plan.chunks * per
    mid_s[plan.mid : plan.mid + 8, :] = jnp.zeros((8, LANES), jnp.float32)
    for oy in range(ny):
        gathered = jnp.concatenate([blocks[ox * ny + oy][...] for ox in range(nx)], axis=0)
        both = lax.dot_general(
            split_rows(gathered), x_matrix, (((0,), (0,)), ((), ())), preferred_element_type=jnp.float32
        )
        mid_s[oy * plan.lanes : (oy + 1) * plan.lanes, :] = both[:, :LANES] + both[:, LANES:]
    group = lax.broadcasted_iota(jnp.int32, (zp, LANES), 1) // plan.step
    for chunk in range(plan.chunks):
        sums = [jnp.zeros((zp, LANES), jnp.float32) for _ in range(per)]
        for oy in range(ny):
            for y in range(kept):
                at = oy * plan.lanes + plan.row(y)
                value = mid_s[at : at + zp, :]
                for b in range(per):
                    row = (oy * kept + y) * span + chunk * per + b
                    sums[b] = sums[b] + value * ytab_s[row : row + 1, :]
        for t in range(TERMS):
            merged = jnp.zeros((zp, LANES), jnp.float32)
            for b in range(per):
                shift = (plan.step * b - SLOT * t) % LANES
                moved = pltpu.roll(sums[b], shift, 1) if shift else sums[b]
                merged = jnp.where(group == b, moved, merged)
            term_s[t * zp : (t + 1) * zp, chunk * LANES : (chunk + 1) * LANES] = merged
    both = jnp.dot(tables[2][...], split_rows(term_s[...]), preferred_element_type=jnp.float32)
    result = both[: nz * zp, :] + both[nz * zp :, :]
    for o in range(nz):
        outs[o][...] = result[o * zp : (o + 1) * zp, :]


def gather_kernel(plan, *refs):
    nz = plan.counts[2]
    parts = refs[:nz]
    outer_s, along_z_s, fine_hbm, atom_hbm = refs[nz : nz + 4]
    field_s, column_s, turned_s, inner_s, order_s, fine_ref, atom_ref, sems = refs[nz + 4 :]
    nbx, nby, nbz = plan.nbins
    zp = plan.zp
    lx, ly, lz = plan.local
    total = parts[0][...]
    for part in parts[1:]:
        total = total + part[...]
    for chunk in range(plan.chunks):
        field_s[chunk * LANES : (chunk + 1) * LANES, :zp] = total[:, chunk * LANES : (chunk + 1) * LANES].T
    nothing = plan.lanes
    field_s[nothing:, :] = jnp.zeros((field_s.shape[0] - nothing, LANES), jnp.float32)
    first = plan.first_here()

    def row_of(y):
        if plan.counts[1] > 2:
            return plan.row(y)
        at_start = plan.row(y - RIM // 2) if y >= RIM // 2 else nothing
        at_end = plan.row(y) if y < plan.kept else nothing
        return jnp.where(first == 0, at_end, at_start)

    rows_of = [row_of(y) for y in range(plan.width[1])]
    left = lax.broadcasted_iota(jnp.int32, (zp, LANES), 1) < 64
    for pair in range(plan.columns // 2):
        for half in range(2):
            a, b = divmod(2 * pair + half, nby)
            for j in range(8):
                to = pair * LANES + half * 64 + j * 8
                turned_s[to : to + 8, :] = field_s[pl.ds(rows_of[4 * b + j] + 4 * a, 8), :]
        both = turned_s[pair * LANES : (pair + 1) * LANES, :zp].T
        turned = pltpu.roll(both, 64, 1)
        column_s[2 * pair * zp : (2 * pair + 1) * zp, :] = jnp.where(left, both, turned)
        column_s[(2 * pair + 1) * zp : (2 * pair + 2) * zp, :] = jnp.where(left, turned, both)
    for chunk in range(plan.chunks):
        inner_s[chunk * LANES : (chunk + 1) * LANES, :lz] = total[
            2 : 2 + lz, chunk * LANES : (chunk + 1) * LANES
        ].T
    for y in range(ly):
        order_s[pl.ds(y, lx, stride=ly), :] = inner_s[pl.ds(rows_of[y + 2] + 2, lx), :]
    for x in range(lx):
        fine_ref[x] = order_s[x * ly : (x + 1) * ly, :lz]
    copies = [pltpu.make_async_copy(fine_ref, fine_hbm, sems.at[0])]
    copies[0].start()
    slots = atom_ref.shape[1]

    def one_column(p):
        rows = []
        for c in range(0, nbz, 2):
            patches = [
                split_rows(column_s[p * zp + 2 * n : p * zp + 2 * n + 8, :]) for n in (c, c + 1)
            ]
            both = jnp.dot(
                jnp.concatenate(patches, axis=0), split_rows(outer_s[(p * nbz + c) // 2]),
                preferred_element_type=jnp.float32,
            )
            for n in range(2):
                field = both[16 * n : 16 * n + 8, n * slots : (n + 1) * slots]
                field = field + both[16 * n + 8 : 16 * n + 16, n * slots : (n + 1) * slots]
                rows.append(jnp.sum(field * along_z_s[p * nbz + c + n], axis=0, keepdims=True))
        atom_ref[p * nbz : (p + 1) * nbz, :] = jnp.concatenate(rows, axis=0)

    for part in range(PARTS):
        span = LANES // PARTS
        for p in range(part * span // nbz, (part + 1) * span // nbz):
            one_column(p)
        rows = pl.ds(part * span, span)
        copies.append(pltpu.make_async_copy(atom_ref.at[rows], atom_hbm.at[rows], sems.at[1 + part]))
        copies[-1].start()
    for copy in copies:
        copy.wait()


def body(charges, offset_x, offset_y, offset_z, counts):
    nbins = charges.shape[:3]
    slots = charges.shape[3]
    sizes = tuple(lax.axis_size(a) for a in ("gx", "gy", "gz"))
    nx, ny, nz = sizes
    plan = Plan(nbins, sizes)
    flat = [v.reshape(LANES, slots) for v in (charges, offset_x, offset_y, offset_z)]
    vmem = pl.BlockSpec(memory_space=pltpu.VMEM)
    hbm = pl.BlockSpec(memory_space=pltpu.HBM)
    f32 = jnp.float32
    params = pltpu.CompilerParams(vmem_limit_bytes=12 << 20)

    def far(value):
        return pltpu.with_memory_space_constraint(value, pltpu.HBM)

    tables = (plan.x_table(), plan.y_table(), plan.z_table())
    spread, *weights = pl.pallas_call(
        functools.partial(spread_kernel, plan),
        out_shape=[
            pltpu.VMEM((plan.xp, plan.lanes), f32),
            pltpu.VMEM((LANES // 2, 64, 2 * slots), f32),
            pltpu.VMEM((LANES, 8, slots), f32),
        ]
        + [pltpu.VMEM(t.shape[1:], t.dtype) for t in tables],
        in_specs=[hbm] * 8,
        out_specs=[vmem] * 6,
        scratch_shapes=[pltpu.VMEM((LANES, slots), f32)] * 4
        + [
            pltpu.SMEM(nbins, jnp.int32),
            pltpu.VMEM((plan.columns // 2 * plan.zp, LANES), f32),
            pltpu.VMEM((plan.columns * 64, LANES), f32),
            pltpu.VMEM((plan.width[1] * plan.xp, LANES), f32),
            pltpu.VMEM((LANES * 8 + 8, slots), f32),
            pltpu.SemaphoreType.DMA((8,)),
        ],
        compiler_params=params,
        name="spread",
    )(*(far(v) for v in (*flat[1:], flat[0], counts, *tables)))
    weights, tables = weights[:2], weights[2:]

    def near(value):
        return pltpu.with_memory_space_constraint(value, pltpu.VMEM)

    def moved(value, axis, pairs):
        return near(lax.ppermute(value, axis, pairs))

    def from_chip(shift, oy):
        if shift == 0 and oy == 0:
            return spread
        pairs = [
            (sx * ny + sy, (sx // pair + shift) % (nx // pair) * pair * ny + sx % pair * ny + (sy + oy) % ny)
            for sx in range(nx)
            for sy in range(ny)
        ]
        return moved(spread, ("gx", "gy"), pairs)

    pair = plan.pair
    blocks = []
    for shift in range(nx // pair):
        own = [from_chip(shift, oy) for oy in range(ny)]
        blocks += own
        if pair == 2:
            blocks += [moved(v, "gx", [(s, s ^ 1) for s in range(nx)]) for v in own]
    outs = pl.pallas_call(
        functools.partial(solve_kernel, plan),
        out_shape=[pltpu.VMEM((plan.zp, plan.lanes), f32)] * nz,
        in_specs=[vmem] * (nx * ny + 3),
        out_specs=[vmem] * nz,
        scratch_shapes=[
            pltpu.VMEM((plan.mid + 8, LANES), f32),
            pltpu.VMEM((TERMS * plan.zp, plan.lanes), f32),
        ],
        compiler_params=params,
        name="solve",
    )(*blocks, *tables)
    parts = [outs[0]] + [
        moved(outs[o], "gz", [(s, partner(s, o, nz)) for s in range(nz)]) for o in range(1, nz)
    ]
    fine, atom = pl.pallas_call(
        functools.partial(gather_kernel, plan),
        out_shape=[
            jax.ShapeDtypeStruct(plan.local, f32),
            jax.ShapeDtypeStruct((LANES, slots), f32),
        ],
        in_specs=[vmem] * (nz + 2),
        out_specs=[hbm, hbm],
        scratch_shapes=[
            pltpu.VMEM((plan.lanes + plan.xp, LANES), f32),
            pltpu.VMEM((plan.columns * plan.zp, LANES), f32),
            pltpu.VMEM((plan.columns * 64, LANES), f32),
            pltpu.VMEM((plan.lanes, LANES), f32),
            pltpu.VMEM((plan.local[0] * plan.local[1], LANES), f32),
            pltpu.VMEM(plan.local, f32),
            pltpu.VMEM((LANES, slots), f32),
            pltpu.SemaphoreType.DMA((1 + PARTS,)),
        ],
        compiler_params=params,
        name="gather",
    )(*parts, *weights)
    return fine, atom.reshape(charges.shape)


def solution(mesh):
    in_specs = (
        P("gx", "gy", "gz", None),
        P("gx", "gy", "gz", None),
        P("gx", "gy", "gz", None),
        P("gx", "gy", "gz", None),
        P("gx", "gy", "gz"),
    )
    out_specs = (P("gx", "gy", "gz"), P("gx", "gy", "gz", None))
    return jax.shard_map(body, mesh=mesh, in_specs=in_specs, out_specs=out_specs, check_vma=False)
```
